32 devices in a mesh: geom: 2 (over x), aux: 16 (over z, y, core).
Axes of the slice: x: 2, y: 2, z: 4, core: 2. Of those that a mesh axis runs over, the one named last changes fastest.
Arguments:
- trial_vecs: float32 [8, 128, 224], P('geom', 'aux'), parts along dimension 0, may hold values from -6 to 6
- occ_energy: float32 [256], P('geom'), parts along dimension 0, may hold values from -1.5 to -0.2
- vir_energy: float32 [448], P('geom'), parts along dimension 0, may hold values from 0.2 to 2.5
- coul_ov: bfloat16 [2048, 128, 224], P(('geom', 'aux')), parts along dimension 0, may hold values from -0.03125 to 0.03125
- exch_oo: bfloat16 [2048, 128, 128], P(('geom', 'aux')), parts along dimension 0, may hold values from -0.0234375 to 0.0234375
- exch_vv: bfloat16 [2048, 224, 224], P(('geom', 'aux')), parts along dimension 0, may hold values from -0.375 to 0.375
Outputs:
- sigma_vecs: float32 [8, 128, 224], P('geom', 'aux'), parts along dimension 0
- update_vecs: float32 [8, 128, 224], P('geom', 'aux'), parts along dimension 0
The draws below stay inside these ranges and needn't reach their ends.
There are 2 independent parts, one for each index of `geom`. The reference program is written for one: setup_inputs(seed, part) draws one part's arguments, and reference() takes and returns one part's arrays. A program takes and returns all parts, laid end to end along the dimension named above; each array names one. Nothing has to cross between parts.
All inputs are finite; a program needn't handle non-finite values.
Results may differ from the reference program's by a relative error of at most 0.0037.
Values may be sent and summed in bfloat16 or wider, within the bound.
No kernel may reach another device: no remote copies, remote signals or barrier semaphores. Data moves between devices by JAX's collectives and lax.ppermute only.
A program may use at most 64 MiB of HBM per device.

```python
import jax
import jax.numpy as jnp
from jax import lax

NT = 4
NO = 128
VB = 224
AUX_DEV = 64
NAUX = 1024
N_AUX = 16


def strengthened(array, rng, source, target, blocks, factor):
    def block_of(axis_at):
        return (jnp.arange(array.shape[axis_at]) // (array.shape[axis_at] // blocks)).reshape((-1,) + (1,) * (array.ndim - 1 - axis_at))

    first = jax.random.permutation(rng, blocks)[block_of(target)]
    second = (block_of(target) + blocks // 2) % blocks
    return jnp.where((block_of(source) == first) | (block_of(source) == second), factor * array, array)


def level_of(key, extent, cuts, low, top_value):
    gain, own = 1.0, jax.random.fold_in(key, 6)
    for axis_at, blocks in cuts:
        heights = jnp.exp(jax.random.uniform(jax.random.fold_in(own, axis_at), (blocks,), jnp.float32, low / len(cuts), top_value / len(cuts)))
        gain = gain * jnp.repeat(heights, extent[axis_at] // blocks).reshape([-1 if axis == axis_at else 1 for axis in range(len(extent))])
    return gain


def gaussian(stream_key, dims, deviation, bound, shards=(), dtype=jnp.bfloat16):
    drawn = jax.random.normal(stream_key, dims, jnp.float32) * deviation
    if len(shards) > 0:
        drawn = level_of(stream_key, dims, shards, -0.22, 0.18) * drawn
    return jnp.clip(drawn, min=-bound, max=bound).astype(dtype)


def gaussian_with(rng, shape, deviation, most, shards, heavy, kind=jnp.bfloat16):
    drawn = deviation * jax.random.normal(rng, shape, jnp.float32)
    if shards:
        drawn = drawn * level_of(rng, shape, shards, -0.22, 0.18)
    return jnp.clip(strengthened(drawn, jax.random.fold_in(rng, 3), *heavy), -most, most).astype(kind)


def setup_inputs(seed: int = 0, part: int = 0) -> dict:
    keys = jax.random.split(jax.random.key(seed), 7)
    part_keys = jax.random.split(jax.random.fold_in(keys[6], part), 7)
    trial_vecs = gaussian(part_keys[0], (NT, NO, VB), 1.0, 6.0, ((1, 16),), jnp.float32)
    occ_energy = jnp.clip(jax.random.uniform(part_keys[1], (NO,), jnp.float32, -1.5, -0.2), -1.5, -0.2)
    vir_energy = jnp.clip(jax.random.uniform(part_keys[2], (VB,), jnp.float32, 0.2, 2.5), 0.2, 2.5)
    coul_ov = gaussian(part_keys[3], (NAUX, NO, VB), (NO * VB) ** -0.5, 0.03125, ((0, 16),))
    exch_oo = gaussian_with(part_keys[4], (NAUX, NO, NO), (AUX_DEV * N_AUX * NO) ** -0.5, 0.0234375, ((0, 16),), (0, 1, 16, 2.0))
    exch_vv = gaussian(part_keys[5], (NAUX, VB, VB), VB ** -0.5, 0.375, ((0, 16),))
    return {"trial_vecs": trial_vecs, "occ_energy": occ_energy, "vir_energy": vir_energy, "coul_ov": coul_ov, "exch_oo": exch_oo, "exch_vv": exch_vv}


def reference(trial_vecs, occ_energy, vir_energy, coul_ov, exch_oo, exch_vv):
    rounded = trial_vecs.astype(jnp.bfloat16)
    wide_x = rounded.astype(jnp.float32)
    n_trial = trial_vecs.shape[0]
    n_occ = trial_vecs.shape[1]
    n_virt = trial_vecs.shape[2]
    ov_blocks = coul_ov.reshape(N_AUX, AUX_DEV, n_occ, n_virt)
    oo_blocks = exch_oo.reshape(N_AUX, AUX_DEV, n_occ, n_occ)
    vv_blocks = exch_vv.reshape(N_AUX, AUX_DEV, n_virt, n_virt)

    def advance(totals, parts):
        ov_part, oo_part, vv_part = parts
        ov_wide = ov_part.astype(jnp.float32)
        aux_coef = jnp.einsum('pia,nia->np', ov_wide, wide_x)
        coef_low = lax.optimization_barrier(aux_coef.astype(jnp.bfloat16))
        coulomb = jnp.einsum('pia,np->nia', ov_wide, coef_low.astype(jnp.float32))
        halfway = jnp.einsum('pab,njb->pnja', vv_part.astype(jnp.float32), wide_x)
        halfway = lax.optimization_barrier(halfway.astype(jnp.bfloat16))
        exchange = jnp.einsum('pij,pnja->nia', oo_part.astype(jnp.float32), halfway.astype(jnp.float32))
        return ((totals[0] + coulomb, totals[1] + exchange), None)
    empty = jnp.zeros((n_trial, n_occ, n_virt), jnp.float32)
    sums, _ = lax.scan(advance, (empty, empty), (ov_blocks, oo_blocks, vv_blocks))
    diagonal = vir_energy[None, :] - occ_energy[:, None]
    sigma_vecs = diagonal[None] * trial_vecs + 2.0 * sums[0] - sums[1]
    omega = lax.optimization_barrier(jnp.sum(trial_vecs * sigma_vecs, axis=(1, 2))) / (lax.optimization_barrier(jnp.sum(trial_vecs * trial_vecs, axis=(1, 2))) + 1e-06)
    resid = sigma_vecs - omega[:, None, None] * trial_vecs
    gap = jnp.maximum(jnp.abs(diagonal[None] - omega[:, None, None]), 1.0)
    precond = resid / gap
    update_vecs = precond * lax.rsqrt(lax.optimization_barrier(jnp.mean(precond * precond, axis=(1, 2))) + 1e-06)[:, None, None]
    return (sigma_vecs, update_vecs)
```

```python
import functools

import jax
import jax.numpy as jnp
from jax import lax
from jax.experimental import pallas as pl
from jax.experimental.pallas import tpu as pltpu
from jax.sharding import PartitionSpec as P


F32 = jnp.float32
BF16 = jnp.bfloat16
LOW_BITS = 2
TILE = 16
VMEM = pl.BlockSpec(memory_space=pltpu.VMEM)
SMEM = pl.BlockSpec(memory_space=pltpu.SMEM)


def bit_groups(size):
    bits = size.bit_length() - 1
    assert size == 1 << bits
    low = min(LOW_BITS, bits)
    return low, [(at, min(LOW_BITS, bits - at)) for at in range(low, bits, LOW_BITS)]


def swap(value, size, offset):
    return lax.ppermute(value, "aux", [(i, i ^ offset) for i in range(size)])


def exchange(value, size, at, width):
    return [swap(value, size, k << at) for k in range(1, 1 << width)]


def dot(a, b):
    return jnp.dot(a, b, preferred_element_type=F32)


def dot_nt(a, b):
    return lax.dot_general(a, b, (((1,), (1,)), ((), ())), preferred_element_type=F32)


def three_parts(value):
    high = value.astype(BF16).astype(F32)
    middle = (value - high).astype(BF16).astype(F32)
    rest = value - high - middle
    lane = lax.broadcasted_iota(jnp.int32, value.shape, 1)
    return jnp.where(
        lane == 0, high, jnp.where(lane == 1, middle, jnp.where(lane == 2, rest, 0.0))
    ).astype(BF16)


def coulomb_into(acc_ref, x, ov_ref):
    n_aux, n_virt, n_occ = ov_ref.shape
    n_trial = x.shape[0]
    tiles = n_virt // TILE
    unit = (
        lax.broadcasted_iota(jnp.int32, (n_virt, n_virt), 0)
        == lax.broadcasted_iota(jnp.int32, (n_virt, n_virt), 1)
    ).astype(BF16)
    x_t = jnp.stack([dot_nt(unit, x[m]).astype(BF16) for m in range(n_trial)], 0)
    rows, cols = n_trial * TILE, n_aux * TILE

    def x_tile(t):
        return x_t[:, t * TILE : (t + 1) * TILE, :].reshape(rows, n_occ)

    def ov_tile(t):
        return ov_ref[:, t * TILE : (t + 1) * TILE, :].reshape(cols, n_occ)

    total = jnp.zeros((rows, cols), F32)
    for t in range(0, tiles, 2):
        span = range(t, min(t + 2, tiles))
        total += dot_nt(
            jnp.concatenate([x_tile(u) for u in span], axis=1),
            jnp.concatenate([ov_tile(u) for u in span], axis=1),
        )
    same = (
        lax.broadcasted_iota(jnp.int32, (rows, cols), 0) % TILE
        == lax.broadcasted_iota(jnp.int32, (rows, cols), 1) % TILE
    )
    coef = jnp.sum(jnp.where(same, total, 0.0).reshape(n_trial, TILE, cols), axis=1)
    lane = lax.broadcasted_iota(jnp.int32, coef.shape, 1)
    step = 1
    while step < TILE:
        coef += jnp.where(
            (lane & step) != 0, pltpu.roll(coef, step, 1), pltpu.roll(coef, cols - step, 1)
        )
        step *= 2
    twice = 2.0 * coef.astype(BF16).astype(F32)
    spread = jnp.broadcast_to(twice[:, None, :], (n_trial, TILE, cols)).reshape(rows, cols)
    weights = jnp.where(same, spread, 0.0).astype(BF16)
    for t in range(tiles):
        acc_ref[:, t * TILE : (t + 1) * TILE, :] = -dot(weights, ov_tile(t)).reshape(
            n_trial, TILE, n_occ
        )


def build_kernel(low, group, cut, me_ref, own_ref, diag_ref, *refs):
    parts = 1 << low
    taken = parts if cut else 1
    pieces, refs = refs[:taken], refs[taken:]
    ov_ref, oo_ref, vv_ref = refs[:3]
    outs, (xs_ref, h_ref, acc_ref) = refs[3:-3], refs[-3:]
    n_trial, rows, n_virt = own_ref.shape
    n_aux, n_occ, _ = oo_ref.shape
    high_count = n_occ // rows >> low
    me = me_ref[0]
    mine, top = me & (parts - 1), me >> low
    if cut:
        for k in range(parts):
            for z in range(high_count):
                at = pl.multiple_of((((top ^ z) << low) | (mine ^ k)) * rows, rows)
                for m in range(n_trial):
                    xs_ref[m, pl.ds(at, rows), :] = pieces[k][z, m].astype(F32)
    else:
        xs_ref[...] = pieces[0][...].astype(F32)
    x = xs_ref[...].astype(BF16)
    flat = x.reshape(n_trial * n_occ, n_virt)
    coulomb_into(acc_ref, x, ov_ref)

    def advance(c, carry):
        first = c * group
        vv = vv_ref[pl.ds(first, group)].reshape(group * n_virt, n_virt)
        h_ref[...] = dot_nt(vv, flat).astype(BF16).reshape(group, n_virt, n_trial * n_occ)
        oo = jnp.concatenate([oo_ref[first + g] for g in range(group)], axis=1)
        for m in range(n_trial):
            half = jnp.concatenate(
                [h_ref[g, :, m * n_occ : (m + 1) * n_occ] for g in range(group)], axis=1
            )
            acc_ref[m] += dot_nt(half, oo)
        return carry

    lax.fori_loop(0, n_aux // group, advance, 0)
    unit = (
        lax.broadcasted_iota(jnp.int32, (n_occ, 2 * n_occ), 0)
        == lax.broadcasted_iota(jnp.int32, (n_occ, 2 * n_occ), 1) % n_occ
    ).astype(BF16)
    lines = []
    for m in range(n_trial):
        turned = acc_ref[m]
        high = turned.astype(BF16)
        rest = (turned - high.astype(F32)).astype(BF16)
        value = -dot_nt(unit, jnp.concatenate([high, rest], axis=1))
        seen = xs_ref[m]
        lines.append(jnp.sum(jnp.sum(seen * value, axis=0, keepdims=True), axis=1, keepdims=True))
        xs_ref[m] = value
    own = own_ref[...]
    square = own * own
    for m in range(n_trial):
        lines[m] += jnp.sum(
            jnp.sum(square[m] * diag_ref[...], axis=0, keepdims=True), axis=1, keepdims=True
        )
    for m in range(n_trial):
        lines.append(
            jnp.sum(jnp.sum(square[m], axis=0, keepdims=True), axis=1, keepdims=True)
        )
    scalars = jnp.concatenate(
        [jnp.broadcast_to(line, (1, n_virt)) for line in lines], axis=0
    )
    single = jnp.where(
        lax.broadcasted_iota(jnp.int32, scalars.shape, 1) == 0, scalars, 0.0
    )
    coded = three_parts(scalars)
    if not cut:
        for ref, value in zip(outs, (xs_ref[...], single, coded)):
            ref[...] = value
        return
    body = high_count * n_trial * rows
    outs[0][body:, :] = single
    for k in range(parts):
        blocks = []
        for z in range(high_count):
            at = pl.multiple_of(((z << low) | (mine ^ k)) * rows, rows)
            blocks += [xs_ref[m, pl.ds(at, rows), :] for m in range(n_trial)]
        whole = jnp.concatenate(blocks, axis=0)
        if k == 0:
            outs[0][:body, :] = whole
        else:
            outs[k][:body, :] = whole.astype(BF16)
            outs[k][body:, :] = coded


def build(me, own, diag_own, pieces, coul_t, exch_oo, exch_vv, low):
    parts = len(pieces)
    high_count, n_trial, rows, n_virt = pieces[0].shape
    n_aux, n_occ, _ = exch_oo.shape
    group = TILE
    while n_aux % group:
        group //= 2
    cut = rows % 8 == 0
    height, extra = high_count * n_trial * rows, 2 * n_trial
    if cut:
        shapes = [jax.ShapeDtypeStruct((height + extra, n_virt), F32)]
        shapes += [jax.ShapeDtypeStruct((height + extra, n_virt), BF16)] * (parts - 1)
    else:
        order = me ^ jnp.arange(high_count * parts)
        placed = jnp.stack(pieces, 1).reshape(-1, n_trial, rows, n_virt)[order]
        pieces = [placed.transpose(1, 0, 2, 3).reshape(n_trial, n_occ, n_virt)]
        shapes = [
            jax.ShapeDtypeStruct((n_trial, n_occ, n_virt), F32),
            jax.ShapeDtypeStruct((extra, n_virt), F32),
            jax.ShapeDtypeStruct((extra, n_virt), BF16),
        ]
    flops = 2 * n_aux * n_trial * n_occ * n_virt * (n_virt + n_occ)
    moved = 2 * (coul_t.size + exch_oo.size + exch_vv.size)
    results = pl.pallas_call(
        functools.partial(build_kernel, low, group, cut),
        out_shape=shapes,
        in_specs=[SMEM] + [VMEM] * (5 + len(pieces)),
        out_specs=[VMEM] * len(shapes),
        scratch_shapes=[
            pltpu.VMEM((n_trial, n_occ, n_virt), F32),
            pltpu.VMEM((group, n_virt, n_trial * n_occ), BF16),
            pltpu.VMEM((n_trial, n_virt, n_occ), F32),
        ],
        compiler_params=pltpu.CompilerParams(vmem_limit_bytes=28 << 20),
        cost_estimate=pl.CostEstimate(flops=flops, bytes_accessed=moved, transcendentals=0),
    )(me[None], own, diag_own, *pieces, coul_t, exch_oo, exch_vv)
    if cut:
        return results
    value, single, coded = results
    value = value.reshape(n_trial, high_count, parts, rows, n_virt).transpose(2, 1, 0, 3, 4)
    mine = me & (parts - 1)
    blocks = [
        lax.dynamic_index_in_dim(value, mine ^ k, 0, keepdims=False).reshape(height, n_virt)
        for k in range(parts)
    ]
    return [jnp.concatenate([blocks[0], single], axis=0)] + [
        jnp.concatenate([block.astype(BF16), coded], axis=0) for block in blocks[1:]
    ]


def summed(own_ref, arrived):
    total = own_ref[...]
    for ref in arrived:
        total += ref[...].astype(F32)
    return total


def combine_kernel(extra, own_ref, *refs):
    arrived, (total_ref, send_ref) = refs[:-2], refs[-2:]
    total = summed(own_ref, arrived)
    body = total.shape[0] - extra
    scalars = jnp.sum(total[body:], axis=1, keepdims=True)
    scalars = jnp.broadcast_to(scalars, (extra, total.shape[1]))
    lane = lax.broadcasted_iota(jnp.int32, scalars.shape, 1)
    total_ref[:body, :] = total[:body]
    total_ref[body:, :] = jnp.where(lane == 0, scalars, 0.0)
    send_ref[:body, :] = total[:body].astype(BF16)
    send_ref[body:, :] = three_parts(scalars)


def combine(own, arrived, extra):
    return pl.pallas_call(
        functools.partial(combine_kernel, extra),
        out_shape=[
            jax.ShapeDtypeStruct(own.shape, F32),
            jax.ShapeDtypeStruct(own.shape, BF16),
        ],
        in_specs=[VMEM] * (1 + len(arrived)),
        out_specs=[VMEM] * 2,
    )(own, *arrived)


def residual_kernel(top_ref, t_ref, diag_ref, own_ref, *refs):
    arrived, (sigma_ref, precond_ref, square_ref) = refs[:-3], refs[-3:]
    high_count, n_trial, rows, n_virt = t_ref.shape
    body = high_count * n_trial * rows
    top = top_ref[0]
    total = summed(own_ref, arrived)
    scalars = jnp.sum(total[body:], axis=1, keepdims=True)
    omega = scalars[:n_trial] / (scalars[n_trial:] + 1e-06)
    squares = [jnp.zeros((rows, n_virt), F32) for _ in range(n_trial)]

    def block(z, m):
        return total[(z * n_trial + m) * rows : (z * n_trial + m + 1) * rows]

    for z in range(high_count):
        gap_from = diag_ref[z]
        for m in range(n_trial):
            t = t_ref[z ^ top, m]
            level = omega[m : m + 1]
            sigma = gap_from * t + block(z, m)
            gap = jnp.maximum(jnp.abs(gap_from - level), 1.0)
            precond = (sigma - level * t) / gap
            squares[m] += precond * precond

            @pl.when(z == top)
            def _():
                sigma_ref[m] = sigma
                precond_ref[m] = precond

    sums = [
        jnp.sum(jnp.sum(s, axis=0, keepdims=True), axis=1, keepdims=True) for s in squares
    ]
    square_ref[...] = jnp.concatenate(
        [jnp.broadcast_to(s, (1, square_ref.shape[1])) for s in sums], axis=0
    )


def residual(top, t, diag, own, arrived):
    _, n_trial, rows, n_virt = t.shape
    block = jax.ShapeDtypeStruct((n_trial, rows, n_virt), F32)
    return pl.pallas_call(
        residual_kernel,
        out_shape=[block, block, jax.ShapeDtypeStruct((n_trial, 128), F32)],
        in_specs=[SMEM] + [VMEM] * (3 + len(arrived)),
        out_specs=[VMEM] * 3,
    )(top, t, diag, own, *arrived)


def on_device(size, trial_vecs, occ_energy, vir_energy, coul_ov, exch_oo, exch_vv):
    n_trial, rows, n_virt = trial_vecs.shape
    n_occ = exch_oo.shape[1]
    low, highs = bit_groups(size)
    parts, high_count = 1 << low, size >> low
    me = lax.axis_index("aux").astype(jnp.int32)
    mine, top = me & (parts - 1), me >> low
    occ = lax.dynamic_index_in_dim(
        occ_energy.reshape(high_count, parts, rows), mine, 1, keepdims=False
    )
    diag = vir_energy[None, None, :] - occ[:, :, None]
    diag_own = lax.dynamic_index_in_dim(diag, top, 0, keepdims=False)

    column = trial_vecs[None]
    for at, width in highs:
        column = jnp.concatenate([column] + exchange(column, size, at, width), axis=0)
    rounded = column.astype(BF16)
    pieces = [rounded] + exchange(rounded, size, 0, low)
    coul_t = jnp.transpose(coul_ov, (0, 2, 1))
    own, *sends = build(
        me, trial_vecs, diag_own, pieces, coul_t, exch_oo, exch_vv, low
    )
    arrived = [swap(send, size, k + 1) for k, send in enumerate(sends)]
    for at, width in highs:
        own, send = combine(own, arrived, 2 * n_trial)
        arrived = exchange(send, size, at, width)
    sigma_vecs, precond, square = residual(top[None], column, diag, own, arrived)
    for other in exchange(square, size, 0, low):
        square = square + other
    scale = lax.rsqrt(square[:, :1] / (n_occ * n_virt) + 1e-06)
    return sigma_vecs, precond * scale[:, :, None]


def solution(mesh):
    in_specs = (
        P("geom", "aux", None),
        P("geom"),
        P("geom"),
        P(("geom", "aux"), None, None),
        P(("geom", "aux"), None, None),
        P(("geom", "aux"), None, None),
    )
    out_specs = (P("geom", "aux", None), P("geom", "aux", None))
    return jax.shard_map(
        functools.partial(on_device, mesh.shape["aux"]),
        mesh=mesh,
        in_specs=in_specs,
        out_specs=out_specs,
        check_vma=False,
    )
```

```python
import functools
import math

import jax
import jax.numpy as jnp
from jax import lax
from jax.experimental import pallas as pl
from jax.experimental.pallas import tpu as pltpu
from jax.sharding import PartitionSpec as P


F32 = jnp.float32
BF16 = jnp.bfloat16
LOW_BITS = 2
TILE = 16
VMEM = pl.BlockSpec(memory_space=pltpu.VMEM)
SMEM = pl.BlockSpec(memory_space=pltpu.SMEM)
SMALL = pltpu.CompilerParams(vmem_limit_bytes=4 << 20)


def bit_groups(size):
    bits = size.bit_length() - 1
    assert size == 1 << bits
    low = min(LOW_BITS, bits)
    return low, [(at, min(LOW_BITS, bits - at)) for at in range(low, bits, LOW_BITS)]


def swap(value, size, offset):
    return lax.ppermute(value, "aux", [(i, i ^ offset) for i in range(size)])


def exchange(value, size, at, width):
    return [swap(value, size, k << at) for k in range(1, 1 << width)]


def dot(a, b):
    return jnp.dot(a, b, preferred_element_type=F32)


def dot_nt(a, b):
    return lax.dot_general(a, b, (((1,), (1,)), ((), ())), preferred_element_type=F32)


def diagonal(occ_ref, vir_ref, first, rows):
    shape = (rows, occ_ref.shape[1])
    wanted = lax.broadcasted_iota(jnp.int32, shape, 0) + first
    picked = jnp.where(lax.broadcasted_iota(jnp.int32, shape, 1) == wanted, occ_ref[...], 0.0)
    return vir_ref[...] - jnp.sum(picked, axis=1, keepdims=True)


def three_parts(value):
    high = value.astype(BF16).astype(F32)
    middle = (value - high).astype(BF16).astype(F32)
    rest = value - high - middle
    lane = lax.broadcasted_iota(jnp.int32, value.shape, 1)
    return jnp.where(
        lane == 0, high, jnp.where(lane == 1, middle, jnp.where(lane == 2, rest, 0.0))
    ).astype(BF16)


def coulomb_into(acc_ref, x, ov_ref):
    n_aux, n_virt, n_occ = ov_ref.shape
    n_trial = x.shape[0]
    tiles = n_virt // TILE
    unit = (
        lax.broadcasted_iota(jnp.int32, (n_virt, n_virt), 0)
        == lax.broadcasted_iota(jnp.int32, (n_virt, n_virt), 1)
    ).astype(BF16)
    x_t = jnp.stack([dot_nt(unit, x[m]).astype(BF16) for m in range(n_trial)], 0)
    rows, cols = n_trial * TILE, n_aux * TILE

    def x_tile(t):
        return x_t[:, t * TILE : (t + 1) * TILE, :].reshape(rows, n_occ)

    def ov_tile(t):
        return ov_ref[:, t * TILE : (t + 1) * TILE, :].reshape(cols, n_occ)

    total = jnp.zeros((rows, cols), F32)
    for t in range(0, tiles, 2):
        span = range(t, min(t + 2, tiles))
        total += dot_nt(
            jnp.concatenate([x_tile(u) for u in span], axis=1),
            jnp.concatenate([ov_tile(u) for u in span], axis=1),
        )
    same = (
        lax.broadcasted_iota(jnp.int32, (rows, cols), 0) % TILE
        == lax.broadcasted_iota(jnp.int32, (rows, cols), 1) % TILE
    )
    coef = jnp.sum(jnp.where(same, total, 0.0).reshape(n_trial, TILE, cols), axis=1)
    lane = lax.broadcasted_iota(jnp.int32, coef.shape, 1)
    step = 1
    while step < TILE:
        coef += jnp.where(
            (lane & step) != 0, pltpu.roll(coef, step, 1), pltpu.roll(coef, cols - step, 1)
        )
        step *= 2
    twice = 2.0 * coef.astype(BF16).astype(F32)
    spread = jnp.broadcast_to(twice[:, None, :], (n_trial, TILE, cols)).reshape(rows, cols)
    weights = jnp.where(same, spread, 0.0).astype(BF16)
    for t in range(tiles):
        acc_ref[:, t * TILE : (t + 1) * TILE, :] = -dot(weights, ov_tile(t)).reshape(
            n_trial, TILE, n_occ
        )


def build_kernel(low, group, cut, me_ref, occ_ref, vir_ref, own_ref, *refs):
    parts = 1 << low
    taken = parts if cut else 1
    pieces, refs = refs[:taken], refs[taken:]
    ov_ref, oo_ref, vv_ref = refs[:3]
    outs, (xs_ref, h_ref, acc_ref) = refs[3:-3], refs[-3:]
    n_trial, rows, n_virt = own_ref.shape
    n_aux, n_occ, _ = oo_ref.shape
    high_count = n_occ // rows >> low
    me = me_ref[0]
    mine, top = me & (parts - 1), me >> low
    if cut:
        for k in range(parts):
            for z in range(high_count):
                at = pl.multiple_of((((top ^ z) << low) | (mine ^ k)) * rows, rows)
                for m in range(n_trial):
                    xs_ref[m, pl.ds(at, rows), :] = pieces[k][z, m].astype(F32)
    else:
        xs_ref[...] = pieces[0][...].astype(F32)
    x = xs_ref[...].astype(BF16)
    flat = x.reshape(n_trial * n_occ, n_virt)
    coulomb_into(acc_ref, x, ov_ref)

    def advance(c, carry):
        first = c * group
        vv = vv_ref[pl.ds(first, group)].reshape(group * n_virt, n_virt)
        h_ref[...] = dot_nt(vv, flat).astype(BF16).reshape(group, n_virt, n_trial * n_occ)
        oo = jnp.concatenate([oo_ref[first + g] for g in range(group)], axis=1)
        for m in range(n_trial):
            half = jnp.concatenate(
                [h_ref[g, :, m * n_occ : (m + 1) * n_occ] for g in range(group)], axis=1
            )
            acc_ref[m] += dot_nt(half, oo)
        return carry

    lax.fori_loop(0, n_aux // group, advance, 0)
    unit = (
        lax.broadcasted_iota(jnp.int32, (n_occ, 2 * n_occ), 0)
        == lax.broadcasted_iota(jnp.int32, (n_occ, 2 * n_occ), 1) % n_occ
    ).astype(BF16)
    lines = []
    for m in range(n_trial):
        turned = acc_ref[m]
        high = turned.astype(BF16)
        rest = (turned - high.astype(F32)).astype(BF16)
        value = -dot_nt(unit, jnp.concatenate([high, rest], axis=1))
        seen = xs_ref[m]
        lines.append(jnp.sum(jnp.sum(seen * value, axis=0, keepdims=True), axis=1, keepdims=True))
        xs_ref[m] = value
    own = own_ref[...]
    square = own * own
    diag = diagonal(occ_ref, vir_ref, me * rows, rows)
    for m in range(n_trial):
        lines[m] += jnp.sum(
            jnp.sum(square[m] * diag, axis=0, keepdims=True), axis=1, keepdims=True
        )
    for m in range(n_trial):
        lines.append(
            jnp.sum(jnp.sum(square[m], axis=0, keepdims=True), axis=1, keepdims=True)
        )
    scalars = jnp.concatenate(
        [jnp.broadcast_to(line, (1, n_virt)) for line in lines], axis=0
    )
    single = jnp.where(
        lax.broadcasted_iota(jnp.int32, scalars.shape, 1) == 0, scalars, 0.0
    )
    coded = three_parts(scalars)
    if not cut:
        for ref, value in zip(outs, (xs_ref[...], single, coded)):
            ref[...] = value
        return
    body = high_count * n_trial * rows
    outs[0][body:, :] = single
    for k in range(parts):
        blocks = []
        for z in range(high_count):
            at = pl.multiple_of(((z << low) | (mine ^ k)) * rows, rows)
            blocks += [xs_ref[m, pl.ds(at, rows), :] for m in range(n_trial)]
        whole = jnp.concatenate(blocks, axis=0)
        if k == 0:
            outs[0][:body, :] = whole
        else:
            outs[k][:body, :] = whole.astype(BF16)
            outs[k][body:, :] = coded


def pack_kernel(*refs):
    for r, ref in enumerate(refs[:-1]):
        refs[-1][r] = ref[...].astype(BF16)


def pack(columns):
    return pl.pallas_call(
        pack_kernel,
        out_shape=jax.ShapeDtypeStruct((len(columns),) + columns[0].shape, BF16),
        in_specs=[VMEM] * len(columns),
        out_specs=VMEM,
        compiler_params=SMALL,
    )(*columns)


def build(me, occ, vir, own, pieces, coul_t, exch_oo, exch_vv, low):
    parts = len(pieces)
    high_count, n_trial, rows, n_virt = pieces[0].shape
    n_aux, n_occ, _ = exch_oo.shape
    group = TILE
    while n_aux % group:
        group //= 2
    cut = rows % 8 == 0
    height, extra = high_count * n_trial * rows, 2 * n_trial
    if cut:
        shapes = [jax.ShapeDtypeStruct((height + extra, n_virt), F32)]
        shapes += [jax.ShapeDtypeStruct((height + extra, n_virt), BF16)] * (parts - 1)
    else:
        order = me ^ jnp.arange(high_count * parts)
        placed = jnp.stack(pieces, 1).reshape(-1, n_trial, rows, n_virt)[order]
        pieces = [placed.transpose(1, 0, 2, 3).reshape(n_trial, n_occ, n_virt)]
        shapes = [
            jax.ShapeDtypeStruct((n_trial, n_occ, n_virt), F32),
            jax.ShapeDtypeStruct((extra, n_virt), F32),
            jax.ShapeDtypeStruct((extra, n_virt), BF16),
        ]
    flops = 2 * n_aux * n_trial * n_occ * n_virt * (n_virt + n_occ)
    moved = 2 * (coul_t.size + exch_oo.size + exch_vv.size)
    results = pl.pallas_call(
        functools.partial(build_kernel, low, group, cut),
        out_shape=shapes,
        in_specs=[SMEM] + [VMEM] * (6 + len(pieces)),
        out_specs=[VMEM] * len(shapes),
        scratch_shapes=[
            pltpu.VMEM((n_trial, n_occ, n_virt), F32),
            pltpu.VMEM((group, n_virt, n_trial * n_occ), BF16),
            pltpu.VMEM((n_trial, n_virt, n_occ), F32),
        ],
        compiler_params=pltpu.CompilerParams(vmem_limit_bytes=28 << 20),
        cost_estimate=pl.CostEstimate(flops=flops, bytes_accessed=moved, transcendentals=0),
    )(me[None], occ, vir, own, *pieces, *[
        pltpu.with_memory_space_constraint(a, pltpu.VMEM) for a in (coul_t, exch_oo, exch_vv)
    ])
    if cut:
        return results
    value, single, coded = results
    value = value.reshape(n_trial, high_count, parts, rows, n_virt).transpose(2, 1, 0, 3, 4)
    mine = me & (parts - 1)
    blocks = [
        lax.dynamic_index_in_dim(value, mine ^ k, 0, keepdims=False).reshape(height, n_virt)
        for k in range(parts)
    ]
    return [jnp.concatenate([blocks[0], single], axis=0)] + [
        jnp.concatenate([block.astype(BF16), coded], axis=0) for block in blocks[1:]
    ]


def summed(own_ref, arrived):
    total = own_ref[...]
    for ref in arrived:
        total += ref[...].astype(F32)
    return total


def combine_kernel(extra, own_ref, *refs):
    arrived, (total_ref, send_ref) = refs[:-2], refs[-2:]
    total = summed(own_ref, arrived)
    body = total.shape[0] - extra
    scalars = jnp.sum(total[body:], axis=1, keepdims=True)
    scalars = jnp.broadcast_to(scalars, (extra, total.shape[1]))
    lane = lax.broadcasted_iota(jnp.int32, scalars.shape, 1)
    total_ref[:body, :] = total[:body]
    total_ref[body:, :] = jnp.where(lane == 0, scalars, 0.0)
    send_ref[:body, :] = total[:body].astype(BF16)
    send_ref[body:, :] = three_parts(scalars)


def combine(own, arrived, extra):
    return pl.pallas_call(
        functools.partial(combine_kernel, extra),
        out_shape=[
            jax.ShapeDtypeStruct(own.shape, F32),
            jax.ShapeDtypeStruct(own.shape, BF16),
        ],
        in_specs=[VMEM] * (1 + len(arrived)),
        out_specs=[VMEM] * 2,
        compiler_params=SMALL,
    )(own, *arrived)


def residual_kernel(low, high_count, me_ref, occ_ref, vir_ref, own_ref, *refs):
    columns, refs = refs[:high_count], refs[high_count:]
    arrived, (sigma_ref, precond_ref, square_ref, held_ref) = refs[:-4], refs[-4:]
    n_trial, rows, n_virt = columns[0].shape
    body = high_count * n_trial * rows
    mine, top = me_ref[0] & ((1 << low) - 1), me_ref[0] >> low
    total = summed(own_ref, arrived)
    held_ref[...] = total[:body].reshape(held_ref.shape)
    scalars = jnp.sum(total[body:], axis=1, keepdims=True)
    omega = scalars[:n_trial] / (scalars[n_trial:] + 1e-06)
    squares = [jnp.zeros((rows, n_virt), F32) for _ in range(n_trial)]
    for r in range(high_count):
        diag = diagonal(occ_ref, vir_ref, (((top ^ r) << low) | mine) * rows, rows)
        block = held_ref[top ^ r]
        for m in range(n_trial):
            t = columns[r][m]
            level = omega[m : m + 1]
            sigma = diag * t + block[m * rows : (m + 1) * rows]
            precond = (sigma - level * t) / jnp.maximum(jnp.abs(diag - level), 1.0)
            squares[m] += precond * precond
            if r == 0:
                sigma_ref[m] = sigma
                precond_ref[m] = precond
    sums = [
        jnp.sum(jnp.sum(s, axis=0, keepdims=True), axis=1, keepdims=True) for s in squares
    ]
    square_ref[...] = jnp.concatenate(
        [jnp.broadcast_to(s, (1, square_ref.shape[1])) for s in sums], axis=0
    )


def residual(me, occ, vir, low, columns, own, arrived):
    n_trial, rows, n_virt = columns[0].shape
    block = jax.ShapeDtypeStruct((n_trial, rows, n_virt), F32)
    return pl.pallas_call(
        functools.partial(residual_kernel, low, len(columns)),
        out_shape=[block, block, jax.ShapeDtypeStruct((n_trial, 128), F32)],
        in_specs=[SMEM] + [VMEM] * (3 + len(columns) + len(arrived)),
        out_specs=[VMEM] * 3,
        scratch_shapes=[pltpu.VMEM((len(columns), n_trial * rows, n_virt), F32)],
        compiler_params=SMALL,
    )(me[None], occ, vir, own, *columns, *arrived)


def finish_kernel(count, precond_ref, *refs):
    update_ref = refs[-1]
    square = refs[0][...]
    for ref in refs[1:-1]:
        square += ref[...]
    scale = lax.rsqrt(square[:, :1] / count + 1e-06)
    for m in range(precond_ref.shape[0]):
        update_ref[m] = precond_ref[m] * scale[m : m + 1]


def finish(count, precond, squares):
    return pl.pallas_call(
        functools.partial(finish_kernel, count),
        out_shape=jax.ShapeDtypeStruct(precond.shape, F32),
        in_specs=[VMEM] * (1 + len(squares)),
        out_specs=VMEM,
        compiler_params=SMALL,
    )(precond, *squares)


def fetch_kernel(cuts, me_ref, *refs):
    del me_ref
    count = len(cuts)
    sources, targets, sem = refs[:count], refs[count : 2 * count], refs[-1]
    copies = []
    for source, target, cut in zip(sources, targets, cuts):
        step = source.shape[0] // cut
        for c in range(cut):
            at = pl.ds(c * step, step)
            copies.append(
                pltpu.make_async_copy(source.at[at], target.at[at], sem.at[len(copies)])
            )
    for copy in copies:
        copy.start()
    for copy in copies:
        copy.wait()


def fetch(me, *arrays):
    cuts = [math.gcd(a.shape[0], 8) if a.size > 1 << 18 else 1 for a in arrays]
    return pl.pallas_call(
        functools.partial(fetch_kernel, cuts),
        out_shape=[pltpu.VMEM(a.shape, a.dtype) for a in arrays],
        in_specs=[SMEM] + [pl.BlockSpec(memory_space=pltpu.HBM)] * len(arrays),
        out_specs=[VMEM] * len(arrays),
        scratch_shapes=[pltpu.SemaphoreType.DMA((sum(cuts),))],
        compiler_params=SMALL,
        cost_estimate=pl.CostEstimate(
            flops=0, bytes_accessed=sum(4 * a.size for a in arrays), transcendentals=0
        ),
    )(me[None], *[pltpu.with_memory_space_constraint(a, pltpu.HBM) for a in arrays])


def on_device(size, trial_vecs, occ_energy, vir_energy, coul_ov, exch_oo, exch_vv):
    n_trial, rows, n_virt = trial_vecs.shape
    n_occ = exch_oo.shape[1]
    low, highs = bit_groups(size)
    me = lax.axis_index("aux").astype(jnp.int32)
    coul_t = jnp.transpose(coul_ov, (0, 2, 1))
    near, occ, vir, coul_t, exch_oo, exch_vv = fetch(
        me, trial_vecs, occ_energy[None], vir_energy[None], coul_t, exch_oo, exch_vv
    )
    columns = [near]
    for at, width in highs:
        if len(columns) == 1:
            columns += exchange(trial_vecs, size, at, width)
        else:
            moved = exchange(jnp.stack(columns), size, at, width)
            columns += [block[r] for block in moved for r in range(len(columns))]
    rounded = pack(columns)
    pieces = [rounded] + exchange(rounded, size, 0, low)
    own, *sends = build(
        me, occ, vir, near, pieces, coul_t, exch_oo, exch_vv, low
    )
    arrived = [swap(send, size, k + 1) for k, send in enumerate(sends)]
    for at, width in highs:
        own, send = combine(own, arrived, 2 * n_trial)
        arrived = exchange(send, size, at, width)
    sigma_vecs, precond, square = residual(me, occ, vir, low, columns, own, arrived)
    squares = [square] + exchange(square, size, 0, low)
    return sigma_vecs, finish(n_occ * n_virt, precond, squares)


def solution(mesh):
    in_specs = (
        P("geom", "aux", None),
        P("geom"),
        P("geom"),
        P(("geom", "aux"), None, None),
        P(("geom", "aux"), None, None),
        P(("geom", "aux"), None, None),
    )
    out_specs = (P("geom", "aux", None), P("geom", "aux", None))
    return jax.shard_map(
        functools.partial(on_device, mesh.shape["aux"]),
        mesh=mesh,
        in_specs=in_specs,
        out_specs=out_specs,
        check_vma=False,
    )
```

```python
import functools
import math

import jax
import jax.numpy as jnp
from jax import lax
from jax.experimental import pallas as pl
from jax.experimental.pallas import tpu as pltpu
from jax.sharding import PartitionSpec as P


F32 = jnp.float32
BF16 = jnp.bfloat16
LOW_BITS = 2
TILE = 16
VMEM = pl.BlockSpec(memory_space=pltpu.VMEM)
SMEM = pl.BlockSpec(memory_space=pltpu.SMEM)
SMALL = pltpu.CompilerParams(vmem_limit_bytes=4 << 20)


def bit_groups(size):
    bits = size.bit_length() - 1
    assert size == 1 << bits
    low = min(LOW_BITS, bits)
    return low, [(at, min(LOW_BITS, bits - at)) for at in range(low, bits, LOW_BITS)]


def swap(value, size, offset):
    return lax.ppermute(value, "aux", [(i, i ^ offset) for i in range(size)])


def exchange(value, size, at, width):
    return [swap(value, size, k << at) for k in range(1, 1 << width)]


def dot(a, b):
    return jnp.dot(a, b, preferred_element_type=F32)


def dot_nt(a, b):
    return lax.dot_general(a, b, (((1,), (1,)), ((), ())), preferred_element_type=F32)


def diagonal(occ_ref, vir_ref, first, rows):
    shape = (rows, occ_ref.shape[1])
    wanted = lax.broadcasted_iota(jnp.int32, shape, 0) + first
    picked = jnp.where(lax.broadcasted_iota(jnp.int32, shape, 1) == wanted, occ_ref[...], 0.0)
    return vir_ref[...] - jnp.sum(picked, axis=1, keepdims=True)


def three_parts(value):
    high = value.astype(BF16).astype(F32)
    middle = (value - high).astype(BF16).astype(F32)
    rest = value - high - middle
    lane = lax.broadcasted_iota(jnp.int32, value.shape, 1)
    return jnp.where(
        lane == 0, high, jnp.where(lane == 1, middle, jnp.where(lane == 2, rest, 0.0))
    ).astype(BF16)


def coulomb_into(acc_ref, x, ov_ref):
    n_aux, n_virt, n_occ = ov_ref.shape
    n_trial = x.shape[0]
    tiles = n_virt // TILE
    unit = (
        lax.broadcasted_iota(jnp.int32, (n_virt, n_virt), 0)
        == lax.broadcasted_iota(jnp.int32, (n_virt, n_virt), 1)
    ).astype(BF16)
    x_t = jnp.stack([dot_nt(unit, x[m]).astype(BF16) for m in range(n_trial)], 0)
    rows, cols = n_trial * TILE, n_aux * TILE

    def x_tile(t):
        return x_t[:, t * TILE : (t + 1) * TILE, :].reshape(rows, n_occ)

    def ov_tile(t):
        return ov_ref[:, t * TILE : (t + 1) * TILE, :].reshape(cols, n_occ)

    total = jnp.zeros((rows, cols), F32)
    for t in range(0, tiles, 2):
        span = range(t, min(t + 2, tiles))
        total += dot_nt(
            jnp.concatenate([x_tile(u) for u in span], axis=1),
            jnp.concatenate([ov_tile(u) for u in span], axis=1),
        )
    same = (
        lax.broadcasted_iota(jnp.int32, (rows, cols), 0) % TILE
        == lax.broadcasted_iota(jnp.int32, (rows, cols), 1) % TILE
    )
    coef = jnp.sum(jnp.where(same, total, 0.0).reshape(n_trial, TILE, cols), axis=1)
    lane = lax.broadcasted_iota(jnp.int32, coef.shape, 1)
    step = 1
    while step < TILE:
        coef += jnp.where(
            (lane & step) != 0, pltpu.roll(coef, step, 1), pltpu.roll(coef, cols - step, 1)
        )
        step *= 2
    twice = 2.0 * coef.astype(BF16).astype(F32)
    spread = jnp.broadcast_to(twice[:, None, :], (n_trial, TILE, cols)).reshape(rows, cols)
    weights = jnp.where(same, spread, 0.0).astype(BF16)
    for t in range(0, tiles, 2):
        span = range(t, min(t + 2, tiles))
        sums = dot(weights, jnp.concatenate([ov_tile(u) for u in span], axis=1))
        for k, u in enumerate(span):
            acc_ref[:, u * TILE : (u + 1) * TILE, :] -= sums[
                :, k * n_occ : (k + 1) * n_occ
            ].reshape(n_trial, TILE, n_occ)


def contract_half(high, x, oo_ref, vv_ref, acc_ref, h_ref, group):
    n_trial, half, n_virt = x.shape
    n_aux, n_occ, _ = oo_ref.shape
    pairs = group // 2
    order = [m ^ 1 for m in range(n_trial)]
    flat = x.reshape(n_trial * half, n_virt)
    turned = jnp.concatenate([x[m] for m in order], axis=0)
    left = lax.broadcasted_iota(jnp.int32, (n_virt, n_occ), 1) < half
    left_oo = left if n_virt == n_occ else lax.broadcasted_iota(jnp.int32, (n_occ, n_occ), 1) < half
    upper = (lax.broadcasted_iota(jnp.int32, (n_occ, n_occ), 1) * 0 + high) == 1

    def advance(c, carry):
        first = c * group
        for odd, columns in enumerate((flat, turned)):
            vv = jnp.concatenate([vv_ref[first + 2 * g + odd] for g in range(pairs)], axis=0)
            h_ref[odd] = dot_nt(vv, columns).reshape(pairs, n_virt, n_trial * half)
        fore, back = [], []
        for g in range(pairs):
            placed = []
            for odd in range(2):
                straight = oo_ref[first + 2 * g + odd].astype(F32)
                moved = pltpu.roll(straight, half, 1)
                placed.append(
                    (jnp.where(upper, moved, straight), jnp.where(upper, straight, moved))
                )
            fore.append(jnp.where(left_oo, placed[0][0], placed[1][1]).astype(BF16))
            back.append(jnp.where(left_oo, placed[1][0], placed[0][1]).astype(BF16))
        weights = [jnp.concatenate(fore, axis=1), jnp.concatenate(back, axis=1)]
        for m in range(n_trial):
            at = slice(m // 2 * n_occ, (m // 2 + 1) * n_occ)
            one, two = (0, 1) if m % 2 == 0 else (1, 0)
            lines = jnp.concatenate(
                [
                    jnp.where(left, h_ref[one, g, :, at], h_ref[two, g, :, at]).astype(BF16)
                    for g in range(pairs)
                ],
                axis=1,
            )
            acc_ref[m] += dot_nt(lines, weights[m % 2])
        return carry

    lax.fori_loop(0, n_aux // group, advance, 0)


def place(target_ref, pieces_ref, first, mask, rows):
    for d in range(pieces_ref.shape[0]):
        at = pl.multiple_of(((first ^ d) & mask) * rows, rows)
        for m in range(pieces_ref.shape[1]):
            target_ref[m, pl.ds(at, rows), :] = pieces_ref[d, m].astype(F32)


def half_kernel(group, cut, me_ref, half_ref, oo_ref, vv_ref, acc_ref, xs_ref, h_ref):
    high = me_ref[1]
    if cut:
        place(xs_ref, half_ref, me_ref[0], half_ref.shape[0] - 1, half_ref.shape[2])
    else:
        xs_ref[...] = half_ref[...].astype(F32)
    acc_ref[...] = jnp.zeros_like(acc_ref)
    contract_half(high, xs_ref[...].astype(BF16), oo_ref, vv_ref, acc_ref, h_ref, group)


def build_kernel(low, group, cut, me_ref, occ_ref, vir_ref, own_ref, held_ref, *refs):
    parts = 1 << low
    pieces, (ov_ref, oo_ref, vv_ref), outs = refs[:2], refs[2:5], refs[5:-3]
    xs_ref, h_ref, acc_ref = refs[-3:]
    n_trial, rows, n_virt = own_ref.shape
    n_aux, n_occ, _ = oo_ref.shape
    size, half = n_occ // rows, n_occ // 2
    high_count = size >> low
    me, other = me_ref[0], 1 - me_ref[1]
    mine = me & (parts - 1)
    if cut:
        place(xs_ref, pieces[0], me, size - 1, rows)
        place(xs_ref, pieces[1], me ^ (size // 2), size - 1, rows)
    else:
        for k, piece in enumerate(pieces):
            at = pl.multiple_of((me_ref[1] ^ k) * half, half)
            for m in range(n_trial):
                xs_ref[m, pl.ds(at, half), :] = piece[m].astype(F32)
    x = xs_ref[...].astype(BF16)
    acc_ref[...] = held_ref[...]
    coulomb_into(acc_ref, x, ov_ref)
    rest = pl.ds(pl.multiple_of(other * half, half), half)
    x_rest = jnp.stack([xs_ref[m, rest, :] for m in range(n_trial)], 0).astype(BF16)
    contract_half(other, x_rest, oo_ref, vv_ref, acc_ref, h_ref, group)
    unit = (
        lax.broadcasted_iota(jnp.int32, (n_occ, 2 * n_occ), 0)
        == lax.broadcasted_iota(jnp.int32, (n_occ, 2 * n_occ), 1) % n_occ
    ).astype(BF16)
    lines = []
    for m in range(n_trial):
        turned = acc_ref[m]
        high = turned.astype(BF16)
        rest = (turned - high.astype(F32)).astype(BF16)
        value = -dot_nt(unit, jnp.concatenate([high, rest], axis=1))
        seen = xs_ref[m]
        lines.append(jnp.sum(jnp.sum(seen * value, axis=0, keepdims=True), axis=1, keepdims=True))
        xs_ref[m] = value
    own = own_ref[...]
    square = own * own
    diag = diagonal(occ_ref, vir_ref, me * rows, rows)
    for m in range(n_trial):
        lines[m] += jnp.sum(
            jnp.sum(square[m] * diag, axis=0, keepdims=True), axis=1, keepdims=True
        )
    for m in range(n_trial):
        lines.append(
            jnp.sum(jnp.sum(square[m], axis=0, keepdims=True), axis=1, keepdims=True)
        )
    scalars = jnp.concatenate(
        [jnp.broadcast_to(line, (1, n_virt)) for line in lines], axis=0
    )
    single = jnp.where(
        lax.broadcasted_iota(jnp.int32, scalars.shape, 1) == 0, scalars, 0.0
    )
    coded = three_parts(scalars)
    if not cut:
        for ref, value in zip(outs, (xs_ref[...], single, coded)):
            ref[...] = value
        return
    body = high_count * n_trial * rows
    outs[0][body:, :] = single
    for k in range(parts):
        blocks = []
        for z in range(high_count):
            at = pl.multiple_of(((z << low) | (mine ^ k)) * rows, rows)
            blocks += [xs_ref[m, pl.ds(at, rows), :] for m in range(n_trial)]
        whole = jnp.concatenate(blocks, axis=0)
        if k == 0:
            outs[0][:body, :] = whole
        else:
            outs[k][:body, :] = whole.astype(BF16)
            outs[k][body:, :] = coded


def pack_kernel(*refs):
    at = 0
    for ref in refs[:-1]:
        count = ref.shape[0]
        refs[-1][at : at + count] = ref[...].astype(BF16)
        at += count


def pack(arrays):
    count = sum(a.shape[0] for a in arrays)
    return pl.pallas_call(
        pack_kernel,
        out_shape=jax.ShapeDtypeStruct((count,) + arrays[0].shape[1:], BF16),
        in_specs=[VMEM] * len(arrays),
        out_specs=VMEM,
        compiler_params=SMALL,
    )(*arrays)


def in_vmem(*arrays):
    return [pltpu.with_memory_space_constraint(a, pltpu.VMEM) for a in arrays]


def group_of(n_aux):
    group = TILE
    while n_aux % group:
        group //= 2
    return group


def in_order(half, me):
    count, n_trial, rows, n_virt = half.shape
    order = (me & (count - 1)) ^ jnp.arange(count)
    return half[order].transpose(1, 0, 2, 3).reshape(n_trial, count * rows, n_virt)


def first_half(me_pair, half, exch_oo, exch_vv):
    cut = half.ndim == 4
    n_aux, n_occ, _ = exch_oo.shape
    n_virt = half.shape[-1]
    n_trial = half.shape[1] if cut else half.shape[0]
    group = group_of(n_aux)
    flops = n_aux * n_trial * n_occ * n_virt * (n_virt + n_occ)
    return pl.pallas_call(
        functools.partial(half_kernel, group, cut),
        out_shape=jax.ShapeDtypeStruct((n_trial, n_virt, n_occ), F32),
        in_specs=[SMEM] + [VMEM] * 3,
        out_specs=VMEM,
        scratch_shapes=[
            pltpu.VMEM((n_trial, n_occ // 2, n_virt), F32),
            pltpu.VMEM((2, group // 2, n_virt, n_trial * n_occ // 2), F32),
        ],
        compiler_params=pltpu.CompilerParams(vmem_limit_bytes=28 << 20),
        cost_estimate=pl.CostEstimate(
            flops=flops,
            bytes_accessed=2 * (exch_oo.size + exch_vv.size),
            transcendentals=0,
        ),
    )(me_pair, half, *in_vmem(exch_oo, exch_vv))


def build(me_pair, occ, vir, own, held, pieces, coul_t, exch_oo, exch_vv, low):
    parts = 1 << low
    n_trial, rows, n_virt = own.shape
    n_aux, n_occ, _ = exch_oo.shape
    high_count = n_occ // rows >> low
    group = group_of(n_aux)
    cut = pieces[0].ndim == 4
    height, extra = high_count * n_trial * rows, 2 * n_trial
    if cut:
        shapes = [jax.ShapeDtypeStruct((height + extra, n_virt), F32)]
        shapes += [jax.ShapeDtypeStruct((height + extra, n_virt), BF16)] * (parts - 1)
    else:
        shapes = [
            jax.ShapeDtypeStruct((n_trial, n_occ, n_virt), F32),
            jax.ShapeDtypeStruct((extra, n_virt), F32),
            jax.ShapeDtypeStruct((extra, n_virt), BF16),
        ]
    flops = n_aux * n_trial * n_occ * n_virt * (n_virt + n_occ)
    moved = 2 * (coul_t.size + exch_oo.size + exch_vv.size)
    results = pl.pallas_call(
        functools.partial(build_kernel, low, group, cut),
        out_shape=shapes,
        in_specs=[SMEM] + [VMEM] * 9,
        out_specs=[VMEM] * len(shapes),
        scratch_shapes=[
            pltpu.VMEM((n_trial, n_occ, n_virt), F32),
            pltpu.VMEM((2, group // 2, n_virt, n_trial * n_occ // 2), F32),
            pltpu.VMEM((n_trial, n_virt, n_occ), F32),
        ],
        compiler_params=pltpu.CompilerParams(vmem_limit_bytes=28 << 20),
        cost_estimate=pl.CostEstimate(flops=flops, bytes_accessed=moved, transcendentals=0),
    )(me_pair, occ, vir, own, held, *pieces, *in_vmem(coul_t, exch_oo, exch_vv))
    if cut:
        return results
    value, single, coded = results
    value = value.reshape(n_trial, high_count, parts, rows, n_virt).transpose(2, 1, 0, 3, 4)
    mine = me_pair[0] & (parts - 1)
    blocks = [
        lax.dynamic_index_in_dim(value, mine ^ k, 0, keepdims=False).reshape(height, n_virt)
        for k in range(parts)
    ]
    return [jnp.concatenate([blocks[0], single], axis=0)] + [
        jnp.concatenate([block.astype(BF16), coded], axis=0) for block in blocks[1:]
    ]


def summed(own_ref, arrived):
    total = own_ref[...]
    for ref in arrived:
        total += ref[...].astype(F32)
    return total


def combine_kernel(extra, own_ref, *refs):
    arrived, (total_ref, send_ref) = refs[:-2], refs[-2:]
    total = summed(own_ref, arrived)
    body = total.shape[0] - extra
    scalars = jnp.sum(total[body:], axis=1, keepdims=True)
    scalars = jnp.broadcast_to(scalars, (extra, total.shape[1]))
    lane = lax.broadcasted_iota(jnp.int32, scalars.shape, 1)
    total_ref[:body, :] = total[:body]
    total_ref[body:, :] = jnp.where(lane == 0, scalars, 0.0)
    send_ref[:body, :] = total[:body].astype(BF16)
    send_ref[body:, :] = three_parts(scalars)


def combine(own, arrived, extra):
    return pl.pallas_call(
        functools.partial(combine_kernel, extra),
        out_shape=[
            jax.ShapeDtypeStruct(own.shape, F32),
            jax.ShapeDtypeStruct(own.shape, BF16),
        ],
        in_specs=[VMEM] * (1 + len(arrived)),
        out_specs=[VMEM] * 2,
        compiler_params=SMALL,
    )(own, *arrived)


def residual_kernel(low, me_ref, occ_ref, vir_ref, near_ref, near_half, far_half, own_ref, *refs):
    arrived, (sigma_ref, precond_ref, square_ref, held_ref) = refs[:-4], refs[-4:]
    n_trial, rows, n_virt = near_ref.shape
    count = near_half.shape[0]
    high_count = 2 * count >> low
    body = high_count * n_trial * rows
    mine, top = me_ref[0] & ((1 << low) - 1), me_ref[0] >> low
    total = summed(own_ref, arrived)
    held_ref[...] = total[:body].reshape(held_ref.shape)
    scalars = jnp.sum(total[body:], axis=1, keepdims=True)
    omega = scalars[:n_trial] / (scalars[n_trial:] + 1e-06)
    squares = [jnp.zeros((rows, n_virt), F32) for _ in range(n_trial)]
    for r in range(high_count):
        diag = diagonal(occ_ref, vir_ref, (((top ^ r) << low) | mine) * rows, rows)
        block = held_ref[top ^ r]
        for m in range(n_trial):
            away = r << low
            if r == 0:
                t = near_ref[m]
            else:
                t = (near_half if away < count else far_half)[away % count, m].astype(F32)
            level = omega[m : m + 1]
            sigma = diag * t + block[m * rows : (m + 1) * rows]
            precond = (sigma - level * t) / jnp.maximum(jnp.abs(diag - level), 1.0)
            squares[m] += precond * precond
            if r == 0:
                sigma_ref[m] = sigma
                precond_ref[m] = precond
    sums = [
        jnp.sum(jnp.sum(s, axis=0, keepdims=True), axis=1, keepdims=True) for s in squares
    ]
    square_ref[...] = jnp.concatenate(
        [jnp.broadcast_to(s, (1, square_ref.shape[1])) for s in sums], axis=0
    )


def residual(me_pair, occ, vir, low, near, halves, own, arrived):
    n_trial, rows, n_virt = near.shape
    high_count = 2 * halves[0].shape[0] >> low
    return pl.pallas_call(
        functools.partial(residual_kernel, low),
        out_shape=[pltpu.VMEM(near.shape, F32)] * 2 + [pltpu.VMEM((n_trial, 128), F32)],
        in_specs=[SMEM] + [VMEM] * (6 + len(arrived)),
        out_specs=[VMEM] * 3,
        scratch_shapes=[pltpu.VMEM((high_count, n_trial * rows, n_virt), F32)],
        compiler_params=SMALL,
    )(me_pair, occ, vir, near, *halves, own, *arrived)


def finish_kernel(count, precond_ref, *refs):
    update_ref = refs[-1]
    square = refs[0][...]
    for ref in refs[1:-1]:
        square += ref[...]
    scale = lax.rsqrt(square[:, :1] / count + 1e-06)
    for m in range(precond_ref.shape[0]):
        update_ref[m] = precond_ref[m] * scale[m : m + 1]


def finish(count, precond, squares):
    return pl.pallas_call(
        functools.partial(finish_kernel, count),
        out_shape=jax.ShapeDtypeStruct(precond.shape, F32),
        in_specs=[VMEM] * (1 + len(squares)),
        out_specs=VMEM,
        compiler_params=SMALL,
    )(precond, *squares)


def fetch_kernel(cuts, after_ref, *refs):
    del after_ref
    count = len(cuts)
    sources, targets, sem = refs[:count], refs[count : 2 * count], refs[-1]
    copies = []
    for source, target, cut in zip(sources, targets, cuts):
        step = source.shape[0] // cut
        for c in range(cut):
            at = pl.ds(c * step, step)
            copies.append(
                pltpu.make_async_copy(source.at[at], target.at[at], sem.at[len(copies)])
            )
    for copy in copies:
        copy.start()
    for copy in copies:
        copy.wait()


def fetch(after, *arrays):
    cuts = [math.gcd(a.shape[0], 8) if a.size > 1 << 18 else 1 for a in arrays]
    return pl.pallas_call(
        functools.partial(fetch_kernel, cuts),
        out_shape=[pltpu.VMEM(a.shape, a.dtype) for a in arrays],
        in_specs=[pl.BlockSpec(memory_space=pl.ANY)] + [pl.BlockSpec(memory_space=pltpu.HBM)] * len(arrays),
        out_specs=[VMEM] * len(arrays),
        scratch_shapes=[pltpu.SemaphoreType.DMA((sum(cuts),))],
        compiler_params=SMALL,
        cost_estimate=pl.CostEstimate(
            flops=0, bytes_accessed=sum(4 * a.size for a in arrays), transcendentals=0
        ),
    )(after, *[pltpu.with_memory_space_constraint(a, pltpu.HBM) for a in arrays])


def on_device(size, trial_vecs, occ_energy, vir_energy, coul_ov, exch_oo, exch_vv):
    n_trial, rows, n_virt = trial_vecs.shape
    n_occ = exch_oo.shape[1]
    low, highs = bit_groups(size)
    me = lax.axis_index("aux").astype(jnp.int32)
    top = size.bit_length() - 2
    me_pair = jnp.stack([me, me >> top])
    near, occ, vir, oo = fetch(me_pair, trial_vecs, occ_energy[None], vir_energy[None], exch_oo)
    held = pack([near[None]] + [a[None] for a in exchange(trial_vecs, size, 0, 1)])
    vv, = fetch(held, exch_vv)
    for at in range(1, top, 2):
        held = pack([held] + exchange(held, size, at, min(2, top - at)))
    far, = exchange(held, size, top, 1)
    halves = [held, far]
    pieces = halves if rows % 8 == 0 else [in_order(half, me) for half in halves]
    half_sum = first_half(me_pair, pieces[0], oo, vv)
    coul_t, = fetch(held, jnp.transpose(coul_ov, (0, 2, 1)))
    own, *sends = build(me_pair, occ, vir, near, half_sum, pieces, coul_t, oo, vv, low)
    arrived = [swap(send, size, k + 1) for k, send in enumerate(sends)]
    for at, width in highs:
        own, send = combine(own, arrived, 2 * n_trial)
        arrived = exchange(send, size, at, width)
    sigma_vecs, precond, square = residual(me_pair, occ, vir, low, near, halves, own, arrived)
    squares = [square] + exchange(square, size, 0, low)
    return sigma_vecs, finish(n_occ * n_virt, precond, squares)


def solution(mesh):
    in_specs = (
        P("geom", "aux", None),
        P("geom"),
        P("geom"),
        P(("geom", "aux"), None, None),
        P(("geom", "aux"), None, None),
        P(("geom", "aux"), None, None),
    )
    out_specs = (P("geom", "aux", None), P("geom", "aux", None))
    return jax.shard_map(
        functools.partial(on_device, mesh.shape["aux"]),
        mesh=mesh,
        in_specs=in_specs,
        out_specs=out_specs,
        check_vma=False,
    )
```

```python
import functools

import jax
import jax.numpy as jnp
from jax import lax
from jax.experimental import pallas as pl
from jax.experimental.pallas import tpu as pltpu
from jax.sharding import PartitionSpec as P


F32 = jnp.float32
BF16 = jnp.bfloat16
LOW_BITS = 2
TILE = 16
VMEM = pl.BlockSpec(memory_space=pltpu.VMEM)
SMEM = pl.BlockSpec(memory_space=pltpu.SMEM)
HBM = pl.BlockSpec(memory_space=pltpu.HBM)
ANY = pl.BlockSpec(memory_space=pl.ANY)
SMALL = pltpu.CompilerParams(vmem_limit_bytes=4 << 20)


def bit_groups(size):
    bits = size.bit_length() - 1
    assert size == 1 << bits
    low = min(LOW_BITS, bits)
    return low, [(at, min(LOW_BITS, bits - at)) for at in range(low, bits, LOW_BITS)]


def swap(value, size, offset):
    return lax.ppermute(value, "aux", [(i, i ^ offset) for i in range(size)])


def exchange(value, size, at, width):
    return [swap(value, size, k << at) for k in range(1, 1 << width)]


def dot(a, b):
    return jnp.dot(a, b, preferred_element_type=F32)


def dot_nt(a, b):
    return lax.dot_general(a, b, (((1,), (1,)), ((), ())), preferred_element_type=F32)


def diagonal(occ_ref, vir_ref, first, rows):
    shape = (rows, occ_ref.shape[1])
    wanted = lax.broadcasted_iota(jnp.int32, shape, 0) + first
    picked = jnp.where(lax.broadcasted_iota(jnp.int32, shape, 1) == wanted, occ_ref[...], 0.0)
    return vir_ref[...] - jnp.sum(picked, axis=1, keepdims=True)


def three_parts(value):
    high = value.astype(BF16).astype(F32)
    middle = (value - high).astype(BF16).astype(F32)
    rest = value - high - middle
    lane = lax.broadcasted_iota(jnp.int32, value.shape, 1)
    return jnp.where(
        lane == 0, high, jnp.where(lane == 1, middle, jnp.where(lane == 2, rest, 0.0))
    ).astype(BF16)


def coulomb_into(acc_ref, x, ov_ref):
    n_aux, n_virt, n_occ = ov_ref.shape
    n_trial = x.shape[0]
    tiles = n_virt // TILE
    unit = (
        lax.broadcasted_iota(jnp.int32, (n_virt, n_virt), 0)
        == lax.broadcasted_iota(jnp.int32, (n_virt, n_virt), 1)
    ).astype(BF16)
    x_t = jnp.stack([dot_nt(unit, x[m]).astype(BF16) for m in range(n_trial)], 0)
    rows, cols = n_trial * TILE, n_aux * TILE

    def x_tile(t):
        return x_t[:, t * TILE : (t + 1) * TILE, :].reshape(rows, n_occ)

    def ov_tile(t):
        return ov_ref[:, t * TILE : (t + 1) * TILE, :].reshape(cols, n_occ)

    total = jnp.zeros((rows, cols), F32)
    for t in range(0, tiles, 2):
        span = range(t, min(t + 2, tiles))
        total += dot_nt(
            jnp.concatenate([x_tile(u) for u in span], axis=1),
            jnp.concatenate([ov_tile(u) for u in span], axis=1),
        )
    same = (
        lax.broadcasted_iota(jnp.int32, (rows, cols), 0) % TILE
        == lax.broadcasted_iota(jnp.int32, (rows, cols), 1) % TILE
    )
    coef = jnp.sum(jnp.where(same, total, 0.0).reshape(n_trial, TILE, cols), axis=1)
    lane = lax.broadcasted_iota(jnp.int32, coef.shape, 1)
    step = 1
    while step < TILE:
        coef += jnp.where(
            (lane & step) != 0, pltpu.roll(coef, step, 1), pltpu.roll(coef, cols - step, 1)
        )
        step *= 2
    twice = 2.0 * coef.astype(BF16).astype(F32)
    spread = jnp.broadcast_to(twice[:, None, :], (n_trial, TILE, cols)).reshape(rows, cols)
    weights = jnp.where(same, spread, 0.0).astype(BF16)
    for t in range(0, tiles, 2):
        span = range(t, min(t + 2, tiles))
        sums = dot(weights, jnp.concatenate([ov_tile(u) for u in span], axis=1))
        for k, u in enumerate(span):
            acc_ref[:, u * TILE : (u + 1) * TILE, :] -= sums[
                :, k * n_occ : (k + 1) * n_occ
            ].reshape(n_trial, TILE, n_occ)


def pair_weights(high, oo_ref, pair_ref):
    n_aux, n_occ, _ = oo_ref.shape
    half = n_occ // 2
    lane = lax.broadcasted_iota(jnp.int32, (n_occ, n_occ), 1)
    left, upper = lane < half, lane * 0 + high == 1

    def pair(g, carry):
        sides = []
        for odd in range(2):
            straight = oo_ref[2 * g + odd].astype(F32)
            moved = pltpu.roll(straight, half, 1)
            same, other = jnp.where(upper, moved, straight), jnp.where(upper, straight, moved)
            sides.append((same, other))
        for k in range(2):
            for odd in range(2):
                pair_ref[k, odd, g] = jnp.where(
                    left, sides[odd][k], sides[1 - odd][1 - k]
                ).astype(BF16)
        return carry

    lax.fori_loop(0, n_aux // 2, pair, 0)


def contract_half(x, pair_ref, k, vv_refs, acc_ref, mid_ref, ready=None):
    n_trial, half, n_virt = x.shape
    n_occ = 2 * half
    width = n_trial * half
    orders = [
        jnp.concatenate([x[m ^ odd] for m in range(n_trial)], axis=0) for odd in range(2)
    ]
    at = 0
    for step, vv_ref in enumerate(vv_refs):
        if ready is not None and step == 1:
            ready()
        pairs = vv_ref.shape[0] // 2
        even, odd = (
            dot_nt(
                jnp.concatenate([vv_ref[2 * g + odd] for g in range(pairs)], axis=0),
                orders[odd],
            )
            for odd in range(2)
        )
        left = lax.broadcasted_iota(jnp.int32, even.shape, 1) % n_occ < half
        shape = (pairs, n_virt, width)
        mid_ref[0, at : at + pairs] = jnp.where(left, even, odd).astype(BF16).reshape(shape)
        mid_ref[1, at : at + pairs] = jnp.where(left, odd, even).astype(BF16).reshape(shape)
        at += pairs
    for odd in range(2):
        weights = jnp.concatenate([pair_ref[k, odd, g] for g in range(at)], axis=1)
        for q in range(n_trial // 2):
            lines = jnp.concatenate(
                [mid_ref[odd, g, :, q * n_occ : (q + 1) * n_occ] for g in range(at)], axis=1
            )
            acc_ref[2 * q + odd] += dot_nt(lines, weights)


def place(target_ref, pieces_ref, first, mask, rows):
    for d in range(pieces_ref.shape[0]):
        at = pl.multiple_of(((first ^ d) & mask) * rows, rows)
        for m in range(pieces_ref.shape[1]):
            target_ref[m, pl.ds(at, rows), :] = pieces_ref[d, m].astype(F32)


def half_kernel(cut, me_ref, half_ref, pair_ref, vv_ref, more_ref, ov_ref, *refs):
    acc_ref, rest_ref, held_ov_ref, xs_ref, mid_ref, sem = refs
    copies = [
        pltpu.make_async_copy(
            more_ref.at[pl.ds(vv_ref.shape[0], rest_ref.shape[0])], rest_ref, sem.at[0]
        ),
        pltpu.make_async_copy(ov_ref, held_ov_ref, sem.at[1]),
    ]
    for copy in copies:
        copy.start()
    if cut:
        place(xs_ref, half_ref, me_ref[0], half_ref.shape[0] - 1, half_ref.shape[2])
    else:
        xs_ref[...] = half_ref[...].astype(F32)
    acc_ref[...] = jnp.zeros_like(acc_ref)
    contract_half(
        xs_ref[...].astype(BF16),
        pair_ref,
        0,
        (vv_ref, rest_ref),
        acc_ref,
        mid_ref,
        copies[0].wait,
    )
    copies[1].wait()


def build_kernel(low, cut, me_ref, occ_ref, vir_ref, own_ref, held_ref, *refs):
    parts = 1 << low
    pieces, (ov_ref, pair_ref, *vv_refs), outs = refs[:2], refs[2:6], refs[6:-3]
    xs_ref, mid_ref, acc_ref = refs[-3:]
    n_trial, rows, n_virt = own_ref.shape
    n_occ = ov_ref.shape[2]
    size, half = n_occ // rows, n_occ // 2
    high_count = size >> low
    me, other = me_ref[0], 1 - me_ref[1]
    mine = me & (parts - 1)
    if cut:
        place(xs_ref, pieces[0], me, size - 1, rows)
        place(xs_ref, pieces[1], me ^ (size // 2), size - 1, rows)
    else:
        for k, piece in enumerate(pieces):
            at = pl.multiple_of((me_ref[1] ^ k) * half, half)
            for m in range(n_trial):
                xs_ref[m, pl.ds(at, half), :] = piece[m].astype(F32)
    x = xs_ref[...].astype(BF16)
    acc_ref[...] = held_ref[...]
    coulomb_into(acc_ref, x, ov_ref)
    rest = pl.ds(pl.multiple_of(other * half, half), half)
    x_rest = jnp.stack([xs_ref[m, rest, :] for m in range(n_trial)], 0).astype(BF16)
    contract_half(x_rest, pair_ref, 1, vv_refs, acc_ref, mid_ref)
    unit = (
        lax.broadcasted_iota(jnp.int32, (n_occ, 2 * n_occ), 0)
        == lax.broadcasted_iota(jnp.int32, (n_occ, 2 * n_occ), 1) % n_occ
    ).astype(BF16)
    lines = []
    for m in range(n_trial):
        turned = acc_ref[m]
        high = turned.astype(BF16)
        rest = (turned - high.astype(F32)).astype(BF16)
        value = -dot_nt(unit, jnp.concatenate([high, rest], axis=1))
        seen = xs_ref[m]
        lines.append(jnp.sum(jnp.sum(seen * value, axis=0, keepdims=True), axis=1, keepdims=True))
        xs_ref[m] = value
    own = own_ref[...]
    square = own * own
    diag = diagonal(occ_ref, vir_ref, me * rows, rows)
    for m in range(n_trial):
        lines[m] += jnp.sum(
            jnp.sum(square[m] * diag, axis=0, keepdims=True), axis=1, keepdims=True
        )
    for m in range(n_trial):
        lines.append(
            jnp.sum(jnp.sum(square[m], axis=0, keepdims=True), axis=1, keepdims=True)
        )
    scalars = jnp.concatenate(
        [jnp.broadcast_to(line, (1, n_virt)) for line in lines], axis=0
    )
    single = jnp.where(
        lax.broadcasted_iota(jnp.int32, scalars.shape, 1) == 0, scalars, 0.0
    )
    coded = three_parts(scalars)
    if not cut:
        for ref, value in zip(outs, (xs_ref[...], single, coded)):
            ref[...] = value
        return
    body = high_count * n_trial * rows
    outs[0][body:, :] = single
    for k in range(parts):
        blocks = []
        for z in range(high_count):
            at = pl.multiple_of(((z << low) | (mine ^ k)) * rows, rows)
            blocks += [xs_ref[m, pl.ds(at, rows), :] for m in range(n_trial)]
        whole = jnp.concatenate(blocks, axis=0)
        if k == 0:
            outs[0][:body, :] = whole
        else:
            outs[k][:body, :] = whole.astype(BF16)
            outs[k][body:, :] = coded


def pack_kernel(*refs):
    at = 0
    for ref in refs[:-1]:
        count = ref.shape[0]
        refs[-1][at : at + count] = ref[...].astype(BF16)
        at += count


def pack(arrays):
    count = sum(a.shape[0] for a in arrays)
    return pl.pallas_call(
        pack_kernel,
        out_shape=jax.ShapeDtypeStruct((count,) + arrays[0].shape[1:], BF16),
        in_specs=[VMEM] * len(arrays),
        out_specs=VMEM,
        compiler_params=SMALL,
    )(*arrays)


def in_vmem(*arrays):
    return [pltpu.with_memory_space_constraint(a, pltpu.VMEM) for a in arrays]


def in_order(half, me):
    count, n_trial, rows, n_virt = half.shape
    order = (me & (count - 1)) ^ jnp.arange(count)
    return half[order].transpose(1, 0, 2, 3).reshape(n_trial, count * rows, n_virt)


def in_hbm(*arrays):
    return [pltpu.with_memory_space_constraint(a, pltpu.HBM) for a in arrays]


def first_half(me_pair, half, pairs, exch_vv, more_vv, coul_t):
    cut = half.ndim == 4
    n_aux, n_virt, n_occ = coul_t.shape
    n_trial = half.shape[1] if cut else half.shape[0]
    flops = n_aux * n_trial * n_occ * n_virt * (n_virt + n_occ)
    return pl.pallas_call(
        functools.partial(half_kernel, cut),
        out_shape=[
            pltpu.VMEM((n_trial, n_virt, n_occ), F32),
            pltpu.VMEM((n_aux - exch_vv.shape[0], n_virt, n_virt), BF16),
            pltpu.VMEM(coul_t.shape, BF16),
        ],
        in_specs=[SMEM] + [VMEM] * 3 + [HBM] * 2,
        out_specs=[VMEM] * 3,
        scratch_shapes=[
            pltpu.VMEM((n_trial, n_occ // 2, n_virt), F32),
            pltpu.VMEM((2, n_aux // 2, n_virt, n_trial * n_occ // 2), BF16),
            pltpu.SemaphoreType.DMA((2,)),
        ],
        compiler_params=pltpu.CompilerParams(vmem_limit_bytes=32 << 20),
        cost_estimate=pl.CostEstimate(
            flops=flops, bytes_accessed=2 * (exch_vv.size + coul_t.size), transcendentals=0
        ),
    )(me_pair, half, *in_vmem(pairs, exch_vv), *in_hbm(more_vv, coul_t))


def build(me_pair, occ, vir, own, held, pieces, coul_t, pairs, exch_vv, low):
    parts = 1 << low
    n_trial, rows, n_virt = own.shape
    n_aux, _, n_occ = coul_t.shape
    high_count = n_occ // rows >> low
    cut = pieces[0].ndim == 4
    height, extra = high_count * n_trial * rows, 2 * n_trial
    if cut:
        shapes = [jax.ShapeDtypeStruct((height + extra, n_virt), F32)]
        shapes += [jax.ShapeDtypeStruct((height + extra, n_virt), BF16)] * (parts - 1)
    else:
        shapes = [
            jax.ShapeDtypeStruct((n_trial, n_occ, n_virt), F32),
            jax.ShapeDtypeStruct((extra, n_virt), F32),
            jax.ShapeDtypeStruct((extra, n_virt), BF16),
        ]
    flops = n_aux * n_trial * n_occ * n_virt * (n_virt + n_occ)
    moved = 2 * (coul_t.size + pairs.size + 2 * exch_vv[0].size)
    results = pl.pallas_call(
        functools.partial(build_kernel, low, cut),
        out_shape=shapes,
        in_specs=[SMEM] + [VMEM] * 10,
        out_specs=[VMEM] * len(shapes),
        scratch_shapes=[
            pltpu.VMEM((n_trial, n_occ, n_virt), F32),
            pltpu.VMEM((2, n_aux // 2, n_virt, n_trial * n_occ // 2), BF16),
            pltpu.VMEM((n_trial, n_virt, n_occ), F32),
        ],
        compiler_params=pltpu.CompilerParams(vmem_limit_bytes=32 << 20),
        cost_estimate=pl.CostEstimate(flops=flops, bytes_accessed=moved, transcendentals=0),
    )(me_pair, occ, vir, own, *in_vmem(held), *pieces, *in_vmem(coul_t, pairs, *exch_vv))
    if cut:
        return results
    value, single, coded = results
    value = value.reshape(n_trial, high_count, parts, rows, n_virt).transpose(2, 1, 0, 3, 4)
    mine = me_pair[0] & (parts - 1)
    blocks = [
        lax.dynamic_index_in_dim(value, mine ^ k, 0, keepdims=False).reshape(height, n_virt)
        for k in range(parts)
    ]
    return [jnp.concatenate([blocks[0], single], axis=0)] + [
        jnp.concatenate([block.astype(BF16), coded], axis=0) for block in blocks[1:]
    ]


def summed(own_ref, arrived):
    total = own_ref[...]
    for ref in arrived:
        total += ref[...].astype(F32)
    return total


def combine_kernel(extra, own_ref, *refs):
    arrived, (total_ref, send_ref) = refs[:-2], refs[-2:]
    total = summed(own_ref, arrived)
    body = total.shape[0] - extra
    scalars = jnp.sum(total[body:], axis=1, keepdims=True)
    scalars = jnp.broadcast_to(scalars, (extra, total.shape[1]))
    lane = lax.broadcasted_iota(jnp.int32, scalars.shape, 1)
    total_ref[:body, :] = total[:body]
    total_ref[body:, :] = jnp.where(lane == 0, scalars, 0.0)
    send_ref[:body, :] = total[:body].astype(BF16)
    send_ref[body:, :] = three_parts(scalars)


def combine(own, arrived, extra):
    return pl.pallas_call(
        functools.partial(combine_kernel, extra),
        out_shape=[
            jax.ShapeDtypeStruct(own.shape, F32),
            jax.ShapeDtypeStruct(own.shape, BF16),
        ],
        in_specs=[VMEM] * (1 + len(arrived)),
        out_specs=[VMEM] * 2,
        compiler_params=SMALL,
    )(own, *arrived)


def residual_kernel(low, me_ref, occ_ref, vir_ref, near_ref, near_half, far_half, own_ref, *refs):
    arrived, (sigma_ref, precond_ref, square_ref, held_ref) = refs[:-4], refs[-4:]
    n_trial, rows, n_virt = near_ref.shape
    count = near_half.shape[0]
    high_count = 2 * count >> low
    body = high_count * n_trial * rows
    mine, top = me_ref[0] & ((1 << low) - 1), me_ref[0] >> low
    total = summed(own_ref, arrived)
    held_ref[...] = total[:body].reshape(held_ref.shape)
    scalars = jnp.sum(total[body:], axis=1, keepdims=True)
    omega = scalars[:n_trial] / (scalars[n_trial:] + 1e-06)
    squares = [jnp.zeros((rows, n_virt), F32) for _ in range(n_trial)]
    for r in range(high_count):
        diag = diagonal(occ_ref, vir_ref, (((top ^ r) << low) | mine) * rows, rows)
        block = held_ref[top ^ r]
        for m in range(n_trial):
            away = r << low
            if r == 0:
                t = near_ref[m]
            else:
                t = (near_half if away < count else far_half)[away % count, m].astype(F32)
            level = omega[m : m + 1]
            sigma = diag * t + block[m * rows : (m + 1) * rows]
            precond = (sigma - level * t) / jnp.maximum(jnp.abs(diag - level), 1.0)
            squares[m] += precond * precond
            if r == 0:
                sigma_ref[m] = sigma
                precond_ref[m] = precond
    sums = [
        jnp.sum(jnp.sum(s, axis=0, keepdims=True), axis=1, keepdims=True) for s in squares
    ]
    square_ref[...] = jnp.concatenate(
        [jnp.broadcast_to(s, (1, square_ref.shape[1])) for s in sums], axis=0
    )


def residual(me_pair, occ, vir, low, near, halves, own, arrived):
    n_trial, rows, n_virt = near.shape
    high_count = 2 * halves[0].shape[0] >> low
    return pl.pallas_call(
        functools.partial(residual_kernel, low),
        out_shape=[pltpu.VMEM(near.shape, F32)] * 2 + [pltpu.VMEM((n_trial, 128), F32)],
        in_specs=[SMEM] + [VMEM] * (6 + len(arrived)),
        out_specs=[VMEM] * 3,
        scratch_shapes=[pltpu.VMEM((high_count, n_trial * rows, n_virt), F32)],
        compiler_params=SMALL,
    )(me_pair, occ, vir, near, *halves, own, *arrived)


def finish_kernel(count, precond_ref, *refs):
    update_ref = refs[-1]
    square = refs[0][...]
    for ref in refs[1:-1]:
        square += ref[...]
    scale = lax.rsqrt(square[:, :1] / count + 1e-06)
    for m in range(precond_ref.shape[0]):
        update_ref[m] = precond_ref[m] * scale[m : m + 1]


def finish(count, precond, squares):
    return pl.pallas_call(
        functools.partial(finish_kernel, count),
        out_shape=jax.ShapeDtypeStruct(precond.shape, F32),
        in_specs=[VMEM] * (1 + len(squares)),
        out_specs=VMEM,
        compiler_params=SMALL,
    )(precond, *squares)


def fetch_kernel(count, after_ref, *refs):
    del after_ref
    sources, targets, sem = refs[:count], refs[count : 2 * count], refs[-1]
    copies = [
        pltpu.make_async_copy(source, target, sem.at[k])
        for k, (source, target) in enumerate(zip(sources, targets))
    ]
    for copy in copies:
        copy.start()
    for copy in copies:
        copy.wait()


def fetch(after, *arrays):
    return pl.pallas_call(
        functools.partial(fetch_kernel, len(arrays)),
        out_shape=[pltpu.VMEM(a.shape, a.dtype) for a in arrays],
        in_specs=[ANY] + [HBM] * len(arrays),
        out_specs=[VMEM] * len(arrays),
        scratch_shapes=[pltpu.SemaphoreType.DMA((len(arrays),))],
        compiler_params=SMALL,
        cost_estimate=pl.CostEstimate(
            flops=0, bytes_accessed=sum(4 * a.size for a in arrays), transcendentals=0
        ),
    )(after, *in_hbm(*arrays))


def prepare_kernel(me_ref, after_ref, oo_ref, vv_ref, pair_ref, held_ref, held_oo_ref, sem):
    del after_ref
    first = pltpu.make_async_copy(oo_ref, held_oo_ref, sem.at[0])
    second = pltpu.make_async_copy(
        vv_ref.at[pl.ds(0, held_ref.shape[0])], held_ref, sem.at[1]
    )
    first.start()
    second.start()
    first.wait()
    pair_weights(me_ref[1], held_oo_ref, pair_ref)
    second.wait()


def prepare(me_pair, after, exch_oo, exch_vv):
    n_aux, n_occ, _ = exch_oo.shape
    return pl.pallas_call(
        prepare_kernel,
        out_shape=[
            pltpu.VMEM((2, 2, n_aux // 2, n_occ, n_occ), BF16),
            pltpu.VMEM((n_aux // 4 * 2,) + exch_vv.shape[1:], BF16),
        ],
        in_specs=[SMEM, ANY, HBM, HBM],
        out_specs=[VMEM] * 2,
        scratch_shapes=[
            pltpu.VMEM(exch_oo.shape, BF16),
            pltpu.SemaphoreType.DMA((2,)),
        ],
        compiler_params=SMALL,
        cost_estimate=pl.CostEstimate(
            flops=0, bytes_accessed=4 * (exch_oo.size + exch_vv.size), transcendentals=0
        ),
    )(me_pair, after, *in_hbm(exch_oo, exch_vv))


def on_device(size, trial_vecs, occ_energy, vir_energy, coul_ov, exch_oo, exch_vv):
    n_trial, rows, n_virt = trial_vecs.shape
    n_occ = exch_oo.shape[1]
    low, highs = bit_groups(size)
    me = lax.axis_index("aux").astype(jnp.int32)
    top = size.bit_length() - 2
    me_pair = jnp.stack([me, me >> top])
    coul_t = jnp.transpose(coul_ov, (0, 2, 1))
    near, occ, vir = fetch(me_pair, trial_vecs, occ_energy[None], vir_energy[None])
    held = pack([near[None]] + [a[None] for a in exchange(trial_vecs, size, 0, 1)])
    pairs, vv = prepare(me_pair, held, exch_oo, exch_vv)
    for at in range(1, top, 2):
        held = pack([held] + exchange(held, size, at, min(2, top - at)))
    far, = exchange(held, size, top, 1)
    halves = [held, far]
    pieces = halves if rows % 8 == 0 else [in_order(half, me) for half in halves]
    half_sum, more_vv, coul_t = first_half(
        me_pair, pieces[0], pairs, vv, exch_vv, coul_t
    )
    own, *sends = build(
        me_pair, occ, vir, near, half_sum, pieces, coul_t, pairs, (vv, more_vv), low
    )
    arrived = [swap(send, size, k + 1) for k, send in enumerate(sends)]
    for at, width in highs:
        own, send = combine(own, arrived, 2 * n_trial)
        arrived = exchange(send, size, at, width)
    sigma_vecs, precond, square = residual(me_pair, occ, vir, low, near, halves, own, arrived)
    squares = [square] + exchange(square, size, 0, low)
    return sigma_vecs, finish(n_occ * n_virt, precond, squares)


def solution(mesh):
    in_specs = (
        P("geom", "aux", None),
        P("geom"),
        P("geom"),
        P(("geom", "aux"), None, None),
        P(("geom", "aux"), None, None),
        P(("geom", "aux"), None, None),
    )
    out_specs = (P("geom", "aux", None), P("geom", "aux", None))
    return jax.shard_map(
        functools.partial(on_device, mesh.shape["aux"]),
        mesh=mesh,
        in_specs=in_specs,
        out_specs=out_specs,
        check_vma=False,
    )
```

```python
import functools

import jax
import jax.numpy as jnp
from jax import lax
from jax.experimental import pallas as pl
from jax.experimental.pallas import tpu as pltpu
from jax.sharding import PartitionSpec as P


F32 = jnp.float32
BF16 = jnp.bfloat16
LOW_BITS = 2
TILE = 16
VMEM = pl.BlockSpec(memory_space=pltpu.VMEM)
SMEM = pl.BlockSpec(memory_space=pltpu.SMEM)
HBM = pl.BlockSpec(memory_space=pltpu.HBM)
ANY = pl.BlockSpec(memory_space=pl.ANY)
SMALL = pltpu.CompilerParams(vmem_limit_bytes=4 << 20)


def bit_groups(size):
    bits = size.bit_length() - 1
    assert size == 1 << bits
    low = min(LOW_BITS, bits)
    return low, [(at, min(LOW_BITS, bits - at)) for at in range(low, bits, LOW_BITS)]


def swap(value, size, offset):
    return lax.ppermute(value, "aux", [(i, i ^ offset) for i in range(size)])


def exchange(value, size, at, width):
    return [swap(value, size, k << at) for k in range(1, 1 << width)]


def dot(a, b):
    return jnp.dot(a, b, preferred_element_type=F32)


def dot_nt(a, b):
    return lax.dot_general(a, b, (((1,), (1,)), ((), ())), preferred_element_type=F32)


def diagonal(occ_ref, vir_ref, first, rows):
    shape = (rows, occ_ref.shape[1])
    wanted = lax.broadcasted_iota(jnp.int32, shape, 0) + first
    picked = jnp.where(lax.broadcasted_iota(jnp.int32, shape, 1) == wanted, occ_ref[...], 0.0)
    return vir_ref[...] - jnp.sum(picked, axis=1, keepdims=True)


def three_parts(value):
    high = value.astype(BF16).astype(F32)
    middle = (value - high).astype(BF16).astype(F32)
    rest = value - high - middle
    lane = lax.broadcasted_iota(jnp.int32, value.shape, 1)
    return jnp.where(
        lane == 0, high, jnp.where(lane == 1, middle, jnp.where(lane == 2, rest, 0.0))
    ).astype(BF16)


def coulomb_into(acc_ref, x, ov_ref):
    n_aux, n_virt, n_occ = ov_ref.shape
    n_trial = x.shape[0]
    tiles = n_virt // TILE
    unit = (
        lax.broadcasted_iota(jnp.int32, (n_virt, n_virt), 0)
        == lax.broadcasted_iota(jnp.int32, (n_virt, n_virt), 1)
    ).astype(BF16)
    x_t = jnp.stack([dot_nt(unit, x[m]).astype(BF16) for m in range(n_trial)], 0)
    rows, cols = n_trial * TILE, n_aux * TILE

    def x_tile(t):
        return x_t[:, t * TILE : (t + 1) * TILE, :].reshape(rows, n_occ)

    def ov_tile(t):
        return ov_ref[:, t * TILE : (t + 1) * TILE, :].reshape(cols, n_occ)

    total = jnp.zeros((rows, cols), F32)
    for t in range(0, tiles, 2):
        span = range(t, min(t + 2, tiles))
        total += dot_nt(
            jnp.concatenate([x_tile(u) for u in span], axis=1),
            jnp.concatenate([ov_tile(u) for u in span], axis=1),
        )
    same = (
        lax.broadcasted_iota(jnp.int32, (rows, cols), 0) % TILE
        == lax.broadcasted_iota(jnp.int32, (rows, cols), 1) % TILE
    )
    coef = jnp.sum(jnp.where(same, total, 0.0).reshape(n_trial, TILE, cols), axis=1)
    lane = lax.broadcasted_iota(jnp.int32, coef.shape, 1)
    step = 1
    while step < TILE:
        coef += jnp.where(
            (lane & step) != 0, pltpu.roll(coef, step, 1), pltpu.roll(coef, cols - step, 1)
        )
        step *= 2
    twice = 2.0 * coef.astype(BF16).astype(F32)
    spread = jnp.broadcast_to(twice[:, None, :], (n_trial, TILE, cols)).reshape(rows, cols)
    weights = jnp.where(same, spread, 0.0).astype(BF16)
    for t in range(0, tiles, 2):
        span = range(t, min(t + 2, tiles))
        sums = dot(weights, jnp.concatenate([ov_tile(u) for u in span], axis=1))
        for k, u in enumerate(span):
            acc_ref[:, u * TILE : (u + 1) * TILE, :] -= sums[
                :, k * n_occ : (k + 1) * n_occ
            ].reshape(n_trial, TILE, n_occ)


def pair_weights(oo_ref, pair_ref):
    n_aux, n_occ, _ = oo_ref.shape
    half = n_occ // 2
    left = lax.broadcasted_iota(jnp.int32, (n_occ, n_occ), 1) < half
    for g in range(n_aux // 2):
        straight = [oo_ref[2 * g + odd].astype(F32) for odd in range(2)]
        moved = [pltpu.roll(value, half, 1) for value in straight]
        for odd in range(2):
            pair_ref[0, odd, g] = jnp.where(left, straight[odd], moved[1 - odd]).astype(BF16)
            pair_ref[1, odd, g] = jnp.where(left, moved[odd], straight[1 - odd]).astype(BF16)


def contract_half(x, pair_ref, k, vv_refs, acc_ref, mid_ref, ready=None):
    n_trial, half, n_virt = x.shape
    n_occ = 2 * half
    width = n_trial * half
    orders = [
        jnp.concatenate([x[m ^ odd] for m in range(n_trial)], axis=0) for odd in range(2)
    ]
    at = 0
    for step, vv_ref in enumerate(vv_refs):
        if ready is not None and step == 1:
            ready()
        pairs = vv_ref.shape[0] // 2
        even, odd = (
            dot_nt(
                jnp.concatenate([vv_ref[2 * g + odd] for g in range(pairs)], axis=0),
                orders[odd],
            )
            for odd in range(2)
        )
        left = lax.broadcasted_iota(jnp.int32, even.shape, 1) % n_occ < half
        shape = (pairs, n_virt, width)
        mid_ref[0, at : at + pairs] = jnp.where(left, even, odd).astype(BF16).reshape(shape)
        mid_ref[1, at : at + pairs] = jnp.where(left, odd, even).astype(BF16).reshape(shape)
        at += pairs
    for odd in range(2):
        weights = jnp.concatenate([pair_ref[k, odd, g] for g in range(at)], axis=1)
        for q in range(n_trial // 2):
            lines = jnp.concatenate(
                [mid_ref[odd, g, :, q * n_occ : (q + 1) * n_occ] for g in range(at)], axis=1
            )
            acc_ref[2 * q + odd] += dot_nt(lines, weights)


def place(target_ref, pieces_ref, first, mask, rows):
    for d in range(pieces_ref.shape[0]):
        at = pl.multiple_of(((first ^ d) & mask) * rows, rows)
        for m in range(pieces_ref.shape[1]):
            target_ref[m, pl.ds(at, rows), :] = pieces_ref[d, m].astype(F32)


def half_kernel(cut, me_ref, half_ref, pair_ref, vv_ref, more_ref, ov_ref, *refs):
    acc_ref, rest_ref, held_ov_ref, xs_ref, mid_ref, sem = refs
    copies = [
        pltpu.make_async_copy(
            more_ref.at[pl.ds(vv_ref.shape[0], rest_ref.shape[0])], rest_ref, sem.at[0]
        ),
        pltpu.make_async_copy(ov_ref, held_ov_ref, sem.at[1]),
    ]
    for copy in copies:
        copy.start()
    if cut:
        place(xs_ref, half_ref, me_ref[0], half_ref.shape[0] - 1, half_ref.shape[2])
    else:
        xs_ref[...] = half_ref[...].astype(F32)
    acc_ref[...] = jnp.zeros_like(acc_ref)
    contract_half(
        xs_ref[...].astype(BF16),
        pair_ref,
        me_ref[1],
        (vv_ref, rest_ref),
        acc_ref,
        mid_ref,
        copies[0].wait,
    )
    copies[1].wait()


def build_kernel(low, cut, me_ref, occ_ref, vir_ref, own_ref, held_ref, *refs):
    parts = 1 << low
    pieces, (ov_ref, pair_ref, *vv_refs), outs = refs[:2], refs[2:6], refs[6:-3]
    xs_ref, mid_ref, acc_ref = refs[-3:]
    n_trial, rows, n_virt = own_ref.shape
    n_occ = ov_ref.shape[2]
    size, half = n_occ // rows, n_occ // 2
    high_count = size >> low
    me, other = me_ref[0], 1 - me_ref[1]
    mine = me & (parts - 1)
    if cut:
        place(xs_ref, pieces[0], me, size - 1, rows)
        place(xs_ref, pieces[1], me ^ (size // 2), size - 1, rows)
    else:
        for k, piece in enumerate(pieces):
            at = pl.multiple_of((me_ref[1] ^ k) * half, half)
            for m in range(n_trial):
                xs_ref[m, pl.ds(at, half), :] = piece[m].astype(F32)
    x = xs_ref[...].astype(BF16)
    acc_ref[...] = held_ref[...]
    coulomb_into(acc_ref, x, ov_ref)
    rest = pl.ds(pl.multiple_of(other * half, half), half)
    x_rest = jnp.stack([xs_ref[m, rest, :] for m in range(n_trial)], 0).astype(BF16)
    contract_half(x_rest, pair_ref, other, vv_refs, acc_ref, mid_ref)
    unit = (
        lax.broadcasted_iota(jnp.int32, (n_occ, 2 * n_occ), 0)
        == lax.broadcasted_iota(jnp.int32, (n_occ, 2 * n_occ), 1) % n_occ
    ).astype(BF16)
    lines = []
    for m in range(n_trial):
        turned = acc_ref[m]
        high = turned.astype(BF16)
        rest = (turned - high.astype(F32)).astype(BF16)
        value = -dot_nt(unit, jnp.concatenate([high, rest], axis=1))
        seen = xs_ref[m]
        lines.append(jnp.sum(jnp.sum(seen * value, axis=0, keepdims=True), axis=1, keepdims=True))
        xs_ref[m] = value
    own = own_ref[...]
    square = own * own
    diag = diagonal(occ_ref, vir_ref, me * rows, rows)
    for m in range(n_trial):
        lines[m] += jnp.sum(
            jnp.sum(square[m] * diag, axis=0, keepdims=True), axis=1, keepdims=True
        )
    for m in range(n_trial):
        lines.append(
            jnp.sum(jnp.sum(square[m], axis=0, keepdims=True), axis=1, keepdims=True)
        )
    scalars = jnp.concatenate(
        [jnp.broadcast_to(line, (1, n_virt)) for line in lines], axis=0
    )
    single = jnp.where(
        lax.broadcasted_iota(jnp.int32, scalars.shape, 1) == 0, scalars, 0.0
    )
    coded = three_parts(scalars)
    if not cut:
        for ref, value in zip(outs, (xs_ref[...], single, coded)):
            ref[...] = value
        return
    body = high_count * n_trial * rows
    outs[0][body:, :] = single
    for k in range(parts):
        blocks = []
        for z in range(high_count):
            at = pl.multiple_of(((z << low) | (mine ^ k)) * rows, rows)
            blocks += [xs_ref[m, pl.ds(at, rows), :] for m in range(n_trial)]
        whole = jnp.concatenate(blocks, axis=0)
        if k == 0:
            outs[0][:body, :] = whole
        else:
            outs[k][:body, :] = whole.astype(BF16)
            outs[k][body:, :] = coded


def pack_kernel(*refs):
    at = 0
    for ref in refs[:-1]:
        count = ref.shape[0]
        refs[-1][at : at + count] = ref[...].astype(BF16)
        at += count


def pack(arrays):
    count = sum(a.shape[0] for a in arrays)
    return pl.pallas_call(
        pack_kernel,
        out_shape=jax.ShapeDtypeStruct((count,) + arrays[0].shape[1:], BF16),
        in_specs=[VMEM] * len(arrays),
        out_specs=VMEM,
        compiler_params=SMALL,
    )(*arrays)


def in_vmem(*arrays):
    return [pltpu.with_memory_space_constraint(a, pltpu.VMEM) for a in arrays]


def in_order(half, me):
    count, n_trial, rows, n_virt = half.shape
    order = (me & (count - 1)) ^ jnp.arange(count)
    return half[order].transpose(1, 0, 2, 3).reshape(n_trial, count * rows, n_virt)


def in_hbm(*arrays):
    return [pltpu.with_memory_space_constraint(a, pltpu.HBM) for a in arrays]


def first_half(me_pair, half, pairs, exch_vv, more_vv, coul_t):
    cut = half.ndim == 4
    n_aux, n_virt, n_occ = coul_t.shape
    n_trial = half.shape[1] if cut else half.shape[0]
    flops = n_aux * n_trial * n_occ * n_virt * (n_virt + n_occ)
    return pl.pallas_call(
        functools.partial(half_kernel, cut),
        out_shape=[
            pltpu.VMEM((n_trial, n_virt, n_occ), F32),
            pltpu.VMEM((n_aux - exch_vv.shape[0], n_virt, n_virt), BF16),
            pltpu.VMEM(coul_t.shape, BF16),
        ],
        in_specs=[SMEM] + [VMEM] * 3 + [HBM] * 2,
        out_specs=[VMEM] * 3,
        scratch_shapes=[
            pltpu.VMEM((n_trial, n_occ // 2, n_virt), F32),
            pltpu.VMEM((2, n_aux // 2, n_virt, n_trial * n_occ // 2), BF16),
            pltpu.SemaphoreType.DMA((2,)),
        ],
        compiler_params=pltpu.CompilerParams(vmem_limit_bytes=32 << 20),
        cost_estimate=pl.CostEstimate(
            flops=flops, bytes_accessed=2 * (exch_vv.size + coul_t.size), transcendentals=0
        ),
    )(me_pair, half, *in_vmem(pairs, exch_vv), *in_hbm(more_vv, coul_t))


def build(me_pair, occ, vir, own, held, pieces, coul_t, pairs, exch_vv, low):
    parts = 1 << low
    n_trial, rows, n_virt = own.shape
    n_aux, _, n_occ = coul_t.shape
    high_count = n_occ // rows >> low
    cut = pieces[0].ndim == 4
    height, extra = high_count * n_trial * rows, 2 * n_trial
    if cut:
        shapes = [jax.ShapeDtypeStruct((height + extra, n_virt), F32)]
        shapes += [jax.ShapeDtypeStruct((height + extra, n_virt), BF16)] * (parts - 1)
    else:
        shapes = [
            jax.ShapeDtypeStruct((n_trial, n_occ, n_virt), F32),
            jax.ShapeDtypeStruct((extra, n_virt), F32),
            jax.ShapeDtypeStruct((extra, n_virt), BF16),
        ]
    flops = n_aux * n_trial * n_occ * n_virt * (n_virt + n_occ)
    moved = 2 * (coul_t.size + pairs.size + 2 * exch_vv[0].size)
    results = pl.pallas_call(
        functools.partial(build_kernel, low, cut),
        out_shape=shapes,
        in_specs=[SMEM] + [VMEM] * 10,
        out_specs=[VMEM] * len(shapes),
        scratch_shapes=[
            pltpu.VMEM((n_trial, n_occ, n_virt), F32),
            pltpu.VMEM((2, n_aux // 2, n_virt, n_trial * n_occ // 2), BF16),
            pltpu.VMEM((n_trial, n_virt, n_occ), F32),
        ],
        compiler_params=pltpu.CompilerParams(vmem_limit_bytes=32 << 20),
        cost_estimate=pl.CostEstimate(flops=flops, bytes_accessed=moved, transcendentals=0),
    )(me_pair, occ, vir, own, *in_vmem(held), *pieces, *in_vmem(coul_t, pairs, *exch_vv))
    if cut:
        return results
    value, single, coded = results
    value = value.reshape(n_trial, high_count, parts, rows, n_virt).transpose(2, 1, 0, 3, 4)
    mine = me_pair[0] & (parts - 1)
    blocks = [
        lax.dynamic_index_in_dim(value, mine ^ k, 0, keepdims=False).reshape(height, n_virt)
        for k in range(parts)
    ]
    return [jnp.concatenate([blocks[0], single], axis=0)] + [
        jnp.concatenate([block.astype(BF16), coded], axis=0) for block in blocks[1:]
    ]


def summed(own_ref, arrived):
    total = own_ref[...]
    for ref in arrived:
        total += ref[...].astype(F32)
    return total


def combine_kernel(extra, own_ref, *refs):
    arrived, (total_ref, send_ref) = refs[:-2], refs[-2:]
    total = summed(own_ref, arrived)
    body = total.shape[0] - extra
    scalars = jnp.sum(total[body:], axis=1, keepdims=True)
    scalars = jnp.broadcast_to(scalars, (extra, total.shape[1]))
    lane = lax.broadcasted_iota(jnp.int32, scalars.shape, 1)
    total_ref[:body, :] = total[:body]
    total_ref[body:, :] = jnp.where(lane == 0, scalars, 0.0)
    send_ref[:body, :] = total[:body].astype(BF16)
    send_ref[body:, :] = three_parts(scalars)


def combine(own, arrived, extra):
    return pl.pallas_call(
        functools.partial(combine_kernel, extra),
        out_shape=[
            jax.ShapeDtypeStruct(own.shape, F32),
            jax.ShapeDtypeStruct(own.shape, BF16),
        ],
        in_specs=[VMEM] * (1 + len(arrived)),
        out_specs=[VMEM] * 2,
        compiler_params=SMALL,
    )(own, *arrived)


def residual_kernel(low, me_ref, occ_ref, vir_ref, near_ref, near_half, far_half, own_ref, *refs):
    arrived, (sigma_ref, precond_ref, square_ref, held_ref) = refs[:-4], refs[-4:]
    n_trial, rows, n_virt = near_ref.shape
    count = near_half.shape[0]
    high_count = 2 * count >> low
    body = high_count * n_trial * rows
    mine, top = me_ref[0] & ((1 << low) - 1), me_ref[0] >> low
    total = summed(own_ref, arrived)
    held_ref[...] = total[:body].reshape(held_ref.shape)
    scalars = jnp.sum(total[body:], axis=1, keepdims=True)
    omega = scalars[:n_trial] / (scalars[n_trial:] + 1e-06)
    squares = [jnp.zeros((rows, n_virt), F32) for _ in range(n_trial)]
    for r in range(high_count):
        diag = diagonal(occ_ref, vir_ref, (((top ^ r) << low) | mine) * rows, rows)
        block = held_ref[top ^ r]
        for m in range(n_trial):
            away = r << low
            if r == 0:
                t = near_ref[m]
            else:
                t = (near_half if away < count else far_half)[away % count, m].astype(F32)
            level = omega[m : m + 1]
            sigma = diag * t + block[m * rows : (m + 1) * rows]
            precond = (sigma - level * t) / jnp.maximum(jnp.abs(diag - level), 1.0)
            squares[m] += precond * precond
            if r == 0:
                sigma_ref[m] = sigma
                precond_ref[m] = precond
    sums = [
        jnp.sum(jnp.sum(s, axis=0, keepdims=True), axis=1, keepdims=True) for s in squares
    ]
    square_ref[...] = jnp.concatenate(
        [jnp.broadcast_to(s, (1, square_ref.shape[1])) for s in sums], axis=0
    )


def residual(me_pair, occ, vir, low, near, halves, own, arrived):
    n_trial, rows, n_virt = near.shape
    high_count = 2 * halves[0].shape[0] >> low
    return pl.pallas_call(
        functools.partial(residual_kernel, low),
        out_shape=[pltpu.VMEM(near.shape, F32)] * 2 + [pltpu.VMEM((n_trial, 128), F32)],
        in_specs=[SMEM] + [VMEM] * (6 + len(arrived)),
        out_specs=[VMEM] * 3,
        scratch_shapes=[pltpu.VMEM((high_count, n_trial * rows, n_virt), F32)],
        compiler_params=SMALL,
    )(me_pair, occ, vir, near, *halves, own, *arrived)


def finish_kernel(count, precond_ref, *refs):
    update_ref = refs[-1]
    square = refs[0][...]
    for ref in refs[1:-1]:
        square += ref[...]
    scale = lax.rsqrt(square[:, :1] / count + 1e-06)
    for m in range(precond_ref.shape[0]):
        update_ref[m] = precond_ref[m] * scale[m : m + 1]


def finish(count, precond, squares):
    return pl.pallas_call(
        functools.partial(finish_kernel, count),
        out_shape=jax.ShapeDtypeStruct(precond.shape, F32),
        in_specs=[VMEM] * (1 + len(squares)),
        out_specs=VMEM,
        compiler_params=SMALL,
    )(precond, *squares)


def fetch_kernel(count, after_ref, *refs):
    del after_ref
    sources, targets, sem = refs[:count], refs[count : 2 * count], refs[-1]
    copies = [
        pltpu.make_async_copy(source, target, sem.at[k])
        for k, (source, target) in enumerate(zip(sources, targets))
    ]
    for copy in copies:
        copy.start()
    for copy in copies:
        copy.wait()


def fetch(after, *arrays):
    return pl.pallas_call(
        functools.partial(fetch_kernel, len(arrays)),
        out_shape=[pltpu.VMEM(a.shape, a.dtype) for a in arrays],
        in_specs=[ANY] + [HBM] * len(arrays),
        out_specs=[VMEM] * len(arrays),
        scratch_shapes=[pltpu.SemaphoreType.DMA((len(arrays),))],
        compiler_params=SMALL,
        cost_estimate=pl.CostEstimate(
            flops=0, bytes_accessed=sum(4 * a.size for a in arrays), transcendentals=0
        ),
    )(after, *in_hbm(*arrays))


def prepare_kernel(after_ref, oo_ref, vv_ref, pair_ref, held_ref, held_oo_ref, sem):
    del after_ref
    first = pltpu.make_async_copy(oo_ref, held_oo_ref, sem.at[0])
    second = pltpu.make_async_copy(
        vv_ref.at[pl.ds(0, held_ref.shape[0])], held_ref, sem.at[1]
    )
    first.start()
    second.start()
    first.wait()
    pair_weights(held_oo_ref, pair_ref)
    second.wait()


def prepare(after, exch_oo, exch_vv):
    n_aux, n_occ, _ = exch_oo.shape
    return pl.pallas_call(
        prepare_kernel,
        out_shape=[
            pltpu.VMEM((2, 2, n_aux // 2, n_occ, n_occ), BF16),
            pltpu.VMEM((n_aux // 4 * 2,) + exch_vv.shape[1:], BF16),
        ],
        in_specs=[ANY, HBM, HBM],
        out_specs=[VMEM] * 2,
        scratch_shapes=[
            pltpu.VMEM(exch_oo.shape, BF16),
            pltpu.SemaphoreType.DMA((2,)),
        ],
        compiler_params=SMALL,
        cost_estimate=pl.CostEstimate(
            flops=0, bytes_accessed=4 * (exch_oo.size + exch_vv.size), transcendentals=0
        ),
    )(after, *in_hbm(exch_oo, exch_vv))


def on_device(size, trial_vecs, occ_energy, vir_energy, coul_ov, exch_oo, exch_vv):
    n_trial, rows, n_virt = trial_vecs.shape
    n_occ = exch_oo.shape[1]
    low, highs = bit_groups(size)
    me = lax.axis_index("aux").astype(jnp.int32)
    top = size.bit_length() - 2
    me_pair = jnp.stack([me, me >> top])
    coul_t = jnp.transpose(coul_ov, (0, 2, 1))
    near, occ, vir = fetch(me_pair, trial_vecs, occ_energy[None], vir_energy[None])
    held = pack([near[None]] + [a[None] for a in exchange(trial_vecs, size, 0, 1)])
    pairs, vv = prepare(held, exch_oo, exch_vv)
    for at in range(1, top, 2):
        held = pack([held] + exchange(held, size, at, min(2, top - at)))
    far, = exchange(held, size, top, 1)
    halves = [held, far]
    pieces = halves if rows % 8 == 0 else [in_order(half, me) for half in halves]
    half_sum, more_vv, coul_t = first_half(
        me_pair, pieces[0], pairs, vv, exch_vv, coul_t
    )
    own, *sends = build(
        me_pair, occ, vir, near, half_sum, pieces, coul_t, pairs, (vv, more_vv), low
    )
    arrived = [swap(send, size, k + 1) for k, send in enumerate(sends)]
    for at, width in highs:
        own, send = combine(own, arrived, 2 * n_trial)
        arrived = exchange(send, size, at, width)
    sigma_vecs, precond, square = residual(me_pair, occ, vir, low, near, halves, own, arrived)
    squares = [square] + exchange(square, size, 0, low)
    return sigma_vecs, finish(n_occ * n_virt, precond, squares)


def solution(mesh):
    in_specs = (
        P("geom", "aux", None),
        P("geom"),
        P("geom"),
        P(("geom", "aux"), None, None),
        P(("geom", "aux"), None, None),
        P(("geom", "aux"), None, None),
    )
    out_specs = (P("geom", "aux", None), P("geom", "aux", None))
    return jax.shard_map(
        functools.partial(on_device, mesh.shape["aux"]),
        mesh=mesh,
        in_specs=in_specs,
        out_specs=out_specs,
        check_vma=False,
    )
```

```python
import functools

import jax
import jax.numpy as jnp
from jax import lax
from jax.experimental import pallas as pl
from jax.experimental.pallas import tpu as pltpu
from jax.sharding import PartitionSpec as P


F32 = jnp.float32
BF16 = jnp.bfloat16
LOW_BITS = 2
LANES = 128
EARLY = 8
TILE = 16
VMEM = pl.BlockSpec(memory_space=pltpu.VMEM)
SMEM = pl.BlockSpec(memory_space=pltpu.SMEM)
HBM = pl.BlockSpec(memory_space=pltpu.HBM)
ANY = pl.BlockSpec(memory_space=pl.ANY)
SMALL = pltpu.CompilerParams(vmem_limit_bytes=4 << 20)


def bit_groups(size):
    bits = size.bit_length() - 1
    assert size == 1 << bits
    low = min(LOW_BITS, bits)
    return low, [(at, min(LOW_BITS, bits - at)) for at in range(low, bits, LOW_BITS)]


def swap(value, size, offset):
    return lax.ppermute(value, "aux", [(i, i ^ offset) for i in range(size)])


def exchange(value, size, at, width):
    return [swap(value, size, k << at) for k in range(1, 1 << width)]


def dot(a, b):
    return jnp.dot(a, b, preferred_element_type=F32)


def dot_nt(a, b):
    return lax.dot_general(a, b, (((1,), (1,)), ((), ())), preferred_element_type=F32)


def diagonal(occ_ref, vir_ref, first, rows):
    shape = (rows, occ_ref.shape[1])
    wanted = lax.broadcasted_iota(jnp.int32, shape, 0) + first
    picked = jnp.where(lax.broadcasted_iota(jnp.int32, shape, 1) == wanted, occ_ref[...], 0.0)
    return vir_ref[...] - jnp.sum(picked, axis=1, keepdims=True)


def packs(rows, width):
    rest, free = width - LANES, 2 * LANES - width
    if not 0 < rest < LANES or rest % free or rows * free % LANES:
        return 0
    given = rows * free // LANES
    return given if given % 8 == 0 else 0


def dense(value):
    rows, width = value.shape
    given = packs(rows, width)
    if not given:
        return value
    rest, free = width - LANES, 2 * LANES - width
    high = jnp.concatenate([value[:, LANES:], jnp.zeros((rows, free), value.dtype)], axis=1)
    kept, last = high[: rows - given], high[rows - given :]
    moved = [
        pltpu.roll(last, (rest - g * free) % LANES, 1) for g in range(rest // free)
    ]
    lane = lax.broadcasted_iota(jnp.int32, kept.shape, 1)
    kept = jnp.where(lane < rest, kept, jnp.concatenate(moved, axis=0))
    return jnp.concatenate([value[:, :LANES], kept], axis=0)


def spread(value, rows, width):
    given = packs(rows, width)
    if not given:
        return value
    rest, free = width - LANES, 2 * LANES - width
    kept = value[rows:]
    last = jnp.zeros((given, LANES), value.dtype)
    lane = lax.broadcasted_iota(jnp.int32, last.shape, 1)
    for g in range(rest // free):
        back = pltpu.roll(kept[g * given : (g + 1) * given], (LANES - rest + g * free) % LANES, 1)
        last = jnp.where((lane >= g * free) & (lane < (g + 1) * free), back, last)
    high = jnp.concatenate([kept, last], axis=0)
    return jnp.concatenate([value[:rows], high[:, :rest]], axis=1)


def message_shape(rows, width, extra):
    if packs(rows, width):
        return rows * width // LANES + extra, LANES
    return rows + extra, width


def three_parts(value):
    high = value.astype(BF16).astype(F32)
    middle = (value - high).astype(BF16).astype(F32)
    rest = value - high - middle
    lane = lax.broadcasted_iota(jnp.int32, value.shape, 1)
    return jnp.where(
        lane == 0, high, jnp.where(lane == 1, middle, jnp.where(lane == 2, rest, 0.0))
    ).astype(BF16)


def coulomb_into(acc_ref, x, ov_ref):
    n_aux, n_virt, n_occ = ov_ref.shape
    n_trial = x.shape[0]
    tiles = n_virt // TILE
    unit = (
        lax.broadcasted_iota(jnp.int32, (n_virt, n_virt), 0)
        == lax.broadcasted_iota(jnp.int32, (n_virt, n_virt), 1)
    ).astype(BF16)
    x_t = jnp.stack([dot_nt(unit, x[m]).astype(BF16) for m in range(n_trial)], 0)
    rows, cols = n_trial * TILE, n_aux * TILE

    def x_tile(t):
        return x_t[:, t * TILE : (t + 1) * TILE, :].reshape(rows, n_occ)

    def ov_tile(t):
        return ov_ref[:, t * TILE : (t + 1) * TILE, :].reshape(cols, n_occ)

    total = jnp.zeros((rows, cols), F32)
    for t in range(0, tiles, 2):
        span = range(t, min(t + 2, tiles))
        total += dot_nt(
            jnp.concatenate([x_tile(u) for u in span], axis=1),
            jnp.concatenate([ov_tile(u) for u in span], axis=1),
        )
    same = (
        lax.broadcasted_iota(jnp.int32, (rows, cols), 0) % TILE
        == lax.broadcasted_iota(jnp.int32, (rows, cols), 1) % TILE
    )
    coef = jnp.sum(jnp.where(same, total, 0.0).reshape(n_trial, TILE, cols), axis=1)
    lane = lax.broadcasted_iota(jnp.int32, coef.shape, 1)
    step = 1
    while step < TILE:
        coef += jnp.where(
            (lane & step) != 0, pltpu.roll(coef, step, 1), pltpu.roll(coef, cols - step, 1)
        )
        step *= 2
    twice = 2.0 * coef.astype(BF16).astype(F32)
    spread = jnp.broadcast_to(twice[:, None, :], (n_trial, TILE, cols)).reshape(rows, cols)
    weights = jnp.where(same, spread, 0.0).astype(BF16)
    for t in range(0, tiles, 2):
        span = range(t, min(t + 2, tiles))
        sums = dot(weights, jnp.concatenate([ov_tile(u) for u in span], axis=1))
        for k, u in enumerate(span):
            acc_ref[:, u * TILE : (u + 1) * TILE, :] -= sums[
                :, k * n_occ : (k + 1) * n_occ
            ].reshape(n_trial, TILE, n_occ)


def pair_weights(oo_refs, pair_ref, ready):
    n_occ = oo_refs[0].shape[1]
    half = n_occ // 2
    left = lax.broadcasted_iota(jnp.int32, (n_occ, n_occ), 1) < half
    at = 0
    for part, oo_ref in enumerate(oo_refs):
        if part == 1:
            ready()
        for g in range(oo_ref.shape[0] // 2):
            straight = [oo_ref[2 * g + odd].astype(F32) for odd in range(2)]
            moved = [pltpu.roll(value, half, 1) for value in straight]
            for odd in range(2):
                low = jnp.where(left, straight[odd], moved[1 - odd])
                high = jnp.where(left, moved[odd], straight[1 - odd])
                pair_ref[0, odd, at] = low.astype(BF16)
                pair_ref[1, odd, at] = high.astype(BF16)
            at += 1


def contract_half(x, pair_ref, k, vv_refs, acc_ref, mid_ref, ready=None):
    n_trial, half, n_virt = x.shape
    n_occ = 2 * half
    width = n_trial * half
    orders = [
        jnp.concatenate([x[m ^ odd] for m in range(n_trial)], axis=0) for odd in range(2)
    ]
    starts = [0]
    for vv_ref in vv_refs:
        starts.append(starts[-1] + vv_ref.shape[0] // 2)

    def transform(part):
        vv_ref, pairs = vv_refs[part], starts[part + 1] - starts[part]
        even, odd = (
            dot_nt(
                jnp.concatenate([vv_ref[2 * g + odd] for g in range(pairs)], axis=0),
                orders[odd],
            )
            for odd in range(2)
        )
        left = lax.broadcasted_iota(jnp.int32, even.shape, 1) % n_occ < half
        shape, span = (pairs, n_virt, width), pl.ds(starts[part], pairs)
        mid_ref[0, span] = jnp.where(left, even, odd).astype(BF16).reshape(shape)
        mid_ref[1, span] = jnp.where(left, odd, even).astype(BF16).reshape(shape)

    def gather_up(first, last):
        for odd in range(2):
            weights = jnp.concatenate(
                [pair_ref[k, odd, g] for g in range(first, last)], axis=1
            )
            for q in range(n_trial // 2):
                at = slice(q * n_occ, (q + 1) * n_occ)
                lines = jnp.concatenate(
                    [mid_ref[odd, g, :, at] for g in range(first, last)], axis=1
                )
                acc_ref[2 * q + odd] += dot_nt(lines, weights)

    if ready is None:
        for part in range(len(vv_refs)):
            transform(part)
        gather_up(0, starts[-1])
    else:
        for part in range(len(vv_refs)):
            if part == 1:
                ready()
            transform(part)
            gather_up(starts[part], starts[part + 1])


def place(target_ref, pieces_ref, first, mask, rows):
    for d in range(pieces_ref.shape[0]):
        at = pl.multiple_of(((first ^ d) & mask) * rows, rows)
        for m in range(pieces_ref.shape[1]):
            target_ref[m, pl.ds(at, rows), :] = pieces_ref[d, m].astype(F32)


def half_kernel(cut, me_ref, half_ref, pair_ref, vv_ref, more_ref, ov_ref, *refs):
    acc_ref, rest_ref, held_ov_ref, xs_ref, mid_ref, sem = refs
    copies = [
        pltpu.make_async_copy(
            more_ref.at[pl.ds(vv_ref.shape[0], rest_ref.shape[0])], rest_ref, sem.at[0]
        ),
        pltpu.make_async_copy(ov_ref, held_ov_ref, sem.at[1]),
    ]
    copies[0].start()

    def ready():
        copies[0].wait()
        copies[1].start()

    if cut:
        place(xs_ref, half_ref, me_ref[0], half_ref.shape[0] - 1, half_ref.shape[2])
    else:
        xs_ref[...] = half_ref[...].astype(F32)
    acc_ref[...] = jnp.zeros_like(acc_ref)
    x = xs_ref[...].astype(BF16)
    contract_half(x, pair_ref, me_ref[1], (vv_ref, rest_ref), acc_ref, mid_ref, ready)
    copies[1].wait()


def build_kernel(low, cut, me_ref, occ_ref, vir_ref, own_ref, held_ref, *refs):
    parts = 1 << low
    pieces, (ov_ref, pair_ref, *vv_refs), outs = refs[:2], refs[2:6], refs[6:-3]
    xs_ref, mid_ref, acc_ref = refs[-3:]
    n_trial, rows, n_virt = own_ref.shape
    n_occ = ov_ref.shape[2]
    size, half = n_occ // rows, n_occ // 2
    high_count = size >> low
    me, other = me_ref[0], 1 - me_ref[1]
    mine = me & (parts - 1)
    if cut:
        place(xs_ref, pieces[0], me, size - 1, rows)
        place(xs_ref, pieces[1], me ^ (size // 2), size - 1, rows)
    else:
        for k, piece in enumerate(pieces):
            at = pl.multiple_of((me_ref[1] ^ k) * half, half)
            for m in range(n_trial):
                xs_ref[m, pl.ds(at, half), :] = piece[m].astype(F32)
    x = xs_ref[...].astype(BF16)
    acc_ref[...] = held_ref[...]
    coulomb_into(acc_ref, x, ov_ref)
    rest = pl.ds(pl.multiple_of(other * half, half), half)
    x_rest = jnp.stack([xs_ref[m, rest, :] for m in range(n_trial)], 0).astype(BF16)
    contract_half(x_rest, pair_ref, other, vv_refs, acc_ref, mid_ref)
    unit = (
        lax.broadcasted_iota(jnp.int32, (n_occ, 2 * n_occ), 0)
        == lax.broadcasted_iota(jnp.int32, (n_occ, 2 * n_occ), 1) % n_occ
    ).astype(BF16)
    lines = []
    for m in range(n_trial):
        turned = acc_ref[m]
        high = turned.astype(BF16)
        rest = (turned - high.astype(F32)).astype(BF16)
        value = -dot_nt(unit, jnp.concatenate([high, rest], axis=1))
        seen = xs_ref[m]
        lines.append(jnp.sum(jnp.sum(seen * value, axis=0, keepdims=True), axis=1, keepdims=True))
        xs_ref[m] = value
    own = own_ref[...]
    square = own * own
    diag = diagonal(occ_ref, vir_ref, me * rows, rows)
    for m in range(n_trial):
        lines[m] += jnp.sum(
            jnp.sum(square[m] * diag, axis=0, keepdims=True), axis=1, keepdims=True
        )
    for m in range(n_trial):
        lines.append(
            jnp.sum(jnp.sum(square[m], axis=0, keepdims=True), axis=1, keepdims=True)
        )
    body = high_count * n_trial * rows
    height, wide = message_shape(body, n_virt, 0)
    scalars = jnp.concatenate([jnp.broadcast_to(line, (1, wide)) for line in lines], axis=0)
    single = jnp.where(
        lax.broadcasted_iota(jnp.int32, scalars.shape, 1) == 0, scalars, 0.0
    )
    coded = three_parts(scalars)
    if not cut:
        for ref, value in zip(outs, (xs_ref[...], single, coded)):
            ref[...] = value
        return
    outs[0][height:, :] = single
    for k in range(parts):
        blocks = []
        for z in range(high_count):
            at = pl.multiple_of(((z << low) | (mine ^ k)) * rows, rows)
            blocks += [xs_ref[m, pl.ds(at, rows), :] for m in range(n_trial)]
        whole = dense(jnp.concatenate(blocks, axis=0))
        if k == 0:
            outs[0][:height, :] = whole
        else:
            outs[k][:height, :] = whole.astype(BF16)
            outs[k][height:, :] = coded


def pack_kernel(*refs):
    at = 0
    for ref in refs[:-1]:
        count = ref.shape[0]
        refs[-1][at : at + count] = ref[...].astype(BF16)
        at += count


def pack(arrays):
    count = sum(a.shape[0] for a in arrays)
    return pl.pallas_call(
        pack_kernel,
        out_shape=jax.ShapeDtypeStruct((count,) + arrays[0].shape[1:], BF16),
        in_specs=[VMEM] * len(arrays),
        out_specs=VMEM,
        compiler_params=SMALL,
    )(*arrays)


def in_vmem(*arrays):
    return [pltpu.with_memory_space_constraint(a, pltpu.VMEM) for a in arrays]


def in_order(half, me):
    count, n_trial, rows, n_virt = half.shape
    order = (me & (count - 1)) ^ jnp.arange(count)
    return half[order].transpose(1, 0, 2, 3).reshape(n_trial, count * rows, n_virt)


def in_hbm(*arrays):
    return [pltpu.with_memory_space_constraint(a, pltpu.HBM) for a in arrays]


def first_half(me_pair, half, pairs, exch_vv, more_vv, coul_t):
    cut = half.ndim == 4
    n_aux, n_virt, n_occ = coul_t.shape
    n_trial = half.shape[1] if cut else half.shape[0]
    flops = n_aux * n_trial * n_occ * n_virt * (n_virt + n_occ)
    return pl.pallas_call(
        functools.partial(half_kernel, cut),
        out_shape=[
            pltpu.VMEM((n_trial, n_virt, n_occ), F32),
            pltpu.VMEM((n_aux - exch_vv.shape[0], n_virt, n_virt), BF16),
            pltpu.VMEM(coul_t.shape, BF16),
        ],
        in_specs=[SMEM] + [VMEM] * 3 + [HBM] * 2,
        out_specs=[VMEM] * 3,
        scratch_shapes=[
            pltpu.VMEM((n_trial, n_occ // 2, n_virt), F32),
            pltpu.VMEM((2, n_aux // 2, n_virt, n_trial * n_occ // 2), BF16),
            pltpu.SemaphoreType.DMA((2,)),
        ],
        compiler_params=pltpu.CompilerParams(vmem_limit_bytes=32 << 20),
        cost_estimate=pl.CostEstimate(
            flops=flops, bytes_accessed=2 * (exch_vv.size + coul_t.size), transcendentals=0
        ),
    )(me_pair, half, *in_vmem(pairs, exch_vv), *in_hbm(more_vv, coul_t))


def dense_call(value):
    def kernel(value_ref, out_ref):
        out_ref[...] = dense(value_ref[...])

    return pl.pallas_call(
        kernel,
        out_shape=jax.ShapeDtypeStruct(message_shape(*value.shape, 0), value.dtype),
        in_specs=[VMEM],
        out_specs=VMEM,
        compiler_params=SMALL,
    )(value)


def build(me_pair, occ, vir, own, held, pieces, coul_t, pairs, exch_vv, low):
    parts = 1 << low
    n_trial, rows, n_virt = own.shape
    n_aux, _, n_occ = coul_t.shape
    high_count = n_occ // rows >> low
    cut = pieces[0].ndim == 4
    height, extra = high_count * n_trial * rows, 2 * n_trial
    shape = message_shape(height, n_virt, extra)
    if cut:
        shapes = [jax.ShapeDtypeStruct(shape, F32)]
        shapes += [jax.ShapeDtypeStruct(shape, BF16)] * (parts - 1)
    else:
        shapes = [
            jax.ShapeDtypeStruct((n_trial, n_occ, n_virt), F32),
            jax.ShapeDtypeStruct((extra, shape[1]), F32),
            jax.ShapeDtypeStruct((extra, shape[1]), BF16),
        ]
    flops = n_aux * n_trial * n_occ * n_virt * (n_virt + n_occ)
    moved = 2 * (coul_t.size + pairs.size + sum(a.size for a in exch_vv))
    results = pl.pallas_call(
        functools.partial(build_kernel, low, cut),
        out_shape=shapes,
        in_specs=[SMEM] + [VMEM] * 10,
        out_specs=[VMEM] * len(shapes),
        scratch_shapes=[
            pltpu.VMEM((n_trial, n_occ, n_virt), F32),
            pltpu.VMEM((2, n_aux // 2, n_virt, n_trial * n_occ // 2), BF16),
            pltpu.VMEM((n_trial, n_virt, n_occ), F32),
        ],
        compiler_params=pltpu.CompilerParams(vmem_limit_bytes=32 << 20),
        cost_estimate=pl.CostEstimate(flops=flops, bytes_accessed=moved, transcendentals=0),
    )(me_pair, occ, vir, own, *in_vmem(held), *pieces, *in_vmem(coul_t, pairs, *exch_vv))
    if cut:
        return results
    value, single, coded = results
    value = value.reshape(n_trial, high_count, parts, rows, n_virt).transpose(2, 1, 0, 3, 4)
    mine = me_pair[0] & (parts - 1)
    blocks = [
        dense_call(
            lax.dynamic_index_in_dim(value, mine ^ k, 0, keepdims=False).reshape(height, n_virt)
        )
        for k in range(parts)
    ]
    return [jnp.concatenate([blocks[0], single], axis=0)] + [
        jnp.concatenate([block.astype(BF16), coded], axis=0) for block in blocks[1:]
    ]


def summed(own_ref, arrived):
    total = own_ref[...]
    for ref in arrived:
        total += ref[...].astype(F32)
    return total


def combine_kernel(extra, own_ref, *refs):
    arrived, (total_ref, send_ref) = refs[:-2], refs[-2:]
    total = summed(own_ref, arrived)
    body = total.shape[0] - extra
    scalars = jnp.sum(total[body:], axis=1, keepdims=True)
    scalars = jnp.broadcast_to(scalars, (extra, total.shape[1]))
    lane = lax.broadcasted_iota(jnp.int32, scalars.shape, 1)
    total_ref[:body, :] = total[:body]
    total_ref[body:, :] = jnp.where(lane == 0, scalars, 0.0)
    send_ref[:body, :] = total[:body].astype(BF16)
    send_ref[body:, :] = three_parts(scalars)


def combine(own, arrived, extra):
    return pl.pallas_call(
        functools.partial(combine_kernel, extra),
        out_shape=[
            jax.ShapeDtypeStruct(own.shape, F32),
            jax.ShapeDtypeStruct(own.shape, BF16),
        ],
        in_specs=[VMEM] * (1 + len(arrived)),
        out_specs=[VMEM] * 2,
        compiler_params=SMALL,
    )(own, *arrived)


def residual_kernel(low, me_ref, occ_ref, vir_ref, near_ref, near_half, far_half, own_ref, *refs):
    arrived, (sigma_ref, precond_ref, square_ref, held_ref) = refs[:-4], refs[-4:]
    n_trial, rows, n_virt = near_ref.shape
    count = near_half.shape[0]
    high_count = 2 * count >> low
    body = high_count * n_trial * rows
    mine, top = me_ref[0] & ((1 << low) - 1), me_ref[0] >> low
    total = summed(own_ref, arrived)
    height = message_shape(body, n_virt, 0)[0]
    held_ref[...] = spread(total[:height], body, n_virt).reshape(held_ref.shape)
    scalars = jnp.sum(total[height:], axis=1, keepdims=True)
    omega = scalars[:n_trial] / (scalars[n_trial:] + 1e-06)
    squares = [jnp.zeros((rows, n_virt), F32) for _ in range(n_trial)]
    for r in range(high_count):
        diag = diagonal(occ_ref, vir_ref, (((top ^ r) << low) | mine) * rows, rows)
        block = held_ref[top ^ r]
        for m in range(n_trial):
            away = r << low
            if r == 0:
                t = near_ref[m]
            else:
                t = (near_half if away < count else far_half)[away % count, m].astype(F32)
            level = omega[m : m + 1]
            sigma = diag * t + block[m * rows : (m + 1) * rows]
            precond = (sigma - level * t) / jnp.maximum(jnp.abs(diag - level), 1.0)
            squares[m] += precond * precond
            if r == 0:
                sigma_ref[m] = sigma
                precond_ref[m] = precond
    sums = [
        jnp.sum(jnp.sum(s, axis=0, keepdims=True), axis=1, keepdims=True) for s in squares
    ]
    square_ref[...] = jnp.concatenate(
        [jnp.broadcast_to(s, (1, square_ref.shape[1])) for s in sums], axis=0
    )


def residual(me_pair, occ, vir, low, near, halves, own, arrived):
    n_trial, rows, n_virt = near.shape
    high_count = 2 * halves[0].shape[0] >> low
    return pl.pallas_call(
        functools.partial(residual_kernel, low),
        out_shape=[pltpu.VMEM(near.shape, F32)] * 2 + [pltpu.VMEM((n_trial, 128), F32)],
        in_specs=[SMEM] + [VMEM] * (6 + len(arrived)),
        out_specs=[VMEM] * 3,
        scratch_shapes=[pltpu.VMEM((high_count, n_trial * rows, n_virt), F32)],
        compiler_params=SMALL,
    )(me_pair, occ, vir, near, *halves, own, *arrived)


def finish_kernel(count, precond_ref, *refs):
    update_ref = refs[-1]
    square = refs[0][...]
    for ref in refs[1:-1]:
        square += ref[...]
    scale = lax.rsqrt(square[:, :1] / count + 1e-06)
    for m in range(precond_ref.shape[0]):
        update_ref[m] = precond_ref[m] * scale[m : m + 1]


def finish(count, precond, squares):
    return pl.pallas_call(
        functools.partial(finish_kernel, count),
        out_shape=jax.ShapeDtypeStruct(precond.shape, F32),
        in_specs=[VMEM] * (1 + len(squares)),
        out_specs=VMEM,
        compiler_params=SMALL,
    )(precond, *squares)


def fetch_kernel(count, after_ref, *refs):
    del after_ref
    sources, targets, sem = refs[:count], refs[count : 2 * count], refs[-1]
    copies = [
        pltpu.make_async_copy(source.at[pl.ds(0, target.shape[0])], target, sem.at[k])
        for k, (source, target) in enumerate(zip(sources, targets))
    ]
    for copy in copies:
        copy.start()
    for copy in copies:
        copy.wait()


def fetch(after, counts, *arrays):
    return pl.pallas_call(
        functools.partial(fetch_kernel, len(arrays)),
        out_shape=[pltpu.VMEM((n,) + a.shape[1:], a.dtype) for n, a in zip(counts, arrays)],
        in_specs=[ANY] + [HBM] * len(arrays),
        out_specs=[VMEM] * len(arrays),
        scratch_shapes=[pltpu.SemaphoreType.DMA((len(arrays),))],
        compiler_params=SMALL,
        cost_estimate=pl.CostEstimate(
            flops=0, bytes_accessed=sum(4 * a.size for a in arrays), transcendentals=0
        ),
    )(after, *in_hbm(*arrays))


def prepare_kernel(after_ref, early_ref, oo_ref, vv_ref, pair_ref, held_ref, late_ref, sem):
    del after_ref
    first = pltpu.make_async_copy(
        oo_ref.at[pl.ds(early_ref.shape[0], late_ref.shape[0])], late_ref, sem.at[0]
    )
    second = pltpu.make_async_copy(
        vv_ref.at[pl.ds(0, held_ref.shape[0])], held_ref, sem.at[1]
    )
    first.start()
    second.start()
    pair_weights((early_ref, late_ref), pair_ref, first.wait)
    second.wait()


def prepare(after, early_oo, exch_oo, exch_vv):
    n_aux, n_occ, _ = exch_oo.shape
    early = early_oo.shape[0]
    return pl.pallas_call(
        prepare_kernel,
        out_shape=[
            pltpu.VMEM((2, 2, n_aux // 2, n_occ, n_occ), BF16),
            pltpu.VMEM((n_aux // 4 * 2,) + exch_vv.shape[1:], BF16),
        ],
        in_specs=[ANY, VMEM, HBM, HBM],
        out_specs=[VMEM] * 2,
        scratch_shapes=[
            pltpu.VMEM((n_aux - early, n_occ, n_occ), BF16),
            pltpu.SemaphoreType.DMA((2,)),
        ],
        compiler_params=SMALL,
        cost_estimate=pl.CostEstimate(
            flops=0, bytes_accessed=4 * (exch_oo.size + exch_vv.size), transcendentals=0
        ),
    )(after, *in_vmem(early_oo), *in_hbm(exch_oo, exch_vv))


def on_device(size, trial_vecs, occ_energy, vir_energy, coul_ov, exch_oo, exch_vv):
    n_trial, rows, n_virt = trial_vecs.shape
    n_occ = exch_oo.shape[1]
    low, highs = bit_groups(size)
    me = lax.axis_index("aux").astype(jnp.int32)
    top = size.bit_length() - 2
    me_pair = jnp.stack([me, me >> top])
    coul_t = jnp.transpose(coul_ov, (0, 2, 1))
    counts = (trial_vecs.shape[0], 1, 1, exch_oo.shape[0] // EARLY * 2)
    near, occ, vir, early_oo = fetch(
        me_pair, counts, trial_vecs, occ_energy[None], vir_energy[None], exch_oo
    )
    held = pack([near[None]] + [a[None] for a in exchange(trial_vecs, size, 0, 1)])
    pairs, vv = prepare(held, early_oo, exch_oo, exch_vv)
    for at in range(1, top, 2):
        held = pack([held] + exchange(held, size, at, min(2, top - at)))
    far, = exchange(held, size, top, 1)
    halves = [held, far]
    pieces = halves if rows % 8 == 0 else [in_order(half, me) for half in halves]
    half_sum, more_vv, coul_t = first_half(
        me_pair, pieces[0], pairs, vv, exch_vv, coul_t
    )
    own, *sends = build(
        me_pair, occ, vir, near, half_sum, pieces, coul_t, pairs, (vv, more_vv), low
    )
    arrived = [swap(send, size, k + 1) for k, send in enumerate(sends)]
    for at, width in highs:
        own, send = combine(own, arrived, 2 * n_trial)
        arrived = exchange(send, size, at, width)
    sigma_vecs, precond, square = residual(me_pair, occ, vir, low, near, halves, own, arrived)
    squares = [square] + exchange(square, size, 0, low)
    return sigma_vecs, finish(n_occ * n_virt, precond, squares)


def solution(mesh):
    in_specs = (
        P("geom", "aux", None),
        P("geom"),
        P("geom"),
        P(("geom", "aux"), None, None),
        P(("geom", "aux"), None, None),
        P(("geom", "aux"), None, None),
    )
    out_specs = (P("geom", "aux", None), P("geom", "aux", None))
    return jax.shard_map(
        functools.partial(on_device, mesh.shape["aux"]),
        mesh=mesh,
        in_specs=in_specs,
        out_specs=out_specs,
        check_vma=False,
    )
```

```python
import functools

import jax
import jax.numpy as jnp
from jax import lax
from jax.experimental import pallas as pl
from jax.experimental.pallas import tpu as pltpu
from jax.sharding import PartitionSpec as P


F32 = jnp.float32
BF16 = jnp.bfloat16
LOW_BITS = 2
LANES = 128
EARLY = 8
TILE = 16
VMEM = pl.BlockSpec(memory_space=pltpu.VMEM)
SMEM = pl.BlockSpec(memory_space=pltpu.SMEM)
HBM = pl.BlockSpec(memory_space=pltpu.HBM)
ANY = pl.BlockSpec(memory_space=pl.ANY)
SMALL = pltpu.CompilerParams(vmem_limit_bytes=4 << 20)


def bit_groups(size):
    bits = size.bit_length() - 1
    assert size == 1 << bits
    low = min(LOW_BITS, bits)
    return low, [(at, min(LOW_BITS, bits - at)) for at in range(low, bits, LOW_BITS)]


def swap(value, size, offset):
    return lax.ppermute(value, "aux", [(i, i ^ offset) for i in range(size)])


def exchange(value, size, at, width):
    return [swap(value, size, k << at) for k in range(1, 1 << width)]


def dot(a, b):
    return jnp.dot(a, b, preferred_element_type=F32)


def dot_nt(a, b):
    return lax.dot_general(a, b, (((1,), (1,)), ((), ())), preferred_element_type=F32)


def diagonal(occ_ref, vir_ref, first, rows):
    shape = (rows, occ_ref.shape[1])
    wanted = lax.broadcasted_iota(jnp.int32, shape, 0) + first
    picked = jnp.where(lax.broadcasted_iota(jnp.int32, shape, 1) == wanted, occ_ref[...], 0.0)
    return vir_ref[...] - jnp.sum(picked, axis=1, keepdims=True)


def packs(rows, width):
    rest, free = width - LANES, 2 * LANES - width
    if not 0 < rest < LANES or rest % free or rows * free % LANES:
        return 0
    given = rows * free // LANES
    return given if given % 8 == 0 else 0


def dense(value):
    rows, width = value.shape
    given = packs(rows, width)
    if not given:
        return value
    rest, free = width - LANES, 2 * LANES - width
    high = jnp.concatenate([value[:, LANES:], jnp.zeros((rows, free), value.dtype)], axis=1)
    kept, last = high[: rows - given], high[rows - given :]
    moved = [
        pltpu.roll(last, (rest - g * free) % LANES, 1) for g in range(rest // free)
    ]
    lane = lax.broadcasted_iota(jnp.int32, kept.shape, 1)
    kept = jnp.where(lane < rest, kept, jnp.concatenate(moved, axis=0))
    return jnp.concatenate([value[:, :LANES], kept], axis=0)


def spread(value, rows, width):
    given = packs(rows, width)
    if not given:
        return value
    rest, free = width - LANES, 2 * LANES - width
    kept = value[rows:]
    last = jnp.zeros((given, LANES), value.dtype)
    lane = lax.broadcasted_iota(jnp.int32, last.shape, 1)
    for g in range(rest // free):
        back = pltpu.roll(kept[g * given : (g + 1) * given], (LANES - rest + g * free) % LANES, 1)
        last = jnp.where((lane >= g * free) & (lane < (g + 1) * free), back, last)
    high = jnp.concatenate([kept, last], axis=0)
    return jnp.concatenate([value[:rows], high[:, :rest]], axis=1)


def message_shape(rows, width, extra):
    if packs(rows, width):
        return rows * width // LANES + extra, LANES
    return rows + extra, width


def three_parts(value):
    high = value.astype(BF16).astype(F32)
    middle = (value - high).astype(BF16).astype(F32)
    rest = value - high - middle
    lane = lax.broadcasted_iota(jnp.int32, value.shape, 1)
    return jnp.where(
        lane == 0, high, jnp.where(lane == 1, middle, jnp.where(lane == 2, rest, 0.0))
    ).astype(BF16)


def coulomb_into(acc_ref, x, ov_ref):
    n_aux, n_virt, n_occ = ov_ref.shape
    n_trial = x.shape[0]
    tiles = n_virt // TILE
    unit = (
        lax.broadcasted_iota(jnp.int32, (n_virt, n_virt), 0)
        == lax.broadcasted_iota(jnp.int32, (n_virt, n_virt), 1)
    ).astype(BF16)
    x_t = jnp.stack([dot_nt(unit, x[m]).astype(BF16) for m in range(n_trial)], 0)
    rows, cols = n_trial * TILE, n_aux * TILE

    def x_tile(t):
        return x_t[:, t * TILE : (t + 1) * TILE, :].reshape(rows, n_occ)

    def ov_tile(t):
        return ov_ref[:, t * TILE : (t + 1) * TILE, :].reshape(cols, n_occ)

    total = jnp.zeros((rows, cols), F32)
    for t in range(0, tiles, 2):
        span = range(t, min(t + 2, tiles))
        total += dot_nt(
            jnp.concatenate([x_tile(u) for u in span], axis=1),
            jnp.concatenate([ov_tile(u) for u in span], axis=1),
        )
    same = (
        lax.broadcasted_iota(jnp.int32, (rows, cols), 0) % TILE
        == lax.broadcasted_iota(jnp.int32, (rows, cols), 1) % TILE
    )
    coef = jnp.sum(jnp.where(same, total, 0.0).reshape(n_trial, TILE, cols), axis=1)
    lane = lax.broadcasted_iota(jnp.int32, coef.shape, 1)
    step = 1
    while step < TILE:
        coef += jnp.where(
            (lane & step) != 0, pltpu.roll(coef, step, 1), pltpu.roll(coef, cols - step, 1)
        )
        step *= 2
    twice = 2.0 * coef.astype(BF16).astype(F32)
    spread = jnp.broadcast_to(twice[:, None, :], (n_trial, TILE, cols)).reshape(rows, cols)
    weights = jnp.where(same, spread, 0.0).astype(BF16)
    for t in range(0, tiles, 2):
        span = range(t, min(t + 2, tiles))
        sums = dot(weights, jnp.concatenate([ov_tile(u) for u in span], axis=1))
        for k, u in enumerate(span):
            acc_ref[:, u * TILE : (u + 1) * TILE, :] -= sums[
                :, k * n_occ : (k + 1) * n_occ
            ].reshape(n_trial, TILE, n_occ)


def pair_weights(oo_refs, pair_ref, ready):
    n_occ = oo_refs[0].shape[1]
    half = n_occ // 2
    left = lax.broadcasted_iota(jnp.int32, (n_occ, n_occ), 1) < half
    at = 0
    for part, oo_ref in enumerate(oo_refs):
        if part == 1:
            ready()
        for g in range(oo_ref.shape[0] // 2):
            straight = [oo_ref[2 * g + odd].astype(F32) for odd in range(2)]
            moved = [pltpu.roll(value, half, 1) for value in straight]
            for odd in range(2):
                low = jnp.where(left, straight[odd], moved[1 - odd])
                high = jnp.where(left, moved[odd], straight[1 - odd])
                pair_ref[0, odd, at] = low.astype(BF16)
                pair_ref[1, odd, at] = high.astype(BF16)
            at += 1


def contract_half(x, pair_ref, k, vv_refs, acc_ref, mid_ref, ready=None):
    n_trial, half, n_virt = x.shape
    n_occ = 2 * half
    width = n_trial * half
    orders = [
        jnp.concatenate([x[m ^ odd] for m in range(n_trial)], axis=0) for odd in range(2)
    ]
    starts = [0]
    for vv_ref in vv_refs:
        starts.append(starts[-1] + vv_ref.shape[0] // 2)

    def transform(part):
        vv_ref, pairs = vv_refs[part], starts[part + 1] - starts[part]
        even, odd = (
            dot_nt(
                jnp.concatenate([vv_ref[2 * g + odd] for g in range(pairs)], axis=0),
                orders[odd],
            )
            for odd in range(2)
        )
        left = lax.broadcasted_iota(jnp.int32, even.shape, 1) % n_occ < half
        shape, span = (pairs, n_virt, width), pl.ds(starts[part], pairs)
        mid_ref[0, span] = jnp.where(left, even, odd).astype(BF16).reshape(shape)
        mid_ref[1, span] = jnp.where(left, odd, even).astype(BF16).reshape(shape)

    def gather_up(first, last):
        for odd in range(2):
            weights = jnp.concatenate(
                [pair_ref[k, odd, g] for g in range(first, last)], axis=1
            )
            for q in range(n_trial // 2):
                at = slice(q * n_occ, (q + 1) * n_occ)
                lines = jnp.concatenate(
                    [mid_ref[odd, g, :, at] for g in range(first, last)], axis=1
                )
                acc_ref[2 * q + odd] += dot_nt(lines, weights)

    if ready is None:
        for part in range(len(vv_refs)):
            transform(part)
        gather_up(0, starts[-1])
    else:
        for part in range(len(vv_refs)):
            if part == 1:
                ready()
            transform(part)
            gather_up(starts[part], starts[part + 1])


def place(target_ref, pieces_ref, first, mask, rows):
    for d in range(pieces_ref.shape[0]):
        at = pl.multiple_of(((first ^ d) & mask) * rows, rows)
        for m in range(pieces_ref.shape[1]):
            target_ref[m, pl.ds(at, rows), :] = pieces_ref[d, m].astype(F32)


def place_rows(target_ref, value, first, mask, rows):
    n_trial = target_ref.shape[0]
    for d in range(value.shape[0] // (n_trial * rows)):
        at = pl.multiple_of(((first ^ d) & mask) * rows, rows)
        for m in range(n_trial):
            row = (d * n_trial + m) * rows
            target_ref[m, pl.ds(at, rows), :] = value[row : row + rows]


def half_kernel(cut, me_ref, half_ref, pair_ref, vv_ref, more_ref, ov_ref, *refs):
    acc_ref, rest_ref, held_ov_ref, xs_ref, mid_ref, sem = refs
    copies = [
        pltpu.make_async_copy(
            more_ref.at[pl.ds(vv_ref.shape[0], rest_ref.shape[0])], rest_ref, sem.at[0]
        ),
        pltpu.make_async_copy(ov_ref, held_ov_ref, sem.at[1]),
    ]
    copies[0].start()

    def ready():
        copies[0].wait()
        copies[1].start()

    if cut:
        place(xs_ref, half_ref, me_ref[0], half_ref.shape[0] - 1, half_ref.shape[2])
    else:
        xs_ref[...] = half_ref[...].astype(F32)
    acc_ref[...] = jnp.zeros_like(acc_ref)
    x = xs_ref[...].astype(BF16)
    contract_half(x, pair_ref, me_ref[1], (vv_ref, rest_ref), acc_ref, mid_ref, ready)
    copies[1].wait()


def build_kernel(low, cut, me_ref, occ_ref, vir_ref, own_ref, held_ref, *refs):
    parts = 1 << low
    pieces, (ov_ref, pair_ref, *vv_refs), outs = refs[:2], refs[2:6], refs[6:-3]
    xs_ref, mid_ref, acc_ref = refs[-3:]
    n_trial, rows, n_virt = own_ref.shape
    n_occ = ov_ref.shape[2]
    size, half = n_occ // rows, n_occ // 2
    high_count = size >> low
    me, other = me_ref[0], 1 - me_ref[1]
    mine = me & (parts - 1)
    if cut:
        place(xs_ref, pieces[0], me, size - 1, rows)
        far = spread(pieces[1][...].astype(F32), half * n_trial, n_virt)
        place_rows(xs_ref, far, me ^ (size // 2), size - 1, rows)
    else:
        for k, piece in enumerate(pieces):
            at = pl.multiple_of((me_ref[1] ^ k) * half, half)
            for m in range(n_trial):
                xs_ref[m, pl.ds(at, half), :] = piece[m].astype(F32)
    x = xs_ref[...].astype(BF16)
    acc_ref[...] = held_ref[...]
    coulomb_into(acc_ref, x, ov_ref)
    rest = pl.ds(pl.multiple_of(other * half, half), half)
    x_rest = jnp.stack([xs_ref[m, rest, :] for m in range(n_trial)], 0).astype(BF16)
    contract_half(x_rest, pair_ref, other, vv_refs, acc_ref, mid_ref)
    unit = (
        lax.broadcasted_iota(jnp.int32, (n_occ, n_occ), 0)
        == lax.broadcasted_iota(jnp.int32, (n_occ, n_occ), 1)
    ).astype(BF16)
    lines = []
    for m in range(n_trial):
        value = -dot_nt(unit, acc_ref[m].astype(BF16))
        seen = xs_ref[m]
        lines.append(jnp.sum(jnp.sum(seen * value, axis=0, keepdims=True), axis=1, keepdims=True))
        xs_ref[m] = value
    own = own_ref[...]
    square = own * own
    diag = diagonal(occ_ref, vir_ref, me * rows, rows)
    for m in range(n_trial):
        lines[m] += jnp.sum(
            jnp.sum(square[m] * diag, axis=0, keepdims=True), axis=1, keepdims=True
        )
    for m in range(n_trial):
        lines.append(
            jnp.sum(jnp.sum(square[m], axis=0, keepdims=True), axis=1, keepdims=True)
        )
    body = high_count * n_trial * rows
    height, wide = message_shape(body, n_virt, 0)
    scalars = jnp.concatenate([jnp.broadcast_to(line, (1, wide)) for line in lines], axis=0)
    single = jnp.where(
        lax.broadcasted_iota(jnp.int32, scalars.shape, 1) == 0, scalars, 0.0
    )
    coded = three_parts(scalars)
    if not cut:
        for ref, value in zip(outs, (xs_ref[...], single, coded)):
            ref[...] = value
        return
    outs[0][height:, :] = single
    for k in range(parts):
        blocks = []
        for z in range(high_count):
            at = pl.multiple_of(((z << low) | (mine ^ k)) * rows, rows)
            blocks += [xs_ref[m, pl.ds(at, rows), :] for m in range(n_trial)]
        whole = dense(jnp.concatenate(blocks, axis=0))
        if k == 0:
            outs[0][:height, :] = whole
        else:
            outs[k][:height, :] = whole.astype(BF16)
            outs[k][height:, :] = coded


def pack_kernel(count, *refs):
    target_ref, at, rows = refs[count], 0, []
    for ref in refs[:count]:
        value = ref[...].astype(F32)
        target_ref[at : at + ref.shape[0]] = value.astype(BF16)
        at += ref.shape[0]
        rows.append(value.reshape(-1, ref.shape[-1]) if refs[count + 1 :] else None)
    for ref in refs[count + 1 :]:
        ref[...] = dense(jnp.concatenate(rows, axis=0)).astype(BF16)


def pack(arrays, message=False):
    shape = (sum(a.shape[0] for a in arrays),) + arrays[0].shape[1:]
    shapes = [shape]
    if message:
        shapes.append(message_shape(shape[0] * shape[1] * shape[2], shape[3], 0))
    return pl.pallas_call(
        functools.partial(pack_kernel, len(arrays)),
        out_shape=[jax.ShapeDtypeStruct(one, BF16) for one in shapes],
        in_specs=[VMEM] * len(arrays),
        out_specs=[VMEM] * len(shapes),
        compiler_params=SMALL,
    )(*arrays)


def in_vmem(*arrays):
    return [pltpu.with_memory_space_constraint(a, pltpu.VMEM) for a in arrays]


def in_order(half, me):
    count, n_trial, rows, n_virt = half.shape
    order = (me & (count - 1)) ^ jnp.arange(count)
    return half[order].transpose(1, 0, 2, 3).reshape(n_trial, count * rows, n_virt)


def in_hbm(*arrays):
    return [pltpu.with_memory_space_constraint(a, pltpu.HBM) for a in arrays]


def first_half(me_pair, half, pairs, exch_vv, more_vv, coul_t):
    cut = half.ndim == 4
    n_aux, n_virt, n_occ = coul_t.shape
    n_trial = half.shape[1] if cut else half.shape[0]
    flops = n_aux * n_trial * n_occ * n_virt * (n_virt + n_occ)
    return pl.pallas_call(
        functools.partial(half_kernel, cut),
        out_shape=[
            pltpu.VMEM((n_trial, n_virt, n_occ), F32),
            pltpu.VMEM((n_aux - exch_vv.shape[0], n_virt, n_virt), BF16),
            pltpu.VMEM(coul_t.shape, BF16),
        ],
        in_specs=[SMEM] + [VMEM] * 3 + [HBM] * 2,
        out_specs=[VMEM] * 3,
        scratch_shapes=[
            pltpu.VMEM((n_trial, n_occ // 2, n_virt), F32),
            pltpu.VMEM((2, n_aux // 2, n_virt, n_trial * n_occ // 2), BF16),
            pltpu.SemaphoreType.DMA((2,)),
        ],
        compiler_params=pltpu.CompilerParams(vmem_limit_bytes=32 << 20),
        cost_estimate=pl.CostEstimate(
            flops=flops, bytes_accessed=2 * (exch_vv.size + coul_t.size), transcendentals=0
        ),
    )(me_pair, half, *in_vmem(pairs, exch_vv), *in_hbm(more_vv, coul_t))


def dense_call(value):
    def kernel(value_ref, out_ref):
        out_ref[...] = dense(value_ref[...])

    return pl.pallas_call(
        kernel,
        out_shape=jax.ShapeDtypeStruct(message_shape(*value.shape, 0), value.dtype),
        in_specs=[VMEM],
        out_specs=VMEM,
        compiler_params=SMALL,
    )(value)


def build(me_pair, occ, vir, own, held, pieces, coul_t, pairs, exch_vv, low):
    parts = 1 << low
    n_trial, rows, n_virt = own.shape
    n_aux, _, n_occ = coul_t.shape
    high_count = n_occ // rows >> low
    cut = rows % 8 == 0
    height, extra = high_count * n_trial * rows, 2 * n_trial
    shape = message_shape(height, n_virt, extra)
    if cut:
        shapes = [jax.ShapeDtypeStruct(shape, F32)]
        shapes += [jax.ShapeDtypeStruct(shape, BF16)] * (parts - 1)
    else:
        shapes = [
            jax.ShapeDtypeStruct((n_trial, n_occ, n_virt), F32),
            jax.ShapeDtypeStruct((extra, shape[1]), F32),
            jax.ShapeDtypeStruct((extra, shape[1]), BF16),
        ]
    flops = n_aux * n_trial * n_occ * n_virt * (n_virt + n_occ)
    moved = 2 * (coul_t.size + pairs.size + sum(a.size for a in exch_vv))
    results = pl.pallas_call(
        functools.partial(build_kernel, low, cut),
        out_shape=shapes,
        in_specs=[SMEM] + [VMEM] * 10,
        out_specs=[VMEM] * len(shapes),
        scratch_shapes=[
            pltpu.VMEM((n_trial, n_occ, n_virt), F32),
            pltpu.VMEM((2, n_aux // 2, n_virt, n_trial * n_occ // 2), BF16),
            pltpu.VMEM((n_trial, n_virt, n_occ), F32),
        ],
        compiler_params=pltpu.CompilerParams(vmem_limit_bytes=32 << 20),
        cost_estimate=pl.CostEstimate(flops=flops, bytes_accessed=moved, transcendentals=0),
    )(me_pair, occ, vir, own, *in_vmem(held), *pieces, *in_vmem(coul_t, pairs, *exch_vv))
    if cut:
        return results
    value, single, coded = results
    value = value.reshape(n_trial, high_count, parts, rows, n_virt).transpose(2, 1, 0, 3, 4)
    mine = me_pair[0] & (parts - 1)
    blocks = [
        dense_call(
            lax.dynamic_index_in_dim(value, mine ^ k, 0, keepdims=False).reshape(height, n_virt)
        )
        for k in range(parts)
    ]
    return [jnp.concatenate([blocks[0], single], axis=0)] + [
        jnp.concatenate([block.astype(BF16), coded], axis=0) for block in blocks[1:]
    ]


def summed(own_ref, arrived):
    total = own_ref[...]
    for ref in arrived:
        total += ref[...].astype(F32)
    return total


def combine_kernel(extra, own_ref, *refs):
    arrived, (total_ref, send_ref) = refs[:-2], refs[-2:]
    total = summed(own_ref, arrived)
    body = total.shape[0] - extra
    scalars = jnp.sum(total[body:], axis=1, keepdims=True)
    scalars = jnp.broadcast_to(scalars, (extra, total.shape[1]))
    lane = lax.broadcasted_iota(jnp.int32, scalars.shape, 1)
    total_ref[:body, :] = total[:body]
    total_ref[body:, :] = jnp.where(lane == 0, scalars, 0.0)
    send_ref[:body, :] = total[:body].astype(BF16)
    send_ref[body:, :] = three_parts(scalars)


def combine(own, arrived, extra):
    return pl.pallas_call(
        functools.partial(combine_kernel, extra),
        out_shape=[
            jax.ShapeDtypeStruct(own.shape, F32),
            jax.ShapeDtypeStruct(own.shape, BF16),
        ],
        in_specs=[VMEM] * (1 + len(arrived)),
        out_specs=[VMEM] * 2,
        compiler_params=SMALL,
    )(own, *arrived)


def outline_kernel(low, cut, me_ref, after_ref, occ_ref, vir_ref, near_ref, half_ref, far_ref, *outs):
    del after_ref
    t_ref, sigma_ref, diag_ref = outs
    n_trial, rows, n_virt = near_ref.shape
    count = half_ref.shape[0]
    mine, top = me_ref[0] & ((1 << low) - 1), me_ref[0] >> low
    far = spread(far_ref[...].astype(F32), count * n_trial * rows, n_virt) if cut else None
    for r in range(t_ref.shape[0]):
        diag = diagonal(occ_ref, vir_ref, (((top ^ r) << low) | mine) * rows, rows)
        diag_ref[r] = diag
        away = r << low
        for m in range(n_trial):
            row = ((away % count) * n_trial + m) * rows
            if r == 0:
                t = near_ref[m]
            elif away < count:
                t = half_ref[away, m].astype(F32)
            elif cut:
                t = far[row : row + rows]
            else:
                t = far_ref[away % count, m].astype(F32)
            t_ref[r, m] = t
            sigma_ref[r, m] = diag * t


def outline(me_pair, after, occ, vir, low, near, half, far):
    n_trial, rows, n_virt = near.shape
    high_count = 2 * half.shape[0] >> low
    blocks = pltpu.VMEM((high_count, n_trial, rows, n_virt), F32)
    return pl.pallas_call(
        functools.partial(outline_kernel, low, rows % 8 == 0),
        out_shape=[blocks, blocks, pltpu.VMEM((high_count, rows, n_virt), F32)],
        in_specs=[SMEM, ANY] + [VMEM] * 5,
        out_specs=[VMEM] * 3,
        compiler_params=SMALL,
        cost_estimate=pl.CostEstimate(
            flops=1 << 20, bytes_accessed=1 << 21, transcendentals=0
        ),
    )(me_pair, after, occ, vir, near, half, far)


def residual_kernel(low, me_ref, t_ref, start_ref, diag_ref, own_ref, *refs):
    arrived, (sigma_ref, precond_ref, square_ref, held_ref) = refs[:-4], refs[-4:]
    high_count, n_trial, rows, n_virt = t_ref.shape
    body = high_count * n_trial * rows
    top = me_ref[0] >> low
    total = summed(own_ref, arrived)
    height = message_shape(body, n_virt, 0)[0]
    held_ref[...] = spread(total[:height], body, n_virt).reshape(held_ref.shape)
    scalars = jnp.sum(total[height:], axis=1, keepdims=True)
    omega = scalars[:n_trial] / (scalars[n_trial:] + 1e-06)
    squares = [jnp.zeros((rows, n_virt), F32) for _ in range(n_trial)]
    for r in range(high_count):
        diag = diag_ref[r]
        block = held_ref[top ^ r]
        for m in range(n_trial):
            level = omega[m : m + 1]
            sigma = start_ref[r, m] + block[m * rows : (m + 1) * rows]
            precond = (sigma - level * t_ref[r, m]) / jnp.maximum(jnp.abs(diag - level), 1.0)
            squares[m] += precond * precond
            if r == 0:
                sigma_ref[m] = sigma
                precond_ref[m] = precond
    sums = [
        jnp.sum(jnp.sum(s, axis=0, keepdims=True), axis=1, keepdims=True) for s in squares
    ]
    square_ref[...] = jnp.concatenate(
        [jnp.broadcast_to(s, (1, square_ref.shape[1])) for s in sums], axis=0
    )


def residual(me_pair, low, outlined, own, arrived):
    high_count, n_trial, rows, n_virt = outlined[0].shape
    block = pltpu.VMEM((n_trial, rows, n_virt), F32)
    return pl.pallas_call(
        functools.partial(residual_kernel, low),
        out_shape=[block, block, pltpu.VMEM((n_trial, 128), F32)],
        in_specs=[SMEM] + [VMEM] * (4 + len(arrived)),
        out_specs=[VMEM] * 3,
        scratch_shapes=[pltpu.VMEM((high_count, n_trial * rows, n_virt), F32)],
        compiler_params=SMALL,
    )(me_pair, *outlined, own, *arrived)


def finish_kernel(count, precond_ref, *refs):
    update_ref = refs[-1]
    square = refs[0][...]
    for ref in refs[1:-1]:
        square += ref[...]
    scale = lax.rsqrt(square[:, :1] / count + 1e-06)
    for m in range(precond_ref.shape[0]):
        update_ref[m] = precond_ref[m] * scale[m : m + 1]


def finish(count, precond, squares):
    return pl.pallas_call(
        functools.partial(finish_kernel, count),
        out_shape=jax.ShapeDtypeStruct(precond.shape, F32),
        in_specs=[VMEM] * (1 + len(squares)),
        out_specs=VMEM,
        compiler_params=SMALL,
    )(precond, *squares)


def fetch_kernel(count, after_ref, *refs):
    del after_ref
    sources, targets, sem = refs[:count], refs[count : 2 * count], refs[-1]
    copies = [
        pltpu.make_async_copy(source.at[pl.ds(0, target.shape[0])], target, sem.at[k])
        for k, (source, target) in enumerate(zip(sources, targets))
    ]
    for copy in copies:
        copy.start()
    for copy in copies:
        copy.wait()


def fetch(after, counts, *arrays):
    return pl.pallas_call(
        functools.partial(fetch_kernel, len(arrays)),
        out_shape=[pltpu.VMEM((n,) + a.shape[1:], a.dtype) for n, a in zip(counts, arrays)],
        in_specs=[ANY] + [HBM] * len(arrays),
        out_specs=[VMEM] * len(arrays),
        scratch_shapes=[pltpu.SemaphoreType.DMA((len(arrays),))],
        compiler_params=SMALL,
        cost_estimate=pl.CostEstimate(
            flops=0, bytes_accessed=sum(4 * a.size for a in arrays), transcendentals=0
        ),
    )(after, *in_hbm(*arrays))


def prepare_kernel(after_ref, early_ref, oo_ref, vv_ref, pair_ref, held_ref, late_ref, sem):
    del after_ref
    first = pltpu.make_async_copy(
        oo_ref.at[pl.ds(early_ref.shape[0], late_ref.shape[0])], late_ref, sem.at[0]
    )
    second = pltpu.make_async_copy(
        vv_ref.at[pl.ds(0, held_ref.shape[0])], held_ref, sem.at[1]
    )
    first.start()
    second.start()
    pair_weights((early_ref, late_ref), pair_ref, first.wait)
    second.wait()


def prepare(after, early_oo, exch_oo, exch_vv):
    n_aux, n_occ, _ = exch_oo.shape
    early = early_oo.shape[0]
    return pl.pallas_call(
        prepare_kernel,
        out_shape=[
            pltpu.VMEM((2, 2, n_aux // 2, n_occ, n_occ), BF16),
            pltpu.VMEM((n_aux // 4 * 2,) + exch_vv.shape[1:], BF16),
        ],
        in_specs=[ANY, VMEM, HBM, HBM],
        out_specs=[VMEM] * 2,
        scratch_shapes=[
            pltpu.VMEM((n_aux - early, n_occ, n_occ), BF16),
            pltpu.SemaphoreType.DMA((2,)),
        ],
        compiler_params=SMALL,
        cost_estimate=pl.CostEstimate(
            flops=0, bytes_accessed=4 * (exch_oo.size + exch_vv.size), transcendentals=0
        ),
    )(after, *in_vmem(early_oo), *in_hbm(exch_oo, exch_vv))


def on_device(size, trial_vecs, occ_energy, vir_energy, coul_ov, exch_oo, exch_vv):
    n_trial, rows, n_virt = trial_vecs.shape
    n_occ = exch_oo.shape[1]
    low, highs = bit_groups(size)
    me = lax.axis_index("aux").astype(jnp.int32)
    top = size.bit_length() - 2
    me_pair = jnp.stack([me, me >> top])
    coul_t = jnp.transpose(coul_ov, (0, 2, 1))
    counts = (trial_vecs.shape[0], 1, 1, exch_oo.shape[0] // EARLY * 2)
    near, occ, vir, early_oo = fetch(
        me_pair, counts, trial_vecs, occ_energy[None], vir_energy[None], exch_oo
    )
    cut = rows % 8 == 0
    held, = pack([near[None]] + [a[None] for a in exchange(trial_vecs, size, 0, 1)])
    pairs, vv = prepare(held, early_oo, exch_oo, exch_vv)
    sent = held
    for at in range(1, top, 2):
        last = cut and at + 2 >= top
        held, *message = pack([held] + exchange(held, size, at, min(2, top - at)), last)
        sent = message[0] if last else held
    far, = exchange(sent, size, top, 1)
    pieces = [held, far] if cut else [in_order(half, me) for half in (held, far)]
    half_sum, more_vv, coul_t = first_half(
        me_pair, pieces[0], pairs, vv, exch_vv, coul_t
    )
    own, *sends = build(
        me_pair, occ, vir, near, half_sum, pieces, coul_t, pairs, (vv, more_vv), low
    )
    outlined = outline(me_pair, own, occ, vir, low, near, held, far)
    arrived = [swap(send, size, k + 1) for k, send in enumerate(sends)]
    for at, width in highs:
        own, send = combine(own, arrived, 2 * n_trial)
        arrived = exchange(send, size, at, width)
    sigma_vecs, precond, square = residual(me_pair, low, outlined, own, arrived)
    squares = [square] + exchange(square, size, 0, low)
    return sigma_vecs, finish(n_occ * n_virt, precond, squares)


def solution(mesh):
    in_specs = (
        P("geom", "aux", None),
        P("geom"),
        P("geom"),
        P(("geom", "aux"), None, None),
        P(("geom", "aux"), None, None),
        P(("geom", "aux"), None, None),
    )
    out_specs = (P("geom", "aux", None), P("geom", "aux", None))
    return jax.shard_map(
        functools.partial(on_device, mesh.shape["aux"]),
        mesh=mesh,
        in_specs=in_specs,
        out_specs=out_specs,
        check_vma=False,
    )
```

```python
import functools

import jax
import jax.numpy as jnp
from jax import lax
from jax.experimental import pallas as pl
from jax.experimental.pallas import tpu as pltpu
from jax.sharding import PartitionSpec as P


F32 = jnp.float32
BF16 = jnp.bfloat16
LOW_BITS = 2
LANES = 128
EARLY = 8
TILE = 16
VMEM = pl.BlockSpec(memory_space=pltpu.VMEM)
SMEM = pl.BlockSpec(memory_space=pltpu.SMEM)
HBM = pl.BlockSpec(memory_space=pltpu.HBM)
ANY = pl.BlockSpec(memory_space=pl.ANY)
SMALL = pltpu.CompilerParams(vmem_limit_bytes=4 << 20)


def bit_groups(size):
    bits = size.bit_length() - 1
    assert size == 1 << bits
    low = min(LOW_BITS, bits)
    return low, [(at, min(LOW_BITS, bits - at)) for at in range(low, bits, LOW_BITS)]


def swap(value, size, offset):
    return lax.ppermute(value, "aux", [(i, i ^ offset) for i in range(size)])


def exchange(value, size, at, width):
    return [swap(value, size, k << at) for k in range(1, 1 << width)]


def dot(a, b):
    return jnp.dot(a, b, preferred_element_type=F32)


def dot_nt(a, b):
    return lax.dot_general(a, b, (((1,), (1,)), ((), ())), preferred_element_type=F32)


def diagonal(occ_ref, vir_ref, first, rows):
    shape = (rows, occ_ref.shape[1])
    wanted = lax.broadcasted_iota(jnp.int32, shape, 0) + first
    picked = jnp.where(lax.broadcasted_iota(jnp.int32, shape, 1) == wanted, occ_ref[...], 0.0)
    return vir_ref[...] - jnp.sum(picked, axis=1, keepdims=True)


def packs(rows, width):
    rest, free = width - LANES, 2 * LANES - width
    if not 0 < rest < LANES or rest % free or rows * free % LANES:
        return 0
    given = rows * free // LANES
    return given if given % 8 == 0 else 0


def dense(value):
    rows, width = value.shape
    given = packs(rows, width)
    if not given:
        return value
    rest, free = width - LANES, 2 * LANES - width
    high = jnp.concatenate([value[:, LANES:], jnp.zeros((rows, free), value.dtype)], axis=1)
    kept, last = high[: rows - given], high[rows - given :]
    moved = [
        pltpu.roll(last, (rest - g * free) % LANES, 1) for g in range(rest // free)
    ]
    lane = lax.broadcasted_iota(jnp.int32, kept.shape, 1)
    kept = jnp.where(lane < rest, kept, jnp.concatenate(moved, axis=0))
    return jnp.concatenate([value[:, :LANES], kept], axis=0)


def spread(value, rows, width):
    given = packs(rows, width)
    if not given:
        return value
    rest, free = width - LANES, 2 * LANES - width
    kept = value[rows:]
    last = jnp.zeros((given, LANES), value.dtype)
    lane = lax.broadcasted_iota(jnp.int32, last.shape, 1)
    for g in range(rest // free):
        back = pltpu.roll(kept[g * given : (g + 1) * given], (LANES - rest + g * free) % LANES, 1)
        last = jnp.where((lane >= g * free) & (lane < (g + 1) * free), back, last)
    high = jnp.concatenate([kept, last], axis=0)
    return jnp.concatenate([value[:rows], high[:, :rest]], axis=1)


def message_shape(rows, width, extra):
    if packs(rows, width):
        return rows * width // LANES + extra, LANES
    return rows + extra, width


def three_parts(value):
    high = value.astype(BF16).astype(F32)
    middle = (value - high).astype(BF16).astype(F32)
    rest = value - high - middle
    lane = lax.broadcasted_iota(jnp.int32, value.shape, 1)
    return jnp.where(
        lane == 0, high, jnp.where(lane == 1, middle, jnp.where(lane == 2, rest, 0.0))
    ).astype(BF16)


def coulomb_stages(acc_ref, x, ov_ref):
    n_aux, n_virt, n_occ = ov_ref.shape
    n_trial = x.shape[0]
    tiles = n_virt // TILE
    unit = (
        lax.broadcasted_iota(jnp.int32, (n_virt, n_virt), 0)
        == lax.broadcasted_iota(jnp.int32, (n_virt, n_virt), 1)
    ).astype(BF16)
    x_t = jnp.stack([dot_nt(unit, x[m]).astype(BF16) for m in range(n_trial)], 0)
    rows, cols = n_trial * TILE, n_aux * TILE

    def x_tile(t):
        return x_t[:, t * TILE : (t + 1) * TILE, :].reshape(rows, n_occ)

    def ov_tile(t):
        return ov_ref[:, t * TILE : (t + 1) * TILE, :].reshape(cols, n_occ)

    def first():
        total = jnp.zeros((rows, cols), F32)
        for t in range(0, tiles, 2):
            span = range(t, min(t + 2, tiles))
            total += dot_nt(
                jnp.concatenate([x_tile(u) for u in span], axis=1),
                jnp.concatenate([ov_tile(u) for u in span], axis=1),
            )
        return total

    def middle(total):
        same = (
            lax.broadcasted_iota(jnp.int32, (rows, cols), 0) % TILE
            == lax.broadcasted_iota(jnp.int32, (rows, cols), 1) % TILE
        )
        coef = jnp.sum(jnp.where(same, total, 0.0).reshape(n_trial, TILE, cols), axis=1)
        lane = lax.broadcasted_iota(jnp.int32, coef.shape, 1)
        step = 1
        while step < TILE:
            coef += jnp.where(
                (lane & step) != 0, pltpu.roll(coef, step, 1), pltpu.roll(coef, cols - step, 1)
            )
            step *= 2
        twice = 2.0 * coef.astype(BF16).astype(F32)
        repeated = jnp.broadcast_to(twice[:, None, :], (n_trial, TILE, cols))
        return jnp.where(same, repeated.reshape(rows, cols), 0.0).astype(BF16)

    def last(weights):
        for t in range(0, tiles, 2):
            span = range(t, min(t + 2, tiles))
            sums = dot(weights, jnp.concatenate([ov_tile(u) for u in span], axis=1))
            for k, u in enumerate(span):
                acc_ref[:, u * TILE : (u + 1) * TILE, :] -= sums[
                    :, k * n_occ : (k + 1) * n_occ
                ].reshape(n_trial, TILE, n_occ)

    return first, middle, last


def pair_weights(oo_refs, pair_ref, ready):
    n_occ = oo_refs[0].shape[1]
    half = n_occ // 2
    left = lax.broadcasted_iota(jnp.int32, (n_occ, n_occ), 1) < half
    at = 0
    for part, oo_ref in enumerate(oo_refs):
        if part == 1:
            ready()
        for g in range(oo_ref.shape[0] // 2):
            straight = [oo_ref[2 * g + odd].astype(F32) for odd in range(2)]
            moved = [pltpu.roll(value, half, 1) for value in straight]
            for odd in range(2):
                low = jnp.where(left, straight[odd], moved[1 - odd])
                high = jnp.where(left, moved[odd], straight[1 - odd])
                pair_ref[0, odd, at] = low.astype(BF16)
                pair_ref[1, odd, at] = high.astype(BF16)
            at += 1


def half_stages(x, pair_ref, k, vv_refs, acc_ref, mid_ref):
    n_trial, half, n_virt = x.shape
    n_occ = 2 * half
    width = n_trial * half
    orders = [
        jnp.concatenate([x[m ^ odd] for m in range(n_trial)], axis=0) for odd in range(2)
    ]
    starts = [0]
    for vv_ref in vv_refs:
        starts.append(starts[-1] + vv_ref.shape[0] // 2)

    def transform(part):
        vv_ref, pairs = vv_refs[part], starts[part + 1] - starts[part]
        even, odd = (
            dot_nt(
                jnp.concatenate([vv_ref[2 * g + odd] for g in range(pairs)], axis=0),
                orders[odd],
            )
            for odd in range(2)
        )
        left = lax.broadcasted_iota(jnp.int32, even.shape, 1) % n_occ < half
        shape, span = (pairs, n_virt, width), pl.ds(starts[part], pairs)
        mid_ref[0, span] = jnp.where(left, even, odd).astype(BF16).reshape(shape)
        mid_ref[1, span] = jnp.where(left, odd, even).astype(BF16).reshape(shape)

    def gather_up(first, last):
        for odd in range(2):
            weights = jnp.concatenate(
                [pair_ref[k, odd, g] for g in range(first, last)], axis=1
            )
            for q in range(n_trial // 2):
                at = slice(q * n_occ, (q + 1) * n_occ)
                lines = jnp.concatenate(
                    [mid_ref[odd, g, :, at] for g in range(first, last)], axis=1
                )
                acc_ref[2 * q + odd] += dot_nt(lines, weights)

    return transform, gather_up, starts


def place(target_ref, pieces_ref, first, mask, rows):
    for d in range(pieces_ref.shape[0]):
        at = pl.multiple_of(((first ^ d) & mask) * rows, rows)
        for m in range(pieces_ref.shape[1]):
            target_ref[m, pl.ds(at, rows), :] = pieces_ref[d, m].astype(F32)


def place_rows(target_ref, value, first, mask, rows):
    n_trial = target_ref.shape[0]
    for d in range(value.shape[0] // (n_trial * rows)):
        at = pl.multiple_of(((first ^ d) & mask) * rows, rows)
        for m in range(n_trial):
            row = (d * n_trial + m) * rows
            target_ref[m, pl.ds(at, rows), :] = value[row : row + rows]


def half_kernel(cut, me_ref, half_ref, pair_ref, vv_ref, more_ref, ov_ref, *refs):
    acc_ref, rest_ref, held_ov_ref, xs_ref, mid_ref, sem = refs
    copies = [
        pltpu.make_async_copy(
            more_ref.at[pl.ds(vv_ref.shape[0], rest_ref.shape[0])], rest_ref, sem.at[0]
        ),
        pltpu.make_async_copy(ov_ref, held_ov_ref, sem.at[1]),
    ]
    copies[0].start()

    if cut:
        place(xs_ref, half_ref, me_ref[0], half_ref.shape[0] - 1, half_ref.shape[2])
    else:
        xs_ref[...] = half_ref[...].astype(F32)
    acc_ref[...] = jnp.zeros_like(acc_ref)
    x = xs_ref[...].astype(BF16)
    transform, gather_up, starts = half_stages(
        x, pair_ref, me_ref[1], (vv_ref, rest_ref), acc_ref, mid_ref
    )
    transform(0)
    gather_up(starts[0], starts[1])
    copies[0].wait()
    copies[1].start()
    transform(1)
    gather_up(starts[1], starts[2])
    copies[1].wait()


def build_kernel(low, cut, me_ref, occ_ref, vir_ref, own_ref, held_ref, *refs):
    parts = 1 << low
    pieces, (ov_ref, pair_ref, *vv_refs), outs = refs[:2], refs[2:6], refs[6:-3]
    xs_ref, mid_ref, acc_ref = refs[-3:]
    n_trial, rows, n_virt = own_ref.shape
    n_occ = ov_ref.shape[2]
    size, half = n_occ // rows, n_occ // 2
    high_count = size >> low
    me, other = me_ref[0], 1 - me_ref[1]
    mine = me & (parts - 1)
    if cut:
        place(xs_ref, pieces[0], me, size - 1, rows)
        far = spread(pieces[1][...].astype(F32), half * n_trial, n_virt)
        place_rows(xs_ref, far, me ^ (size // 2), size - 1, rows)
    else:
        for k, piece in enumerate(pieces):
            at = pl.multiple_of((me_ref[1] ^ k) * half, half)
            for m in range(n_trial):
                xs_ref[m, pl.ds(at, half), :] = piece[m].astype(F32)
    x = xs_ref[...].astype(BF16)
    acc_ref[...] = held_ref[...]
    rest = pl.ds(pl.multiple_of(other * half, half), half)
    x_rest = jnp.stack([xs_ref[m, rest, :] for m in range(n_trial)], 0).astype(BF16)
    first, middle, last = coulomb_stages(acc_ref, x, ov_ref)
    transform, gather_up, starts = half_stages(
        x_rest, pair_ref, other, vv_refs, acc_ref, mid_ref
    )
    total = first()
    transform(0)
    weights = middle(total)
    transform(1)
    last(weights)
    gather_up(0, starts[-1])
    unit = (
        lax.broadcasted_iota(jnp.int32, (n_occ, n_occ), 0)
        == lax.broadcasted_iota(jnp.int32, (n_occ, n_occ), 1)
    ).astype(BF16)
    lines = []
    for m in range(n_trial):
        value = -dot_nt(unit, acc_ref[m].astype(BF16))
        seen = xs_ref[m]
        lines.append(jnp.sum(jnp.sum(seen * value, axis=0, keepdims=True), axis=1, keepdims=True))
        xs_ref[m] = value
    own = own_ref[...]
    square = own * own
    diag = diagonal(occ_ref, vir_ref, me * rows, rows)
    for m in range(n_trial):
        lines[m] += jnp.sum(
            jnp.sum(square[m] * diag, axis=0, keepdims=True), axis=1, keepdims=True
        )
    for m in range(n_trial):
        lines.append(
            jnp.sum(jnp.sum(square[m], axis=0, keepdims=True), axis=1, keepdims=True)
        )
    body = high_count * n_trial * rows
    height, wide = message_shape(body, n_virt, 0)
    scalars = jnp.concatenate([jnp.broadcast_to(line, (1, wide)) for line in lines], axis=0)
    single = jnp.where(
        lax.broadcasted_iota(jnp.int32, scalars.shape, 1) == 0, scalars, 0.0
    )
    coded = three_parts(scalars)
    if not cut:
        for ref, value in zip(outs, (xs_ref[...], single, coded)):
            ref[...] = value
        return
    outs[0][height:, :] = single
    for k in range(parts):
        blocks = []
        for z in range(high_count):
            at = pl.multiple_of(((z << low) | (mine ^ k)) * rows, rows)
            blocks += [xs_ref[m, pl.ds(at, rows), :] for m in range(n_trial)]
        whole = dense(jnp.concatenate(blocks, axis=0))
        if k == 0:
            outs[0][:height, :] = whole
        else:
            outs[k][:height, :] = whole.astype(BF16)
            outs[k][height:, :] = coded


def pack_kernel(count, *refs):
    target_ref, at, rows = refs[count], 0, []
    for ref in refs[:count]:
        value = ref[...].astype(F32)
        target_ref[at : at + ref.shape[0]] = value.astype(BF16)
        at += ref.shape[0]
        rows.append(value.reshape(-1, ref.shape[-1]) if refs[count + 1 :] else None)
    for ref in refs[count + 1 :]:
        ref[...] = dense(jnp.concatenate(rows, axis=0)).astype(BF16)


def pack(arrays, message=False):
    shape = (sum(a.shape[0] for a in arrays),) + arrays[0].shape[1:]
    shapes = [shape]
    if message:
        shapes.append(message_shape(shape[0] * shape[1] * shape[2], shape[3], 0))
    return pl.pallas_call(
        functools.partial(pack_kernel, len(arrays)),
        out_shape=[jax.ShapeDtypeStruct(one, BF16) for one in shapes],
        in_specs=[VMEM] * len(arrays),
        out_specs=[VMEM] * len(shapes),
        compiler_params=SMALL,
    )(*arrays)


def in_vmem(*arrays):
    return [pltpu.with_memory_space_constraint(a, pltpu.VMEM) for a in arrays]


def in_order(half, me):
    count, n_trial, rows, n_virt = half.shape
    order = (me & (count - 1)) ^ jnp.arange(count)
    return half[order].transpose(1, 0, 2, 3).reshape(n_trial, count * rows, n_virt)


def in_hbm(*arrays):
    return [pltpu.with_memory_space_constraint(a, pltpu.HBM) for a in arrays]


def first_half(me_pair, half, pairs, exch_vv, more_vv, coul_t):
    cut = half.ndim == 4
    n_aux, n_virt, n_occ = coul_t.shape
    n_trial = half.shape[1] if cut else half.shape[0]
    flops = n_aux * n_trial * n_occ * n_virt * (n_virt + n_occ)
    return pl.pallas_call(
        functools.partial(half_kernel, cut),
        out_shape=[
            pltpu.VMEM((n_trial, n_virt, n_occ), F32),
            pltpu.VMEM((n_aux - exch_vv.shape[0], n_virt, n_virt), BF16),
            pltpu.VMEM(coul_t.shape, BF16),
        ],
        in_specs=[SMEM] + [VMEM] * 3 + [HBM] * 2,
        out_specs=[VMEM] * 3,
        scratch_shapes=[
            pltpu.VMEM((n_trial, n_occ // 2, n_virt), F32),
            pltpu.VMEM((2, n_aux // 2, n_virt, n_trial * n_occ // 2), BF16),
            pltpu.SemaphoreType.DMA((2,)),
        ],
        compiler_params=pltpu.CompilerParams(vmem_limit_bytes=32 << 20),
        cost_estimate=pl.CostEstimate(
            flops=flops, bytes_accessed=2 * (exch_vv.size + coul_t.size), transcendentals=0
        ),
    )(me_pair, half, *in_vmem(pairs, exch_vv), *in_hbm(more_vv, coul_t))


def dense_call(value):
    def kernel(value_ref, out_ref):
        out_ref[...] = dense(value_ref[...])

    return pl.pallas_call(
        kernel,
        out_shape=jax.ShapeDtypeStruct(message_shape(*value.shape, 0), value.dtype),
        in_specs=[VMEM],
        out_specs=VMEM,
        compiler_params=SMALL,
    )(value)


def build(me_pair, occ, vir, own, held, pieces, coul_t, pairs, exch_vv, low):
    parts = 1 << low
    n_trial, rows, n_virt = own.shape
    n_aux, _, n_occ = coul_t.shape
    high_count = n_occ // rows >> low
    cut = rows % 8 == 0
    height, extra = high_count * n_trial * rows, 2 * n_trial
    shape = message_shape(height, n_virt, extra)
    if cut:
        shapes = [jax.ShapeDtypeStruct(shape, F32)]
        shapes += [jax.ShapeDtypeStruct(shape, BF16)] * (parts - 1)
    else:
        shapes = [
            jax.ShapeDtypeStruct((n_trial, n_occ, n_virt), F32),
            jax.ShapeDtypeStruct((extra, shape[1]), F32),
            jax.ShapeDtypeStruct((extra, shape[1]), BF16),
        ]
    flops = n_aux * n_trial * n_occ * n_virt * (n_virt + n_occ)
    moved = 2 * (coul_t.size + pairs.size + sum(a.size for a in exch_vv))
    results = pl.pallas_call(
        functools.partial(build_kernel, low, cut),
        out_shape=shapes,
        in_specs=[SMEM] + [VMEM] * 10,
        out_specs=[VMEM] * len(shapes),
        scratch_shapes=[
            pltpu.VMEM((n_trial, n_occ, n_virt), F32),
            pltpu.VMEM((2, n_aux // 2, n_virt, n_trial * n_occ // 2), BF16),
            pltpu.VMEM((n_trial, n_virt, n_occ), F32),
        ],
        compiler_params=pltpu.CompilerParams(vmem_limit_bytes=32 << 20),
        cost_estimate=pl.CostEstimate(flops=flops, bytes_accessed=moved, transcendentals=0),
    )(me_pair, occ, vir, own, *in_vmem(held), *pieces, *in_vmem(coul_t, pairs, *exch_vv))
    if cut:
        return results
    value, single, coded = results
    value = value.reshape(n_trial, high_count, parts, rows, n_virt).transpose(2, 1, 0, 3, 4)
    mine = me_pair[0] & (parts - 1)
    blocks = [
        dense_call(
            lax.dynamic_index_in_dim(value, mine ^ k, 0, keepdims=False).reshape(height, n_virt)
        )
        for k in range(parts)
    ]
    return [jnp.concatenate([blocks[0], single], axis=0)] + [
        jnp.concatenate([block.astype(BF16), coded], axis=0) for block in blocks[1:]
    ]


def summed(own_ref, arrived):
    total = own_ref[...]
    for ref in arrived:
        total += ref[...].astype(F32)
    return total


def combine_kernel(extra, own_ref, *refs):
    arrived, (total_ref, send_ref) = refs[:-2], refs[-2:]
    total = summed(own_ref, arrived)
    body = total.shape[0] - extra
    scalars = jnp.sum(total[body:], axis=1, keepdims=True)
    scalars = jnp.broadcast_to(scalars, (extra, total.shape[1]))
    lane = lax.broadcasted_iota(jnp.int32, scalars.shape, 1)
    total_ref[:body, :] = total[:body]
    total_ref[body:, :] = jnp.where(lane == 0, scalars, 0.0)
    send_ref[:body, :] = total[:body].astype(BF16)
    send_ref[body:, :] = three_parts(scalars)


def combine(own, arrived, extra):
    return pl.pallas_call(
        functools.partial(combine_kernel, extra),
        out_shape=[
            jax.ShapeDtypeStruct(own.shape, F32),
            jax.ShapeDtypeStruct(own.shape, BF16),
        ],
        in_specs=[VMEM] * (1 + len(arrived)),
        out_specs=[VMEM] * 2,
        compiler_params=SMALL,
    )(own, *arrived)


def outline_kernel(low, cut, me_ref, after_ref, occ_ref, vir_ref, near_ref, half_ref, far_ref, *outs):
    del after_ref
    t_ref, sigma_ref, diag_ref = outs
    n_trial, rows, n_virt = near_ref.shape
    count = half_ref.shape[0]
    mine, top = me_ref[0] & ((1 << low) - 1), me_ref[0] >> low
    far = spread(far_ref[...].astype(F32), count * n_trial * rows, n_virt) if cut else None
    for r in range(t_ref.shape[0]):
        diag = diagonal(occ_ref, vir_ref, (((top ^ r) << low) | mine) * rows, rows)
        diag_ref[r] = diag
        away = r << low
        for m in range(n_trial):
            row = ((away % count) * n_trial + m) * rows
            if r == 0:
                t = near_ref[m]
            elif away < count:
                t = half_ref[away, m].astype(F32)
            elif cut:
                t = far[row : row + rows]
            else:
                t = far_ref[away % count, m].astype(F32)
            t_ref[r, m] = t
            sigma_ref[r, m] = diag * t


def outline(me_pair, after, occ, vir, low, near, half, far):
    n_trial, rows, n_virt = near.shape
    high_count = 2 * half.shape[0] >> low
    blocks = pltpu.VMEM((high_count, n_trial, rows, n_virt), F32)
    return pl.pallas_call(
        functools.partial(outline_kernel, low, rows % 8 == 0),
        out_shape=[blocks, blocks, pltpu.VMEM((high_count, rows, n_virt), F32)],
        in_specs=[SMEM, ANY] + [VMEM] * 5,
        out_specs=[VMEM] * 3,
        compiler_params=SMALL,
        cost_estimate=pl.CostEstimate(
            flops=1 << 20, bytes_accessed=1 << 21, transcendentals=0
        ),
    )(me_pair, after, occ, vir, near, half, far)


def residual_kernel(low, me_ref, t_ref, start_ref, diag_ref, own_ref, *refs):
    arrived, (sigma_ref, precond_ref, square_ref, held_ref) = refs[:-4], refs[-4:]
    high_count, n_trial, rows, n_virt = t_ref.shape
    body = high_count * n_trial * rows
    top = me_ref[0] >> low
    total = summed(own_ref, arrived)
    height = message_shape(body, n_virt, 0)[0]
    held_ref[...] = spread(total[:height], body, n_virt).reshape(held_ref.shape)
    scalars = jnp.sum(total[height:], axis=1, keepdims=True)
    omega = scalars[:n_trial] / (scalars[n_trial:] + 1e-06)
    squares = [jnp.zeros((rows, n_virt), F32) for _ in range(n_trial)]
    for r in range(high_count):
        diag = diag_ref[r]
        block = held_ref[top ^ r]
        for m in range(n_trial):
            level = omega[m : m + 1]
            sigma = start_ref[r, m] + block[m * rows : (m + 1) * rows]
            precond = (sigma - level * t_ref[r, m]) / jnp.maximum(jnp.abs(diag - level), 1.0)
            squares[m] += precond * precond
            if r == 0:
                sigma_ref[m] = sigma
                precond_ref[m] = precond
    sums = [
        jnp.sum(jnp.sum(s, axis=0, keepdims=True), axis=1, keepdims=True) for s in squares
    ]
    square_ref[...] = jnp.concatenate(
        [jnp.broadcast_to(s, (1, square_ref.shape[1])) for s in sums], axis=0
    )


def residual(me_pair, low, outlined, own, arrived):
    high_count, n_trial, rows, n_virt = outlined[0].shape
    block = pltpu.VMEM((n_trial, rows, n_virt), F32)
    return pl.pallas_call(
        functools.partial(residual_kernel, low),
        out_shape=[block, block, pltpu.VMEM((n_trial, 128), F32)],
        in_specs=[SMEM] + [VMEM] * (4 + len(arrived)),
        out_specs=[VMEM] * 3,
        scratch_shapes=[pltpu.VMEM((high_count, n_trial * rows, n_virt), F32)],
        compiler_params=SMALL,
    )(me_pair, *outlined, own, *arrived)


def finish_kernel(count, precond_ref, *refs):
    update_ref = refs[-1]
    square = refs[0][...]
    for ref in refs[1:-1]:
        square += ref[...]
    scale = lax.rsqrt(square[:, :1] / count + 1e-06)
    for m in range(precond_ref.shape[0]):
        update_ref[m] = precond_ref[m] * scale[m : m + 1]


def finish(count, precond, squares):
    return pl.pallas_call(
        functools.partial(finish_kernel, count),
        out_shape=jax.ShapeDtypeStruct(precond.shape, F32),
        in_specs=[VMEM] * (1 + len(squares)),
        out_specs=VMEM,
        compiler_params=SMALL,
    )(precond, *squares)


def fetch_kernel(count, after_ref, *refs):
    del after_ref
    sources, targets, sem = refs[:count], refs[count : 2 * count], refs[-1]
    copies = [
        pltpu.make_async_copy(source.at[pl.ds(0, target.shape[0])], target, sem.at[k])
        for k, (source, target) in enumerate(zip(sources, targets))
    ]
    for copy in copies:
        copy.start()
    for copy in copies:
        copy.wait()


def fetch(after, counts, *arrays):
    return pl.pallas_call(
        functools.partial(fetch_kernel, len(arrays)),
        out_shape=[pltpu.VMEM((n,) + a.shape[1:], a.dtype) for n, a in zip(counts, arrays)],
        in_specs=[ANY] + [HBM] * len(arrays),
        out_specs=[VMEM] * len(arrays),
        scratch_shapes=[pltpu.SemaphoreType.DMA((len(arrays),))],
        compiler_params=SMALL,
        cost_estimate=pl.CostEstimate(
            flops=0, bytes_accessed=sum(4 * a.size for a in arrays), transcendentals=0
        ),
    )(after, *in_hbm(*arrays))


def prepare_kernel(after_ref, early_ref, oo_ref, vv_ref, pair_ref, held_ref, late_ref, sem):
    del after_ref
    first = pltpu.make_async_copy(
        oo_ref.at[pl.ds(early_ref.shape[0], late_ref.shape[0])], late_ref, sem.at[0]
    )
    second = pltpu.make_async_copy(
        vv_ref.at[pl.ds(0, held_ref.shape[0])], held_ref, sem.at[1]
    )
    first.start()
    second.start()
    pair_weights((early_ref, late_ref), pair_ref, first.wait)
    second.wait()


def prepare(after, early_oo, exch_oo, exch_vv):
    n_aux, n_occ, _ = exch_oo.shape
    early = early_oo.shape[0]
    return pl.pallas_call(
        prepare_kernel,
        out_shape=[
            pltpu.VMEM((2, 2, n_aux // 2, n_occ, n_occ), BF16),
            pltpu.VMEM((n_aux // 4 * 2,) + exch_vv.shape[1:], BF16),
        ],
        in_specs=[ANY, VMEM, HBM, HBM],
        out_specs=[VMEM] * 2,
        scratch_shapes=[
            pltpu.VMEM((n_aux - early, n_occ, n_occ), BF16),
            pltpu.SemaphoreType.DMA((2,)),
        ],
        compiler_params=SMALL,
        cost_estimate=pl.CostEstimate(
            flops=0, bytes_accessed=4 * (exch_oo.size + exch_vv.size), transcendentals=0
        ),
    )(after, *in_vmem(early_oo), *in_hbm(exch_oo, exch_vv))


def on_device(size, trial_vecs, occ_energy, vir_energy, coul_ov, exch_oo, exch_vv):
    n_trial, rows, n_virt = trial_vecs.shape
    n_occ = exch_oo.shape[1]
    low, highs = bit_groups(size)
    me = lax.axis_index("aux").astype(jnp.int32)
    top = size.bit_length() - 2
    me_pair = jnp.stack([me, me >> top])
    coul_t = jnp.transpose(coul_ov, (0, 2, 1))
    counts = (trial_vecs.shape[0], 1, 1, exch_oo.shape[0] // EARLY * 2)
    near, occ, vir, early_oo = fetch(
        me_pair, counts, trial_vecs, occ_energy[None], vir_energy[None], exch_oo
    )
    cut = rows % 8 == 0
    held, = pack([near[None]] + [a[None] for a in exchange(trial_vecs, size, 0, 1)])
    pairs, vv = prepare(held, early_oo, exch_oo, exch_vv)
    sent = held
    for at in range(1, top, 2):
        last = cut and at + 2 >= top
        held, *message = pack([held] + exchange(held, size, at, min(2, top - at)), last)
        sent = message[0] if last else held
    far, = exchange(sent, size, top, 1)
    pieces = [held, far] if cut else [in_order(half, me) for half in (held, far)]
    half_sum, more_vv, coul_t = first_half(
        me_pair, pieces[0], pairs, vv, exch_vv, coul_t
    )
    own, *sends = build(
        me_pair, occ, vir, near, half_sum, pieces, coul_t, pairs, (vv, more_vv), low
    )
    outlined = outline(me_pair, own, occ, vir, low, near, held, far)
    arrived = [swap(send, size, k + 1) for k, send in enumerate(sends)]
    for at, width in highs:
        own, send = combine(own, arrived, 2 * n_trial)
        arrived = exchange(send, size, at, width)
    sigma_vecs, precond, square = residual(me_pair, low, outlined, own, arrived)
    squares = [square] + exchange(square, size, 0, low)
    return sigma_vecs, finish(n_occ * n_virt, precond, squares)


def solution(mesh):
    in_specs = (
        P("geom", "aux", None),
        P("geom"),
        P("geom"),
        P(("geom", "aux"), None, None),
        P(("geom", "aux"), None, None),
        P(("geom", "aux"), None, None),
    )
    out_specs = (P("geom", "aux", None), P("geom", "aux", None))
    return jax.shard_map(
        functools.partial(on_device, mesh.shape["aux"]),
        mesh=mesh,
        in_specs=in_specs,
        out_specs=out_specs,
        check_vma=False,
    )
```

```python
import functools

import jax
import jax.numpy as jnp
from jax import lax
from jax.experimental import pallas as pl
from jax.experimental.pallas import tpu as pltpu
from jax.sharding import PartitionSpec as P


F32 = jnp.float32
BF16 = jnp.bfloat16
LOW_BITS = 2
LANES = 128
EARLY = 8
TILE = 16
VMEM = pl.BlockSpec(memory_space=pltpu.VMEM)
HBM = pl.BlockSpec(memory_space=pltpu.HBM)
ANY = pl.BlockSpec(memory_space=pl.ANY)
SMALL = pltpu.CompilerParams(vmem_limit_bytes=4 << 20)


def bit_groups(size):
    bits = size.bit_length() - 1
    assert size == 1 << bits
    low = min(LOW_BITS, bits)
    return low, [(at, min(LOW_BITS, bits - at)) for at in range(low, bits, LOW_BITS)]


def swap(value, size, offset):
    return lax.ppermute(value, "aux", [(i, i ^ offset) for i in range(size)])


def exchange(value, size, at, width):
    return [swap(value, size, k << at) for k in range(1, 1 << width)]


def dot(a, b):
    return jnp.dot(a, b, preferred_element_type=F32)


def dot_nt(a, b):
    return lax.dot_general(a, b, (((1,), (1,)), ((), ())), preferred_element_type=F32)


def diagonal(occ_ref, vir_ref, first, rows):
    shape = (rows, occ_ref.shape[1])
    wanted = lax.broadcasted_iota(jnp.int32, shape, 0) + first
    picked = jnp.where(lax.broadcasted_iota(jnp.int32, shape, 1) == wanted, occ_ref[...], 0.0)
    return vir_ref[...] - jnp.sum(picked, axis=1, keepdims=True)


def packs(rows, width):
    rest, free = width - LANES, 2 * LANES - width
    if not 0 < rest < LANES or rest % free or rows * free % LANES:
        return 0
    given = rows * free // LANES
    return given if given % 8 == 0 else 0


def dense(value):
    rows, width = value.shape
    given = packs(rows, width)
    if not given:
        return value
    rest, free = width - LANES, 2 * LANES - width
    high = jnp.concatenate([value[:, LANES:], jnp.zeros((rows, free), value.dtype)], axis=1)
    kept, last = high[: rows - given], high[rows - given :]
    moved = [
        pltpu.roll(last, (rest - g * free) % LANES, 1) for g in range(rest // free)
    ]
    lane = lax.broadcasted_iota(jnp.int32, kept.shape, 1)
    kept = jnp.where(lane < rest, kept, jnp.concatenate(moved, axis=0))
    return jnp.concatenate([value[:, :LANES], kept], axis=0)


def spread(value, rows, width):
    given = packs(rows, width)
    if not given:
        return value
    rest, free = width - LANES, 2 * LANES - width
    kept = value[rows:]
    last = jnp.zeros((given, LANES), value.dtype)
    lane = lax.broadcasted_iota(jnp.int32, last.shape, 1)
    for g in range(rest // free):
        back = pltpu.roll(kept[g * given : (g + 1) * given], (LANES - rest + g * free) % LANES, 1)
        last = jnp.where((lane >= g * free) & (lane < (g + 1) * free), back, last)
    high = jnp.concatenate([kept, last], axis=0)
    return jnp.concatenate([value[:rows], high[:, :rest]], axis=1)


def message_shape(rows, width, extra):
    if packs(rows, width):
        return rows * width // LANES + extra, LANES
    return rows + extra, width


def three_parts(value):
    high = value.astype(BF16).astype(F32)
    middle = (value - high).astype(BF16).astype(F32)
    rest = value - high - middle
    lane = lax.broadcasted_iota(jnp.int32, value.shape, 1)
    return jnp.where(
        lane == 0, high, jnp.where(lane == 1, middle, jnp.where(lane == 2, rest, 0.0))
    ).astype(BF16)


def coulomb_stages(acc_ref, x, ov_ref):
    n_aux, n_virt, n_occ = ov_ref.shape
    n_trial = x.shape[0]
    tiles = n_virt // TILE
    unit = (
        lax.broadcasted_iota(jnp.int32, (n_virt, n_virt), 0)
        == lax.broadcasted_iota(jnp.int32, (n_virt, n_virt), 1)
    ).astype(BF16)
    x_t = jnp.stack([dot_nt(unit, x[m]).astype(BF16) for m in range(n_trial)], 0)
    rows, cols = n_trial * TILE, n_aux * TILE

    def x_tile(t):
        return x_t[:, t * TILE : (t + 1) * TILE, :].reshape(rows, n_occ)

    def ov_tile(t):
        return ov_ref[:, t * TILE : (t + 1) * TILE, :].reshape(cols, n_occ)

    def first():
        total = jnp.zeros((rows, cols), F32)
        for t in range(0, tiles, 2):
            span = range(t, min(t + 2, tiles))
            total += dot_nt(
                jnp.concatenate([x_tile(u) for u in span], axis=1),
                jnp.concatenate([ov_tile(u) for u in span], axis=1),
            )
        return total

    def middle(total):
        same = (
            lax.broadcasted_iota(jnp.int32, (rows, cols), 0) % TILE
            == lax.broadcasted_iota(jnp.int32, (rows, cols), 1) % TILE
        )
        coef = jnp.sum(jnp.where(same, total, 0.0).reshape(n_trial, TILE, cols), axis=1)
        lane = lax.broadcasted_iota(jnp.int32, coef.shape, 1)
        step = 1
        while step < TILE:
            coef += jnp.where(
                (lane & step) != 0, pltpu.roll(coef, step, 1), pltpu.roll(coef, cols - step, 1)
            )
            step *= 2
        twice = 2.0 * coef.astype(BF16).astype(F32)
        repeated = jnp.broadcast_to(twice[:, None, :], (n_trial, TILE, cols))
        return jnp.where(same, repeated.reshape(rows, cols), 0.0).astype(BF16)

    def last(weights):
        for t in range(0, tiles, 2):
            span = range(t, min(t + 2, tiles))
            sums = dot(weights, jnp.concatenate([ov_tile(u) for u in span], axis=1))
            for k, u in enumerate(span):
                acc_ref[:, u * TILE : (u + 1) * TILE, :] -= sums[
                    :, k * n_occ : (k + 1) * n_occ
                ].reshape(n_trial, TILE, n_occ)

    return first, middle, last


def pair_weights(oo_refs, pair_ref, ready):
    n_occ = oo_refs[0].shape[1]
    half = n_occ // 2
    left = lax.broadcasted_iota(jnp.int32, (n_occ, n_occ), 1) < half
    at = 0
    for part, oo_ref in enumerate(oo_refs):
        if part == 1:
            ready()
        for g in range(oo_ref.shape[0] // 2):
            straight = [oo_ref[2 * g + odd].astype(F32) for odd in range(2)]
            moved = [pltpu.roll(value, half, 1) for value in straight]
            for odd in range(2):
                low = jnp.where(left, straight[odd], moved[1 - odd])
                high = jnp.where(left, moved[odd], straight[1 - odd])
                pair_ref[0, odd, at] = low.astype(BF16)
                pair_ref[1, odd, at] = high.astype(BF16)
            at += 1


def half_stages(x, pair_ref, k, vv_refs, acc_ref, mid_ref):
    n_trial, half, n_virt = x.shape
    n_occ = 2 * half
    width = n_trial * half
    orders = [
        jnp.concatenate([x[m ^ odd] for m in range(n_trial)], axis=0) for odd in range(2)
    ]
    starts = [0]
    for vv_ref in vv_refs:
        starts.append(starts[-1] + vv_ref.shape[0] // 2)

    def transform(part):
        vv_ref, pairs = vv_refs[part], starts[part + 1] - starts[part]
        even, odd = (
            dot_nt(
                jnp.concatenate([vv_ref[2 * g + odd] for g in range(pairs)], axis=0),
                orders[odd],
            )
            for odd in range(2)
        )
        left = lax.broadcasted_iota(jnp.int32, even.shape, 1) % n_occ < half
        shape, span = (pairs, n_virt, width), pl.ds(starts[part], pairs)
        mid_ref[0, span] = jnp.where(left, even, odd).astype(BF16).reshape(shape)
        mid_ref[1, span] = jnp.where(left, odd, even).astype(BF16).reshape(shape)

    def gather_up(first, last):
        for odd in range(2):
            weights = jnp.concatenate(
                [pair_ref[k, odd, g] for g in range(first, last)], axis=1
            )
            for q in range(n_trial // 2):
                at = slice(q * n_occ, (q + 1) * n_occ)
                lines = jnp.concatenate(
                    [mid_ref[odd, g, :, at] for g in range(first, last)], axis=1
                )
                acc_ref[2 * q + odd] += dot_nt(lines, weights)

    return transform, gather_up, starts


def place(target_ref, pieces_ref, first, mask, rows):
    for d in range(pieces_ref.shape[0]):
        at = pl.multiple_of(((first ^ d) & mask) * rows, rows)
        for m in range(pieces_ref.shape[1]):
            target_ref[m, pl.ds(at, rows), :] = pieces_ref[d, m].astype(F32)


def place_rows(target_ref, value, first, mask, rows):
    n_trial = target_ref.shape[0]
    for d in range(value.shape[0] // (n_trial * rows)):
        at = pl.multiple_of(((first ^ d) & mask) * rows, rows)
        for m in range(n_trial):
            row = (d * n_trial + m) * rows
            target_ref[m, pl.ds(at, rows), :] = value[row : row + rows]


def half_kernel(cut, top, half_ref, pair_ref, vv_ref, more_ref, ov_ref, *refs):
    acc_ref, rest_ref, held_ov_ref, xs_ref, mid_ref, sem = refs
    me = lax.axis_index("aux")
    copies = [
        pltpu.make_async_copy(
            more_ref.at[pl.ds(vv_ref.shape[0], rest_ref.shape[0])], rest_ref, sem.at[0]
        ),
        pltpu.make_async_copy(ov_ref, held_ov_ref, sem.at[1]),
    ]
    copies[0].start()

    if cut:
        place(xs_ref, half_ref, me, half_ref.shape[0] - 1, half_ref.shape[2])
    else:
        xs_ref[...] = half_ref[...].astype(F32)
    acc_ref[...] = jnp.zeros_like(acc_ref)
    x = xs_ref[...].astype(BF16)
    transform, gather_up, starts = half_stages(
        x, pair_ref, me >> top, (vv_ref, rest_ref), acc_ref, mid_ref
    )
    transform(0)
    gather_up(starts[0], starts[1])
    copies[0].wait()
    copies[1].start()
    transform(1)
    gather_up(starts[1], starts[2])
    copies[1].wait()


def build_kernel(low, cut, top, occ_ref, vir_ref, own_ref, held_ref, *refs):
    parts = 1 << low
    pieces, (ov_ref, pair_ref, *vv_refs), outs = refs[:2], refs[2:6], refs[6:-3]
    xs_ref, mid_ref, acc_ref = refs[-3:]
    n_trial, rows, n_virt = own_ref.shape
    n_occ = ov_ref.shape[2]
    size, half = n_occ // rows, n_occ // 2
    high_count = size >> low
    me = lax.axis_index("aux")
    other = 1 - (me >> top)
    mine = me & (parts - 1)
    if cut:
        place(xs_ref, pieces[0], me, size - 1, rows)
        far = spread(pieces[1][...].astype(F32), half * n_trial, n_virt)
        place_rows(xs_ref, far, me ^ (size // 2), size - 1, rows)
    else:
        for k, piece in enumerate(pieces):
            at = pl.multiple_of(((me >> top) ^ k) * half, half)
            for m in range(n_trial):
                xs_ref[m, pl.ds(at, half), :] = piece[m].astype(F32)
    x = xs_ref[...].astype(BF16)
    acc_ref[...] = held_ref[...]
    rest = pl.ds(pl.multiple_of(other * half, half), half)
    x_rest = jnp.stack([xs_ref[m, rest, :] for m in range(n_trial)], 0).astype(BF16)
    first, middle, last = coulomb_stages(acc_ref, x, ov_ref)
    transform, gather_up, starts = half_stages(
        x_rest, pair_ref, other, vv_refs, acc_ref, mid_ref
    )
    total = first()
    transform(0)
    weights = middle(total)
    transform(1)
    last(weights)
    gather_up(0, starts[-1])
    unit = (
        lax.broadcasted_iota(jnp.int32, (n_occ, n_occ), 0)
        == lax.broadcasted_iota(jnp.int32, (n_occ, n_occ), 1)
    ).astype(BF16)
    lines = []
    for m in range(n_trial):
        value = -dot_nt(unit, acc_ref[m].astype(BF16))
        seen = xs_ref[m]
        lines.append(jnp.sum(jnp.sum(seen * value, axis=0, keepdims=True), axis=1, keepdims=True))
        xs_ref[m] = value
    own = own_ref[...]
    square = own * own
    diag = diagonal(occ_ref, vir_ref, me * rows, rows)
    for m in range(n_trial):
        lines[m] += jnp.sum(
            jnp.sum(square[m] * diag, axis=0, keepdims=True), axis=1, keepdims=True
        )
    for m in range(n_trial):
        lines.append(
            jnp.sum(jnp.sum(square[m], axis=0, keepdims=True), axis=1, keepdims=True)
        )
    body = high_count * n_trial * rows
    height, wide = message_shape(body, n_virt, 0)
    scalars = jnp.concatenate([jnp.broadcast_to(line, (1, wide)) for line in lines], axis=0)
    single = jnp.where(
        lax.broadcasted_iota(jnp.int32, scalars.shape, 1) == 0, scalars, 0.0
    )
    coded = three_parts(scalars)
    if not cut:
        for ref, value in zip(outs, (xs_ref[...], single, coded)):
            ref[...] = value
        return
    outs[0][height:, :] = single
    for k in range(parts):
        blocks = []
        for z in range(high_count):
            at = pl.multiple_of(((z << low) | (mine ^ k)) * rows, rows)
            blocks += [xs_ref[m, pl.ds(at, rows), :] for m in range(n_trial)]
        whole = dense(jnp.concatenate(blocks, axis=0))
        if k == 0:
            outs[0][:height, :] = whole
        else:
            outs[k][:height, :] = whole.astype(BF16)
            outs[k][height:, :] = coded


def pack_kernel(count, *refs):
    target_ref, at, rows = refs[count], 0, []
    for ref in refs[:count]:
        value = ref[...].astype(F32)
        target_ref[at : at + ref.shape[0]] = value.astype(BF16)
        at += ref.shape[0]
        rows.append(value.reshape(-1, ref.shape[-1]) if refs[count + 1 :] else None)
    for ref in refs[count + 1 :]:
        ref[...] = dense(jnp.concatenate(rows, axis=0)).astype(BF16)


def pack(arrays, message=False):
    shape = (sum(a.shape[0] for a in arrays),) + arrays[0].shape[1:]
    shapes = [shape]
    if message:
        shapes.append(message_shape(shape[0] * shape[1] * shape[2], shape[3], 0))
    return pl.pallas_call(
        functools.partial(pack_kernel, len(arrays)),
        out_shape=[jax.ShapeDtypeStruct(one, BF16) for one in shapes],
        in_specs=[VMEM] * len(arrays),
        out_specs=[VMEM] * len(shapes),
        compiler_params=SMALL,
    )(*arrays)


def in_vmem(*arrays):
    return [pltpu.with_memory_space_constraint(a, pltpu.VMEM) for a in arrays]


def in_order(half, me):
    count, n_trial, rows, n_virt = half.shape
    order = (me & (count - 1)) ^ jnp.arange(count)
    return half[order].transpose(1, 0, 2, 3).reshape(n_trial, count * rows, n_virt)


def in_hbm(*arrays):
    return [pltpu.with_memory_space_constraint(a, pltpu.HBM) for a in arrays]


def first_half(top, half, pairs, exch_vv, more_vv, coul_t):
    cut = half.ndim == 4
    n_aux, n_virt, n_occ = coul_t.shape
    n_trial = half.shape[1] if cut else half.shape[0]
    flops = n_aux * n_trial * n_occ * n_virt * (n_virt + n_occ)
    return pl.pallas_call(
        functools.partial(half_kernel, cut, top),
        out_shape=[
            pltpu.VMEM((n_trial, n_virt, n_occ), F32),
            pltpu.VMEM((n_aux - exch_vv.shape[0], n_virt, n_virt), BF16),
            pltpu.VMEM(coul_t.shape, BF16),
        ],
        in_specs=[VMEM] * 3 + [HBM] * 2,
        out_specs=[VMEM] * 3,
        scratch_shapes=[
            pltpu.VMEM((n_trial, n_occ // 2, n_virt), F32),
            pltpu.VMEM((2, n_aux // 2, n_virt, n_trial * n_occ // 2), BF16),
            pltpu.SemaphoreType.DMA((2,)),
        ],
        compiler_params=pltpu.CompilerParams(vmem_limit_bytes=32 << 20),
        cost_estimate=pl.CostEstimate(
            flops=flops, bytes_accessed=2 * (exch_vv.size + coul_t.size), transcendentals=0
        ),
    )(half, *in_vmem(pairs, exch_vv), *in_hbm(more_vv, coul_t))


def dense_call(value):
    def kernel(value_ref, out_ref):
        out_ref[...] = dense(value_ref[...])

    return pl.pallas_call(
        kernel,
        out_shape=jax.ShapeDtypeStruct(message_shape(*value.shape, 0), value.dtype),
        in_specs=[VMEM],
        out_specs=VMEM,
        compiler_params=SMALL,
    )(value)


def build(me, top, occ, vir, own, held, pieces, coul_t, pairs, exch_vv, low):
    parts = 1 << low
    n_trial, rows, n_virt = own.shape
    n_aux, _, n_occ = coul_t.shape
    high_count = n_occ // rows >> low
    cut = rows % 8 == 0
    height, extra = high_count * n_trial * rows, 2 * n_trial
    shape = message_shape(height, n_virt, extra)
    if cut:
        shapes = [jax.ShapeDtypeStruct(shape, F32)]
        shapes += [jax.ShapeDtypeStruct(shape, BF16)] * (parts - 1)
    else:
        shapes = [
            jax.ShapeDtypeStruct((n_trial, n_occ, n_virt), F32),
            jax.ShapeDtypeStruct((extra, shape[1]), F32),
            jax.ShapeDtypeStruct((extra, shape[1]), BF16),
        ]
    flops = n_aux * n_trial * n_occ * n_virt * (n_virt + n_occ)
    moved = 2 * (coul_t.size + pairs.size + sum(a.size for a in exch_vv))
    results = pl.pallas_call(
        functools.partial(build_kernel, low, cut, top),
        out_shape=shapes,
        in_specs=[VMEM] * 10,
        out_specs=[VMEM] * len(shapes),
        scratch_shapes=[
            pltpu.VMEM((n_trial, n_occ, n_virt), F32),
            pltpu.VMEM((2, n_aux // 2, n_virt, n_trial * n_occ // 2), BF16),
            pltpu.VMEM((n_trial, n_virt, n_occ), F32),
        ],
        compiler_params=pltpu.CompilerParams(vmem_limit_bytes=32 << 20),
        cost_estimate=pl.CostEstimate(flops=flops, bytes_accessed=moved, transcendentals=0),
    )(occ, vir, own, *in_vmem(held), *pieces, *in_vmem(coul_t, pairs, *exch_vv))
    if cut:
        return results
    value, single, coded = results
    value = value.reshape(n_trial, high_count, parts, rows, n_virt).transpose(2, 1, 0, 3, 4)
    mine = me & (parts - 1)
    blocks = [
        dense_call(
            lax.dynamic_index_in_dim(value, mine ^ k, 0, keepdims=False).reshape(height, n_virt)
        )
        for k in range(parts)
    ]
    return [jnp.concatenate([blocks[0], single], axis=0)] + [
        jnp.concatenate([block.astype(BF16), coded], axis=0) for block in blocks[1:]
    ]


def summed(own_ref, arrived):
    total = own_ref[...]
    for ref in arrived:
        total += ref[...].astype(F32)
    return total


def combine_kernel(extra, own_ref, *refs):
    arrived, (total_ref, send_ref) = refs[:-2], refs[-2:]
    total = summed(own_ref, arrived)
    body = total.shape[0] - extra
    scalars = jnp.sum(total[body:], axis=1, keepdims=True)
    scalars = jnp.broadcast_to(scalars, (extra, total.shape[1]))
    lane = lax.broadcasted_iota(jnp.int32, scalars.shape, 1)
    total_ref[:body, :] = total[:body]
    total_ref[body:, :] = jnp.where(lane == 0, scalars, 0.0)
    send_ref[:body, :] = total[:body].astype(BF16)
    send_ref[body:, :] = three_parts(scalars)


def combine(own, arrived, extra):
    return pl.pallas_call(
        functools.partial(combine_kernel, extra),
        out_shape=[
            jax.ShapeDtypeStruct(own.shape, F32),
            jax.ShapeDtypeStruct(own.shape, BF16),
        ],
        in_specs=[VMEM] * (1 + len(arrived)),
        out_specs=[VMEM] * 2,
        compiler_params=SMALL,
    )(own, *arrived)


def outline_kernel(low, cut, after_ref, occ_ref, vir_ref, near_ref, half_ref, far_ref, *outs):
    del after_ref
    t_ref, sigma_ref, diag_ref = outs
    n_trial, rows, n_virt = near_ref.shape
    count = half_ref.shape[0]
    me = lax.axis_index("aux")
    mine, top = me & ((1 << low) - 1), me >> low
    far = spread(far_ref[...].astype(F32), count * n_trial * rows, n_virt) if cut else None
    for r in range(t_ref.shape[0]):
        diag = diagonal(occ_ref, vir_ref, (((top ^ r) << low) | mine) * rows, rows)
        diag_ref[r] = diag
        away = r << low
        for m in range(n_trial):
            row = ((away % count) * n_trial + m) * rows
            if r == 0:
                t = near_ref[m]
            elif away < count:
                t = half_ref[away, m].astype(F32)
            elif cut:
                t = far[row : row + rows]
            else:
                t = far_ref[away % count, m].astype(F32)
            t_ref[r, m] = t
            sigma_ref[r, m] = diag * t


def outline(after, occ, vir, low, near, half, far):
    n_trial, rows, n_virt = near.shape
    high_count = 2 * half.shape[0] >> low
    blocks = pltpu.VMEM((high_count, n_trial, rows, n_virt), F32)
    return pl.pallas_call(
        functools.partial(outline_kernel, low, rows % 8 == 0),
        out_shape=[blocks, blocks, pltpu.VMEM((high_count, rows, n_virt), F32)],
        in_specs=[ANY] + [VMEM] * 5,
        out_specs=[VMEM] * 3,
        compiler_params=SMALL,
        cost_estimate=pl.CostEstimate(
            flops=1 << 20, bytes_accessed=1 << 21, transcendentals=0
        ),
    )(after, occ, vir, near, half, far)


def residual_kernel(low, t_ref, start_ref, diag_ref, own_ref, *refs):
    arrived, (sigma_ref, precond_ref, square_ref, held_ref) = refs[:-4], refs[-4:]
    high_count, n_trial, rows, n_virt = t_ref.shape
    body = high_count * n_trial * rows
    top = lax.axis_index("aux") >> low
    total = summed(own_ref, arrived)
    height = message_shape(body, n_virt, 0)[0]
    held_ref[...] = spread(total[:height], body, n_virt).reshape(held_ref.shape)
    scalars = jnp.sum(total[height:], axis=1, keepdims=True)
    omega = scalars[:n_trial] / (scalars[n_trial:] + 1e-06)
    squares = [jnp.zeros((rows, n_virt), F32) for _ in range(n_trial)]
    for r in range(high_count):
        diag = diag_ref[r]
        block = held_ref[top ^ r]
        for m in range(n_trial):
            level = omega[m : m + 1]
            sigma = start_ref[r, m] + block[m * rows : (m + 1) * rows]
            precond = (sigma - level * t_ref[r, m]) / jnp.maximum(jnp.abs(diag - level), 1.0)
            squares[m] += precond * precond
            if r == 0:
                sigma_ref[m] = sigma
                precond_ref[m] = precond
    sums = [
        jnp.sum(jnp.sum(s, axis=0, keepdims=True), axis=1, keepdims=True) for s in squares
    ]
    square_ref[...] = jnp.concatenate(
        [jnp.broadcast_to(s, (1, square_ref.shape[1])) for s in sums], axis=0
    )


def residual(low, outlined, own, arrived):
    high_count, n_trial, rows, n_virt = outlined[0].shape
    block = pltpu.VMEM((n_trial, rows, n_virt), F32)
    return pl.pallas_call(
        functools.partial(residual_kernel, low),
        out_shape=[block, block, pltpu.VMEM((n_trial, 128), F32)],
        in_specs=[VMEM] * (4 + len(arrived)),
        out_specs=[VMEM] * 3,
        scratch_shapes=[pltpu.VMEM((high_count, n_trial * rows, n_virt), F32)],
        compiler_params=SMALL,
    )(*outlined, own, *arrived)


def finish_kernel(count, precond_ref, *refs):
    update_ref = refs[-1]
    square = refs[0][...]
    for ref in refs[1:-1]:
        square += ref[...]
    scale = lax.rsqrt(square[:, :1] / count + 1e-06)
    for m in range(precond_ref.shape[0]):
        update_ref[m] = precond_ref[m] * scale[m : m + 1]


def finish(count, precond, squares):
    return pl.pallas_call(
        functools.partial(finish_kernel, count),
        out_shape=jax.ShapeDtypeStruct(precond.shape, F32),
        in_specs=[VMEM] * (1 + len(squares)),
        out_specs=VMEM,
        compiler_params=SMALL,
    )(precond, *squares)


def fetch_kernel(count, after_ref, *refs):
    del after_ref
    sources, targets, sem = refs[:count], refs[count : 2 * count], refs[-1]
    copies = [
        pltpu.make_async_copy(source.at[pl.ds(0, target.shape[0])], target, sem.at[k])
        for k, (source, target) in enumerate(zip(sources, targets))
    ]
    for copy in copies:
        copy.start()
    for copy in copies:
        copy.wait()


def fetch(after, counts, *arrays):
    return pl.pallas_call(
        functools.partial(fetch_kernel, len(arrays)),
        out_shape=[pltpu.VMEM((n,) + a.shape[1:], a.dtype) for n, a in zip(counts, arrays)],
        in_specs=[ANY] + [HBM] * len(arrays),
        out_specs=[VMEM] * len(arrays),
        scratch_shapes=[pltpu.SemaphoreType.DMA((len(arrays),))],
        compiler_params=SMALL,
        cost_estimate=pl.CostEstimate(
            flops=0, bytes_accessed=sum(4 * a.size for a in arrays), transcendentals=0
        ),
    )(after, *in_hbm(*arrays))


def prepare_kernel(after_ref, early_ref, oo_ref, vv_ref, pair_ref, held_ref, late_ref, sem):
    del after_ref
    first = pltpu.make_async_copy(
        oo_ref.at[pl.ds(early_ref.shape[0], late_ref.shape[0])], late_ref, sem.at[0]
    )
    second = pltpu.make_async_copy(
        vv_ref.at[pl.ds(0, held_ref.shape[0])], held_ref, sem.at[1]
    )
    first.start()
    second.start()
    pair_weights((early_ref, late_ref), pair_ref, first.wait)
    second.wait()


def prepare(after, early_oo, exch_oo, exch_vv):
    n_aux, n_occ, _ = exch_oo.shape
    early = early_oo.shape[0]
    return pl.pallas_call(
        prepare_kernel,
        out_shape=[
            pltpu.VMEM((2, 2, n_aux // 2, n_occ, n_occ), BF16),
            pltpu.VMEM((n_aux // 4 * 2,) + exch_vv.shape[1:], BF16),
        ],
        in_specs=[ANY, VMEM, HBM, HBM],
        out_specs=[VMEM] * 2,
        scratch_shapes=[
            pltpu.VMEM((n_aux - early, n_occ, n_occ), BF16),
            pltpu.SemaphoreType.DMA((2,)),
        ],
        compiler_params=SMALL,
        cost_estimate=pl.CostEstimate(
            flops=0, bytes_accessed=4 * (exch_oo.size + exch_vv.size), transcendentals=0
        ),
    )(after, *in_vmem(early_oo), *in_hbm(exch_oo, exch_vv))


def on_device(size, trial_vecs, occ_energy, vir_energy, coul_ov, exch_oo, exch_vv):
    n_trial, rows, n_virt = trial_vecs.shape
    n_occ = exch_oo.shape[1]
    low, highs = bit_groups(size)
    me = lax.axis_index("aux").astype(jnp.int32)
    top = size.bit_length() - 2
    coul_t = jnp.transpose(coul_ov, (0, 2, 1))
    counts = (trial_vecs.shape[0], 1, 1, exch_oo.shape[0] // EARLY * 2)
    near, occ, vir, early_oo = fetch(
        trial_vecs, counts, trial_vecs, occ_energy[None], vir_energy[None], exch_oo
    )
    cut = rows % 8 == 0
    held, = pack([near[None]] + [a[None] for a in exchange(trial_vecs, size, 0, 1)])
    pairs, vv = prepare(held, early_oo, exch_oo, exch_vv)
    sent = held
    for at in range(1, top, 2):
        last = cut and at + 2 >= top
        held, *message = pack([held] + exchange(held, size, at, min(2, top - at)), last)
        sent = message[0] if last else held
    far, = exchange(sent, size, top, 1)
    pieces = [held, far] if cut else [in_order(half, me) for half in (held, far)]
    half_sum, more_vv, coul_t = first_half(
        top, pieces[0], pairs, vv, exch_vv, coul_t
    )
    own, *sends = build(
        me, top, occ, vir, near, half_sum, pieces, coul_t, pairs, (vv, more_vv), low
    )
    outlined = outline(own, occ, vir, low, near, held, far)
    arrived = [swap(send, size, k + 1) for k, send in enumerate(sends)]
    for at, width in highs:
        own, send = combine(own, arrived, 2 * n_trial)
        arrived = exchange(send, size, at, width)
    sigma_vecs, precond, square = residual(low, outlined, own, arrived)
    squares = [square] + exchange(square, size, 0, low)
    return sigma_vecs, finish(n_occ * n_virt, precond, squares)


def solution(mesh):
    in_specs = (
        P("geom", "aux", None),
        P("geom"),
        P("geom"),
        P(("geom", "aux"), None, None),
        P(("geom", "aux"), None, None),
        P(("geom", "aux"), None, None),
    )
    out_specs = (P("geom", "aux", None), P("geom", "aux", None))
    return jax.shard_map(
        functools.partial(on_device, mesh.shape["aux"]),
        mesh=mesh,
        in_specs=in_specs,
        out_specs=out_specs,
        check_vma=False,
    )
```

```python
import functools

import jax
import jax.numpy as jnp
from jax import lax
from jax.experimental import pallas as pl
from jax.experimental.pallas import tpu as pltpu
from jax.sharding import PartitionSpec as P


F32 = jnp.float32
BF16 = jnp.bfloat16
LOW_BITS = 2
LANES = 128
EARLY = 8
TILE = 16
VMEM = pl.BlockSpec(memory_space=pltpu.VMEM)
HBM = pl.BlockSpec(memory_space=pltpu.HBM)
ANY = pl.BlockSpec(memory_space=pl.ANY)
SMALL = pltpu.CompilerParams(vmem_limit_bytes=4 << 20)


def bit_groups(size):
    bits = size.bit_length() - 1
    assert size == 1 << bits
    low = min(LOW_BITS, bits)
    return low, [(at, min(LOW_BITS, bits - at)) for at in range(low, bits, LOW_BITS)]


def swap(value, size, offset):
    return lax.ppermute(value, "aux", [(i, i ^ offset) for i in range(size)])


def exchange(value, size, at, width):
    return [swap(value, size, k << at) for k in range(1, 1 << width)]


def dot(a, b):
    return jnp.dot(a, b, preferred_element_type=F32)


def dot_nt(a, b):
    return lax.dot_general(a, b, (((1,), (1,)), ((), ())), preferred_element_type=F32)


def diagonal(occ_ref, vir_ref, first, rows):
    shape = (rows, occ_ref.shape[1])
    wanted = lax.broadcasted_iota(jnp.int32, shape, 0) + first
    picked = jnp.where(lax.broadcasted_iota(jnp.int32, shape, 1) == wanted, occ_ref[...], 0.0)
    return vir_ref[...] - jnp.sum(picked, axis=1, keepdims=True)


def packs(rows, width):
    rest, free = width - LANES, 2 * LANES - width
    if not 0 < rest < LANES or rest % free or rows * free % LANES:
        return 0
    given = rows * free // LANES
    return given if given % 8 == 0 else 0


def dense(value):
    rows, width = value.shape
    given = packs(rows, width)
    if not given:
        return value
    rest, free = width - LANES, 2 * LANES - width
    high = jnp.concatenate([value[:, LANES:], jnp.zeros((rows, free), value.dtype)], axis=1)
    kept, last = high[: rows - given], high[rows - given :]
    moved = [
        pltpu.roll(last, (rest - g * free) % LANES, 1) for g in range(rest // free)
    ]
    lane = lax.broadcasted_iota(jnp.int32, kept.shape, 1)
    kept = jnp.where(lane < rest, kept, jnp.concatenate(moved, axis=0))
    return jnp.concatenate([value[:, :LANES], kept], axis=0)


def spread(value, rows, width):
    given = packs(rows, width)
    if not given:
        return value
    rest, free = width - LANES, 2 * LANES - width
    kept = value[rows:]
    last = jnp.zeros((given, LANES), value.dtype)
    lane = lax.broadcasted_iota(jnp.int32, last.shape, 1)
    for g in range(rest // free):
        back = pltpu.roll(kept[g * given : (g + 1) * given], (LANES - rest + g * free) % LANES, 1)
        last = jnp.where((lane >= g * free) & (lane < (g + 1) * free), back, last)
    high = jnp.concatenate([kept, last], axis=0)
    return jnp.concatenate([value[:rows], high[:, :rest]], axis=1)


def message_shape(rows, width, extra):
    if packs(rows, width):
        return rows * width // LANES + extra, LANES
    return rows + extra, width


def three_parts(value):
    high = value.astype(BF16).astype(F32)
    middle = (value - high).astype(BF16).astype(F32)
    rest = value - high - middle
    lane = lax.broadcasted_iota(jnp.int32, value.shape, 1)
    return jnp.where(
        lane == 0, high, jnp.where(lane == 1, middle, jnp.where(lane == 2, rest, 0.0))
    ).astype(BF16)


def coulomb_stages(acc_ref, x, ov_ref):
    n_aux, n_virt, n_occ = ov_ref.shape
    n_trial = x.shape[0]
    tiles = n_virt // TILE
    unit = (
        lax.broadcasted_iota(jnp.int32, (n_virt, n_virt), 0)
        == lax.broadcasted_iota(jnp.int32, (n_virt, n_virt), 1)
    ).astype(BF16)
    x_t = jnp.stack([dot_nt(unit, x[m]).astype(BF16) for m in range(n_trial)], 0)
    rows, cols = n_trial * TILE, n_aux * TILE

    def x_tile(t):
        return x_t[:, t * TILE : (t + 1) * TILE, :].reshape(rows, n_occ)

    def ov_tile(t):
        return ov_ref[:, t * TILE : (t + 1) * TILE, :].reshape(cols, n_occ)

    def first():
        total = jnp.zeros((rows, cols), F32)
        for t in range(0, tiles, 2):
            span = range(t, min(t + 2, tiles))
            total += dot_nt(
                jnp.concatenate([x_tile(u) for u in span], axis=1),
                jnp.concatenate([ov_tile(u) for u in span], axis=1),
            )
        return total

    def middle(total):
        same = (
            lax.broadcasted_iota(jnp.int32, (rows, cols), 0) % TILE
            == lax.broadcasted_iota(jnp.int32, (rows, cols), 1) % TILE
        )
        coef = jnp.sum(jnp.where(same, total, 0.0).reshape(n_trial, TILE, cols), axis=1)
        lane = lax.broadcasted_iota(jnp.int32, coef.shape, 1)
        step = 1
        while step < TILE:
            coef += jnp.where(
                (lane & step) != 0, pltpu.roll(coef, step, 1), pltpu.roll(coef, cols - step, 1)
            )
            step *= 2
        twice = 2.0 * coef.astype(BF16).astype(F32)
        repeated = jnp.broadcast_to(twice[:, None, :], (n_trial, TILE, cols))
        return jnp.where(same, repeated.reshape(rows, cols), 0.0).astype(BF16)

    def last(weights):
        for t in range(0, tiles, 2):
            span = range(t, min(t + 2, tiles))
            sums = dot(weights, jnp.concatenate([ov_tile(u) for u in span], axis=1))
            for k, u in enumerate(span):
                acc_ref[:, u * TILE : (u + 1) * TILE, :] -= sums[
                    :, k * n_occ : (k + 1) * n_occ
                ].reshape(n_trial, TILE, n_occ)

    return first, middle, last


def pair_weights(oo_refs, pair_ref, ready):
    n_occ = oo_refs[0].shape[1]
    half = n_occ // 2
    left = lax.broadcasted_iota(jnp.int32, (n_occ, n_occ), 1) < half
    at = 0
    for part, oo_ref in enumerate(oo_refs):
        if part == 1:
            ready()
        for g in range(oo_ref.shape[0] // 2):
            straight = [oo_ref[2 * g + odd].astype(F32) for odd in range(2)]
            moved = [pltpu.roll(value, half, 1) for value in straight]
            for odd in range(2):
                low = jnp.where(left, straight[odd], moved[1 - odd])
                high = jnp.where(left, moved[odd], straight[1 - odd])
                pair_ref[0, odd, at] = low.astype(BF16)
                pair_ref[1, odd, at] = high.astype(BF16)
            at += 1


def half_stages(x, pair_ref, k, vv_refs, acc_ref, mid_ref):
    n_trial, half, n_virt = x.shape
    n_occ = 2 * half
    width = n_trial * half
    orders = [
        jnp.concatenate([x[m ^ odd] for m in range(n_trial)], axis=0) for odd in range(2)
    ]
    starts = [0]
    for vv_ref in vv_refs:
        starts.append(starts[-1] + vv_ref.shape[0] // 2)

    def transform(part):
        vv_ref, pairs = vv_refs[part], starts[part + 1] - starts[part]
        even, odd = (
            dot_nt(
                jnp.concatenate([vv_ref[2 * g + odd] for g in range(pairs)], axis=0),
                orders[odd],
            )
            for odd in range(2)
        )
        left = lax.broadcasted_iota(jnp.int32, even.shape, 1) % n_occ < half
        shape, span = (pairs, n_virt, width), pl.ds(starts[part], pairs)
        mid_ref[0, span] = jnp.where(left, even, odd).astype(BF16).reshape(shape)
        mid_ref[1, span] = jnp.where(left, odd, even).astype(BF16).reshape(shape)

    def gather_up(first, last):
        for odd in range(2):
            weights = jnp.concatenate(
                [pair_ref[k, odd, g] for g in range(first, last)], axis=1
            )
            for q in range(n_trial // 2):
                at = slice(q * n_occ, (q + 1) * n_occ)
                lines = jnp.concatenate(
                    [mid_ref[odd, g, :, at] for g in range(first, last)], axis=1
                )
                acc_ref[2 * q + odd] += dot_nt(lines, weights)

    return transform, gather_up, starts


def place(target_ref, pieces_ref, first, mask, rows):
    for d in range(pieces_ref.shape[0]):
        at = pl.multiple_of(((first ^ d) & mask) * rows, rows)
        for m in range(pieces_ref.shape[1]):
            target_ref[m, pl.ds(at, rows), :] = pieces_ref[d, m].astype(F32)


def place_rows(target_ref, value, first, mask, rows):
    n_trial = target_ref.shape[0]
    for d in range(value.shape[0] // (n_trial * rows)):
        at = pl.multiple_of(((first ^ d) & mask) * rows, rows)
        for m in range(n_trial):
            row = (d * n_trial + m) * rows
            target_ref[m, pl.ds(at, rows), :] = value[row : row + rows]


def half_kernel(cut, top, half_ref, pair_ref, vv_ref, more_ref, ov_ref, *refs):
    acc_ref, rest_ref, held_ov_ref, seen_ref, xs_ref, mid_ref, sem = refs
    me = lax.axis_index("aux")
    copies = [
        pltpu.make_async_copy(
            more_ref.at[pl.ds(vv_ref.shape[0], rest_ref.shape[0])], rest_ref, sem.at[0]
        ),
        pltpu.make_async_copy(ov_ref, held_ov_ref, sem.at[1]),
    ]
    copies[0].start()

    if cut:
        place(xs_ref, half_ref, me, half_ref.shape[0] - 1, half_ref.shape[2])
    else:
        xs_ref[...] = half_ref[...].astype(F32)
    acc_ref[...] = jnp.zeros_like(acc_ref)
    x = xs_ref[...].astype(BF16)
    seen_ref[...] = x
    transform, gather_up, starts = half_stages(
        x, pair_ref, me >> top, (vv_ref, rest_ref), acc_ref, mid_ref
    )
    transform(0)
    gather_up(starts[0], starts[1])
    copies[0].wait()
    copies[1].start()
    transform(1)
    gather_up(starts[1], starts[2])
    copies[1].wait()


def build_kernel(low, cut, top, occ_ref, vir_ref, own_ref, held_ref, *refs):
    parts = 1 << low
    pieces, (ov_ref, pair_ref, *vv_refs), outs = refs[:2], refs[2:6], refs[6:-3]
    xs_ref, mid_ref, acc_ref = refs[-3:]
    n_trial, rows, n_virt = own_ref.shape
    n_occ = ov_ref.shape[2]
    size, half = n_occ // rows, n_occ // 2
    high_count = size >> low
    me = lax.axis_index("aux")
    other = 1 - (me >> top)
    mine = me & (parts - 1)
    at = pl.multiple_of((1 - other) * half, half)
    for m in range(n_trial):
        xs_ref[m, pl.ds(at, half), :] = pieces[0][m].astype(F32)
    if cut:
        far = spread(pieces[1][...].astype(F32), half * n_trial, n_virt)
        place_rows(xs_ref, far, me ^ (size // 2), size - 1, rows)
    else:
        at = pl.multiple_of(other * half, half)
        for m in range(n_trial):
            xs_ref[m, pl.ds(at, half), :] = pieces[1][m].astype(F32)
    x = xs_ref[...].astype(BF16)
    acc_ref[...] = held_ref[...]
    rest = pl.ds(pl.multiple_of(other * half, half), half)
    x_rest = jnp.stack([xs_ref[m, rest, :] for m in range(n_trial)], 0).astype(BF16)
    first, middle, last = coulomb_stages(acc_ref, x, ov_ref)
    transform, gather_up, starts = half_stages(
        x_rest, pair_ref, other, vv_refs, acc_ref, mid_ref
    )
    total = first()
    transform(0)
    transform(1)
    weights = middle(total)
    last(weights)
    gather_up(0, starts[-1])
    unit = (
        lax.broadcasted_iota(jnp.int32, (n_occ, n_occ), 0)
        == lax.broadcasted_iota(jnp.int32, (n_occ, n_occ), 1)
    ).astype(BF16)
    lines = []
    for m in range(n_trial):
        value = -dot_nt(unit, acc_ref[m].astype(BF16))
        seen = xs_ref[m]
        lines.append(jnp.sum(jnp.sum(seen * value, axis=0, keepdims=True), axis=1, keepdims=True))
        xs_ref[m] = value
    own = own_ref[...]
    square = own * own
    diag = diagonal(occ_ref, vir_ref, me * rows, rows)
    for m in range(n_trial):
        lines[m] += jnp.sum(
            jnp.sum(square[m] * diag, axis=0, keepdims=True), axis=1, keepdims=True
        )
    for m in range(n_trial):
        lines.append(
            jnp.sum(jnp.sum(square[m], axis=0, keepdims=True), axis=1, keepdims=True)
        )
    body = high_count * n_trial * rows
    height, wide = message_shape(body, n_virt, 0)
    scalars = jnp.concatenate([jnp.broadcast_to(line, (1, wide)) for line in lines], axis=0)
    single = jnp.where(
        lax.broadcasted_iota(jnp.int32, scalars.shape, 1) == 0, scalars, 0.0
    )
    coded = three_parts(scalars)
    if not cut:
        for ref, value in zip(outs, (xs_ref[...], single, coded)):
            ref[...] = value
        return
    outs[0][height:, :] = single
    for k in range(parts):
        blocks = []
        for z in range(high_count):
            at = pl.multiple_of(((z << low) | (mine ^ k)) * rows, rows)
            blocks += [xs_ref[m, pl.ds(at, rows), :] for m in range(n_trial)]
        whole = dense(jnp.concatenate(blocks, axis=0))
        if k == 0:
            outs[0][:height, :] = whole
        else:
            outs[k][:height, :] = whole.astype(BF16)
            outs[k][height:, :] = coded


def pack_kernel(count, *refs):
    target_ref, at, rows = refs[count], 0, []
    for ref in refs[:count]:
        value = ref[...].astype(F32)
        target_ref[at : at + ref.shape[0]] = value.astype(BF16)
        at += ref.shape[0]
        rows.append(value.reshape(-1, ref.shape[-1]) if refs[count + 1 :] else None)
    for ref in refs[count + 1 :]:
        ref[...] = dense(jnp.concatenate(rows, axis=0)).astype(BF16)


def pack(arrays, message=False):
    shape = (sum(a.shape[0] for a in arrays),) + arrays[0].shape[1:]
    shapes = [shape]
    if message:
        shapes.append(message_shape(shape[0] * shape[1] * shape[2], shape[3], 0))
    return pl.pallas_call(
        functools.partial(pack_kernel, len(arrays)),
        out_shape=[jax.ShapeDtypeStruct(one, BF16) for one in shapes],
        in_specs=[VMEM] * len(arrays),
        out_specs=[VMEM] * len(shapes),
        compiler_params=SMALL,
    )(*arrays)


def in_vmem(*arrays):
    return [pltpu.with_memory_space_constraint(a, pltpu.VMEM) for a in arrays]


def in_order(half, me):
    count, n_trial, rows, n_virt = half.shape
    order = (me & (count - 1)) ^ jnp.arange(count)
    return half[order].transpose(1, 0, 2, 3).reshape(n_trial, count * rows, n_virt)


def in_hbm(*arrays):
    return [pltpu.with_memory_space_constraint(a, pltpu.HBM) for a in arrays]


def first_half(top, half, pairs, exch_vv, more_vv, coul_t):
    cut = half.ndim == 4
    n_aux, n_virt, n_occ = coul_t.shape
    n_trial = half.shape[1] if cut else half.shape[0]
    flops = n_aux * n_trial * n_occ * n_virt * (n_virt + n_occ)
    return pl.pallas_call(
        functools.partial(half_kernel, cut, top),
        out_shape=[
            pltpu.VMEM((n_trial, n_virt, n_occ), F32),
            pltpu.VMEM((n_aux - exch_vv.shape[0], n_virt, n_virt), BF16),
            pltpu.VMEM(coul_t.shape, BF16),
            pltpu.VMEM((n_trial, n_occ // 2, n_virt), BF16),
        ],
        in_specs=[VMEM] * 3 + [HBM] * 2,
        out_specs=[VMEM] * 4,
        scratch_shapes=[
            pltpu.VMEM((n_trial, n_occ // 2, n_virt), F32),
            pltpu.VMEM((2, n_aux // 2, n_virt, n_trial * n_occ // 2), BF16),
            pltpu.SemaphoreType.DMA((2,)),
        ],
        compiler_params=pltpu.CompilerParams(vmem_limit_bytes=32 << 20),
        cost_estimate=pl.CostEstimate(
            flops=flops, bytes_accessed=2 * (exch_vv.size + coul_t.size), transcendentals=0
        ),
    )(half, *in_vmem(pairs, exch_vv), *in_hbm(more_vv, coul_t))


def dense_call(value):
    def kernel(value_ref, out_ref):
        out_ref[...] = dense(value_ref[...])

    return pl.pallas_call(
        kernel,
        out_shape=jax.ShapeDtypeStruct(message_shape(*value.shape, 0), value.dtype),
        in_specs=[VMEM],
        out_specs=VMEM,
        compiler_params=SMALL,
    )(value)


def build(me, top, occ, vir, own, held, pieces, coul_t, pairs, exch_vv, low):
    parts = 1 << low
    n_trial, rows, n_virt = own.shape
    n_aux, _, n_occ = coul_t.shape
    high_count = n_occ // rows >> low
    cut = rows % 8 == 0
    height, extra = high_count * n_trial * rows, 2 * n_trial
    shape = message_shape(height, n_virt, extra)
    if cut:
        shapes = [jax.ShapeDtypeStruct(shape, F32)]
        shapes += [jax.ShapeDtypeStruct(shape, BF16)] * (parts - 1)
    else:
        shapes = [
            jax.ShapeDtypeStruct((n_trial, n_occ, n_virt), F32),
            jax.ShapeDtypeStruct((extra, shape[1]), F32),
            jax.ShapeDtypeStruct((extra, shape[1]), BF16),
        ]
    flops = n_aux * n_trial * n_occ * n_virt * (n_virt + n_occ)
    moved = 2 * (coul_t.size + pairs.size + sum(a.size for a in exch_vv))
    results = pl.pallas_call(
        functools.partial(build_kernel, low, cut, top),
        out_shape=shapes,
        in_specs=[VMEM] * 10,
        out_specs=[VMEM] * len(shapes),
        scratch_shapes=[
            pltpu.VMEM((n_trial, n_occ, n_virt), F32),
            pltpu.VMEM((2, n_aux // 2, n_virt, n_trial * n_occ // 2), BF16),
            pltpu.VMEM((n_trial, n_virt, n_occ), F32),
        ],
        compiler_params=pltpu.CompilerParams(vmem_limit_bytes=32 << 20),
        cost_estimate=pl.CostEstimate(flops=flops, bytes_accessed=moved, transcendentals=0),
    )(occ, vir, own, *in_vmem(held), *pieces, *in_vmem(coul_t, pairs, *exch_vv))
    if cut:
        return results
    value, single, coded = results
    value = value.reshape(n_trial, high_count, parts, rows, n_virt).transpose(2, 1, 0, 3, 4)
    mine = me & (parts - 1)
    blocks = [
        dense_call(
            lax.dynamic_index_in_dim(value, mine ^ k, 0, keepdims=False).reshape(height, n_virt)
        )
        for k in range(parts)
    ]
    return [jnp.concatenate([blocks[0], single], axis=0)] + [
        jnp.concatenate([block.astype(BF16), coded], axis=0) for block in blocks[1:]
    ]


def summed(own_ref, arrived):
    total = own_ref[...]
    for ref in arrived:
        total += ref[...].astype(F32)
    return total


def combine_kernel(extra, own_ref, *refs):
    arrived, (total_ref, send_ref) = refs[:-2], refs[-2:]
    total = summed(own_ref, arrived)
    body = total.shape[0] - extra
    scalars = jnp.sum(total[body:], axis=1, keepdims=True)
    scalars = jnp.broadcast_to(scalars, (extra, total.shape[1]))
    lane = lax.broadcasted_iota(jnp.int32, scalars.shape, 1)
    total_ref[:body, :] = total[:body]
    total_ref[body:, :] = jnp.where(lane == 0, scalars, 0.0)
    send_ref[:body, :] = total[:body].astype(BF16)
    send_ref[body:, :] = three_parts(scalars)


def combine(own, arrived, extra):
    return pl.pallas_call(
        functools.partial(combine_kernel, extra),
        out_shape=[
            jax.ShapeDtypeStruct(own.shape, F32),
            jax.ShapeDtypeStruct(own.shape, BF16),
        ],
        in_specs=[VMEM] * (1 + len(arrived)),
        out_specs=[VMEM] * 2,
        compiler_params=SMALL,
    )(own, *arrived)


def outline_kernel(low, cut, after_ref, occ_ref, vir_ref, near_ref, half_ref, far_ref, *outs):
    del after_ref
    t_ref, sigma_ref, diag_ref = outs
    n_trial, rows, n_virt = near_ref.shape
    count = half_ref.shape[0]
    me = lax.axis_index("aux")
    mine, top = me & ((1 << low) - 1), me >> low
    far = spread(far_ref[...].astype(F32), count * n_trial * rows, n_virt) if cut else None
    for r in range(t_ref.shape[0]):
        diag = diagonal(occ_ref, vir_ref, (((top ^ r) << low) | mine) * rows, rows)
        diag_ref[r] = diag
        away = r << low
        for m in range(n_trial):
            row = ((away % count) * n_trial + m) * rows
            if r == 0:
                t = near_ref[m]
            elif away < count:
                t = half_ref[away, m].astype(F32)
            elif cut:
                t = far[row : row + rows]
            else:
                t = far_ref[away % count, m].astype(F32)
            t_ref[r, m] = t
            sigma_ref[r, m] = diag * t


def outline(after, occ, vir, low, near, half, far):
    n_trial, rows, n_virt = near.shape
    high_count = 2 * half.shape[0] >> low
    blocks = pltpu.VMEM((high_count, n_trial, rows, n_virt), F32)
    return pl.pallas_call(
        functools.partial(outline_kernel, low, rows % 8 == 0),
        out_shape=[blocks, blocks, pltpu.VMEM((high_count, rows, n_virt), F32)],
        in_specs=[ANY] + [VMEM] * 5,
        out_specs=[VMEM] * 3,
        compiler_params=SMALL,
        cost_estimate=pl.CostEstimate(
            flops=1 << 20, bytes_accessed=1 << 21, transcendentals=0
        ),
    )(after, occ, vir, near, half, far)


def residual_kernel(low, t_ref, start_ref, diag_ref, own_ref, *refs):
    arrived, (sigma_ref, precond_ref, square_ref, held_ref) = refs[:-4], refs[-4:]
    high_count, n_trial, rows, n_virt = t_ref.shape
    body = high_count * n_trial * rows
    top = lax.axis_index("aux") >> low
    total = summed(own_ref, arrived)
    height = message_shape(body, n_virt, 0)[0]
    held_ref[...] = spread(total[:height], body, n_virt).reshape(held_ref.shape)
    scalars = jnp.sum(total[height:], axis=1, keepdims=True)
    omega = scalars[:n_trial] / (scalars[n_trial:] + 1e-06)
    squares = [jnp.zeros((rows, n_virt), F32) for _ in range(n_trial)]
    for r in range(high_count):
        diag = diag_ref[r]
        block = held_ref[top ^ r]
        for m in range(n_trial):
            level = omega[m : m + 1]
            sigma = start_ref[r, m] + block[m * rows : (m + 1) * rows]
            precond = (sigma - level * t_ref[r, m]) / jnp.maximum(jnp.abs(diag - level), 1.0)
            squares[m] += precond * precond
            if r == 0:
                sigma_ref[m] = sigma
                precond_ref[m] = precond
    sums = [
        jnp.sum(jnp.sum(s, axis=0, keepdims=True), axis=1, keepdims=True) for s in squares
    ]
    square_ref[...] = jnp.concatenate(
        [jnp.broadcast_to(s, (1, square_ref.shape[1])) for s in sums], axis=0
    )


def residual(low, outlined, own, arrived):
    high_count, n_trial, rows, n_virt = outlined[0].shape
    block = pltpu.VMEM((n_trial, rows, n_virt), F32)
    return pl.pallas_call(
        functools.partial(residual_kernel, low),
        out_shape=[block, block, pltpu.VMEM((n_trial, 128), F32)],
        in_specs=[VMEM] * (4 + len(arrived)),
        out_specs=[VMEM] * 3,
        scratch_shapes=[pltpu.VMEM((high_count, n_trial * rows, n_virt), F32)],
        compiler_params=SMALL,
    )(*outlined, own, *arrived)


def finish_kernel(count, precond_ref, *refs):
    update_ref = refs[-1]
    square = refs[0][...]
    for ref in refs[1:-1]:
        square += ref[...]
    scale = lax.rsqrt(square[:, :1] / count + 1e-06)
    for m in range(precond_ref.shape[0]):
        update_ref[m] = precond_ref[m] * scale[m : m + 1]


def finish(count, precond, squares):
    return pl.pallas_call(
        functools.partial(finish_kernel, count),
        out_shape=jax.ShapeDtypeStruct(precond.shape, F32),
        in_specs=[VMEM] * (1 + len(squares)),
        out_specs=VMEM,
        compiler_params=SMALL,
    )(precond, *squares)


def fetch_kernel(count, after_ref, *refs):
    del after_ref
    sources, targets, sem = refs[:count], refs[count : 2 * count], refs[-1]
    copies = [
        pltpu.make_async_copy(source.at[pl.ds(0, target.shape[0])], target, sem.at[k])
        for k, (source, target) in enumerate(zip(sources, targets))
    ]
    for copy in copies:
        copy.start()
    for copy in copies:
        copy.wait()


def fetch(after, counts, *arrays):
    return pl.pallas_call(
        functools.partial(fetch_kernel, len(arrays)),
        out_shape=[pltpu.VMEM((n,) + a.shape[1:], a.dtype) for n, a in zip(counts, arrays)],
        in_specs=[ANY] + [HBM] * len(arrays),
        out_specs=[VMEM] * len(arrays),
        scratch_shapes=[pltpu.SemaphoreType.DMA((len(arrays),))],
        compiler_params=SMALL,
        cost_estimate=pl.CostEstimate(
            flops=0, bytes_accessed=sum(4 * a.size for a in arrays), transcendentals=0
        ),
    )(after, *in_hbm(*arrays))


def prepare_kernel(after_ref, early_ref, oo_ref, vv_ref, pair_ref, held_ref, late_ref, sem):
    del after_ref
    first = pltpu.make_async_copy(
        oo_ref.at[pl.ds(early_ref.shape[0], late_ref.shape[0])], late_ref, sem.at[0]
    )
    second = pltpu.make_async_copy(
        vv_ref.at[pl.ds(0, held_ref.shape[0])], held_ref, sem.at[1]
    )
    first.start()
    second.start()
    pair_weights((early_ref, late_ref), pair_ref, first.wait)
    second.wait()


def prepare(after, early_oo, exch_oo, exch_vv):
    n_aux, n_occ, _ = exch_oo.shape
    early = early_oo.shape[0]
    return pl.pallas_call(
        prepare_kernel,
        out_shape=[
            pltpu.VMEM((2, 2, n_aux // 2, n_occ, n_occ), BF16),
            pltpu.VMEM((n_aux // 4 * 2,) + exch_vv.shape[1:], BF16),
        ],
        in_specs=[ANY, VMEM, HBM, HBM],
        out_specs=[VMEM] * 2,
        scratch_shapes=[
            pltpu.VMEM((n_aux - early, n_occ, n_occ), BF16),
            pltpu.SemaphoreType.DMA((2,)),
        ],
        compiler_params=SMALL,
        cost_estimate=pl.CostEstimate(
            flops=0, bytes_accessed=4 * (exch_oo.size + exch_vv.size), transcendentals=0
        ),
    )(after, *in_vmem(early_oo), *in_hbm(exch_oo, exch_vv))


def on_device(size, trial_vecs, occ_energy, vir_energy, coul_ov, exch_oo, exch_vv):
    n_trial, rows, n_virt = trial_vecs.shape
    n_occ = exch_oo.shape[1]
    low, highs = bit_groups(size)
    me = lax.axis_index("aux").astype(jnp.int32)
    top = size.bit_length() - 2
    coul_t = jnp.transpose(coul_ov, (0, 2, 1))
    counts = (trial_vecs.shape[0], 1, 1, exch_oo.shape[0] // EARLY * 2)
    near, occ, vir, early_oo = fetch(
        trial_vecs, counts, trial_vecs, occ_energy[None], vir_energy[None], exch_oo
    )
    cut = rows % 8 == 0
    held, = pack([near[None]] + [a[None] for a in exchange(trial_vecs, size, 0, 1)])
    pairs, vv = prepare(held, early_oo, exch_oo, exch_vv)
    sent = held
    for at in range(1, top, 2):
        last = cut and at + 2 >= top
        held, *message = pack([held] + exchange(held, size, at, min(2, top - at)), last)
        sent = message[0] if last else held
    far, = exchange(sent, size, top, 1)
    pieces = [held, far] if cut else [in_order(half, me) for half in (held, far)]
    half_sum, more_vv, coul_t, seen = first_half(
        top, pieces[0], pairs, vv, exch_vv, coul_t
    )
    own, *sends = build(
        me, top, occ, vir, near, half_sum, [seen, pieces[1]], coul_t, pairs, (vv, more_vv), low
    )
    outlined = outline(own, occ, vir, low, near, held, far)
    arrived = [swap(send, size, k + 1) for k, send in enumerate(sends)]
    for at, width in highs:
        own, send = combine(own, arrived, 2 * n_trial)
        arrived = exchange(send, size, at, width)
    sigma_vecs, precond, square = residual(low, outlined, own, arrived)
    squares = [square] + exchange(square, size, 0, low)
    return sigma_vecs, finish(n_occ * n_virt, precond, squares)


def solution(mesh):
    in_specs = (
        P("geom", "aux", None),
        P("geom"),
        P("geom"),
        P(("geom", "aux"), None, None),
        P(("geom", "aux"), None, None),
        P(("geom", "aux"), None, None),
    )
    out_specs = (P("geom", "aux", None), P("geom", "aux", None))
    return jax.shard_map(
        functools.partial(on_device, mesh.shape["aux"]),
        mesh=mesh,
        in_specs=in_specs,
        out_specs=out_specs,
        check_vma=False,
    )
```
